256 devices in a mesh: tile: 32 (over x_hi, z, core), depth: 8 (over y, x_lo).
Axes of the slice: x: 4 (x_hi: 2, x_lo: 2; x = x_hi * 2 + x_lo), y: 4, z: 8, core: 2. Of those that a mesh axis runs over, the one named last changes fastest.
Arguments:
- mask_tiles: float32 [64, 128, 128], P('tile'), may hold values from 0 to 1
- target_tiles: int32 [64, 128, 128], P('tile'), may hold values 0 or 1
- kernels: float32 [2, 8, 6, 25, 25], P(None, 'depth'), may hold values from -0.25 to 0.25
- socs_weights: float32 [8, 6], P('depth'), may hold values from 0.1 to 1
- thresholds: float32 [8], P('depth'), may hold values from 0.8 to 2.4
- partner_table: int32 [64], P('tile'), may hold values from 0 to 63, as said below
- mirror_flags: int32 [64], P('tile'), may hold values from 0 to 1, as said below
Outputs:
- mask_final: float32 [64, 128, 128], P('tile')
- step_gradient: float32 [64, 128, 128], P('tile')
The draws below stay inside these ranges and needn't reach their ends.
Inputs may be any that keep to these rules, and one draw needn't show every extreme that they name: partner_table[t] is t itself or t XOR 2^b for some bit b, and partner_table[partner_table[t]] = t. mirror_flags is equal for the two tiles of a matched pair.
All inputs are finite; a program needn't handle non-finite values. No bound on the sum of `target_tiles` on one device may be relied on, other than what follows from the above.
Results may differ from the reference program's by a relative error of at most 0.0003.
Values sent between devices are 32-bit elements; how exact they have to be, the bound alone decides.
A program may use at most 128 MiB of HBM per device.

```python
import math
import jax
import jax.numpy as jnp
from jax import lax

HALO = 12
CORE = 128
FRAME = 152
KSIZE = 25
KERN = 6
PLANES = 8
TILES_DEV = 2
TILES = 64
STEPS = 2
N_TILE = 32


def matching(key):
    nbits = TILES.bit_length() - 1
    tile_ids = jnp.arange(TILES, dtype=jnp.int32)
    partner = tile_ids
    for rounds in range(4):
        chosen = jax.random.randint(jax.random.fold_in(key, 11 + rounds), (TILES,), 0, nbits)
        candidate = jnp.bitwise_xor(tile_ids, jnp.left_shift(jnp.int32(1), chosen))
        unmatched = partner == tile_ids
        accept = unmatched & unmatched[candidate] & (chosen[candidate] == chosen)
        partner = jnp.where(accept, candidate, partner)
    flips = jax.random.randint(jax.random.fold_in(key, 29), (TILES,), 0, 2)
    mirror = flips[jnp.minimum(tile_ids, partner)]
    return (partner.astype(jnp.int32), mirror.astype(jnp.int32))


def draw_partner_table(key, part):
    return matching(jax.random.fold_in(key, 5))[0]


def draw_mirror_flags(key, part):
    return matching(jax.random.fold_in(key, 5))[1]


def set_ends(drawn, own_key, least, top_value):
    longest = drawn.shape.index(max(drawn.shape))
    spots = []
    for shift in (0, 1):
        where = [jax.random.randint(jax.random.fold_in(own_key, axis), (), 0, length) for axis, length in enumerate(drawn.shape)]
        where[longest] = (where[longest] + shift) % drawn.shape[longest]
        spots.append(tuple(where))
    return drawn.at[spots[0]].set(least).at[spots[1]].set(top_value)


def block_levels(stream_key, dims, cuts, low, largest):
    factor_of = 1.0
    for axis_at, blocks in cuts:
        steps = jax.random.uniform(jax.random.fold_in(jax.random.fold_in(stream_key, 6), axis_at), (blocks,), jnp.float32, low / len(cuts), largest / len(cuts))
        factor_of = factor_of * jnp.repeat(jnp.exp(steps), dims[axis_at] // blocks).reshape((-1,) + (1,) * (len(dims) - 1 - axis_at))
    return factor_of


def gaussian(own_key, shape, spread, limit, pieces=(), kind=jnp.bfloat16):
    values = jax.random.normal(own_key, shape, jnp.float32) * spread
    if len(pieces) > 0:
        values = block_levels(own_key, shape, pieces, -0.22, 0.18) * values
    return jnp.clip(values, min=-limit, max=limit).astype(kind)


def setup_inputs(seed: int = 0) -> dict:
    streams_of = jax.random.split(jax.random.key(seed), 8)
    mask_tiles = jnp.clip(1.0 * jax.random.uniform(streams_of[0], (TILES, CORE, CORE), jnp.float32) ** block_levels(streams_of[0], (TILES, CORE, CORE), ((0, 32),), -0.2, 0.2), 0.0, 1.0)
    target_tiles = set_ends((jax.random.randint(streams_of[1], (TILES, CORE, CORE), 0, 2) < 1).astype(jnp.int32), jax.random.fold_in(streams_of[1], 1), 0, 1)
    kernels = gaussian(streams_of[2], (2, PLANES, KERN, KSIZE, KSIZE), (KSIZE * KSIZE) ** -0.5, 0.25, ((1, 8),), jnp.float32)
    socs_weights = jnp.clip(jnp.exp(math.log(1.0) - 2.3025851 * jax.random.uniform(streams_of[3], (PLANES, KERN), jnp.float32) ** block_levels(streams_of[3], (PLANES, KERN), ((0, 8),), -0.2, 0.2)), 0.1, 1.0)
    thresholds = jnp.clip(0.8 + 1.6000001 * jax.random.uniform(streams_of[4], (PLANES,), jnp.float32) ** block_levels(streams_of[4], (PLANES,), ((0, 8),), -0.2, 0.2), 0.8, 2.4)
    partner_table = draw_partner_table(jax.random.fold_in(streams_of[7], 71), 0)
    mirror_flags = draw_mirror_flags(jax.random.fold_in(streams_of[7], 71), 0)
    return {"mask_tiles": mask_tiles, "target_tiles": target_tiles, "kernels": kernels, "socs_weights": socs_weights, "thresholds": thresholds, "partner_table": partner_table, "mirror_flags": mirror_flags}


steepness = 3.0
step_rate = 0.05


def kernel_spectra(kernels):
    complex_kern = kernels[0] + 1j * kernels[1]
    padded = jnp.pad(complex_kern, ((0, 0), (0, 0), (0, FRAME - KSIZE), (0, FRAME - KSIZE)))
    rolled = jnp.roll(padded, (-HALO, -HALO), axis=(2, 3))
    return jnp.fft.fft2(rolled)


def frame_gradient(frame_data, target_core, spectra, socs_weights, thresholds):
    spectrum = jnp.fft.fft2(frame_data)
    fields = jnp.fft.ifft2(spectra * spectrum[None, None])
    intensity = jnp.sum(socs_weights[:, :, None, None] * (fields.real ** 2 + fields.imag ** 2), axis=1)
    interior = intensity[:, HALO:HALO + CORE, HALO:HALO + CORE]
    resist = jax.nn.sigmoid(steepness * (interior - thresholds[:, None, None]))
    slope = 2.0 * (resist - target_core[None]) * steepness * resist * (1.0 - resist)
    full_slope = jnp.pad(slope, ((0, 0), (HALO, HALO), (HALO, HALO)))
    factor = 2.0 * socs_weights[:, :, None, None] * full_slope[:, None]
    back = jnp.sum(jnp.conj(spectra) * jnp.fft.fft2(factor * fields), axis=(0, 1))
    return jnp.fft.ifft2(back).real


def reference(mask_tiles, target_tiles, kernels, socs_weights, thresholds, partner_table, mirror_flags):
    spectra = kernel_spectra(kernels)
    target_f = target_tiles.astype(jnp.float32)
    step_gradient = jnp.zeros_like(mask_tiles)
    tile_ids = jnp.arange(TILES, dtype=jnp.int32)
    for step_index in range(STEPS):
        picture = mask_tiles.reshape(N_TILE, TILES_DEV, CORE, CORE).transpose(1, 2, 0, 3)
        picture = picture.reshape(TILES_DEV * CORE, N_TILE * CORE)
        padded = jnp.pad(picture, HALO)

        def accumulate(canvas, inputs):
            tile_index, target_core = inputs
            row_start = ((tile_index % TILES_DEV) * CORE).astype(jnp.int32)
            col_start = ((tile_index // TILES_DEV) * CORE).astype(jnp.int32)
            frame_data = lax.dynamic_slice(padded, (row_start, col_start), (FRAME, FRAME))
            frame_grad = frame_gradient(frame_data, target_core, spectra, socs_weights, thresholds)
            current = lax.dynamic_slice(canvas, (row_start, col_start), (FRAME, FRAME))
            canvas = lax.dynamic_update_slice(canvas, current + frame_grad, (row_start, col_start))
            return canvas, None

        canvas, unused = lax.scan(accumulate, jnp.zeros(padded.shape, jnp.float32), (tile_ids, target_f))
        inner = canvas[HALO:HALO + TILES_DEV * CORE, HALO:HALO + N_TILE * CORE]
        gradient = inner.reshape(TILES_DEV, CORE, N_TILE, CORE).transpose(2, 0, 1, 3).reshape(TILES, CORE, CORE)
        partner_vals = gradient[partner_table]
        flipped = jnp.where((mirror_flags == 1)[:, None, None], partner_vals[:, :, ::-1], partner_vals)
        step_gradient = 0.5 * (gradient + flipped)
        mask_tiles = mask_tiles - step_rate * step_gradient
    return mask_tiles, step_gradient
```

```python
import jax
import jax.numpy as jnp
import numpy as np
from jax import lax
from jax.sharding import PartitionSpec as P

HALO = 12
FRAME = 152
KSIZE = 25
STEPS = 2


steepness = 3.0
step_rate = 0.05


def extended_2(cells, sides, width):
    for axis, dim in sides:
        count = lax.axis_size(axis)
        ends = count - 1
        head = lax.slice_in_dim(cells, 0, width, axis=dim)
        tail = lax.slice_in_dim(cells, cells.shape[dim] - width, cells.shape[dim], axis=dim)
        cells = jnp.concatenate(
            [
                lax.ppermute(tail, axis, [(i, (i + 1) % count) for i in range(ends)]),
                cells,
                lax.ppermute(head, axis, [((i + 1) % count, i) for i in range(ends)]),
            ],
            axis=dim,
        )
    return cells


def mult_left(matrix, values):
    return jnp.einsum("jk,...kl->...jl", matrix, values, precision=lax.Precision.HIGHEST)


def mult_right(values, matrix):
    return jnp.einsum("...jk,kl->...jl", values, matrix, precision=lax.Precision.HIGHEST)


def left_apply(cos_table, sin_table, sign, real_in, imag_in):
    if imag_in is None:
        return (mult_left(cos_table, real_in), sign * mult_left(sin_table, real_in))
    real_out = mult_left(cos_table, real_in) - sign * mult_left(sin_table, imag_in)
    imag_out = mult_left(cos_table, imag_in) + sign * mult_left(sin_table, real_in)
    return (real_out, imag_out)


def right_apply(real_in, imag_in, cos_table, sin_table, sign):
    real_out = mult_right(real_in, cos_table) - sign * mult_right(imag_in, sin_table)
    imag_out = mult_right(imag_in, cos_table) + sign * mult_right(real_in, sin_table)
    return (real_out, imag_out)


def angle_tables(rows_idx, cols_idx, points):
    product = rows_idx[:, None] * cols_idx[None, :] % points
    theta = product.astype(jnp.float32) * (2.0 * np.pi / points)
    return (jnp.cos(theta), jnp.sin(theta))


def frame_gradient(
    frame_data, target_core, spec_re, spec_im, weights, levels, cos_table, sin_table
):
    points = frame_data.shape[0]
    core = target_core.shape[0]
    scale = 1.0 / (points * points)
    freq_re, freq_im = left_apply(cos_table, sin_table, -1.0, frame_data, None)
    freq_re, freq_im = right_apply(freq_re, freq_im, cos_table, sin_table, -1.0)
    prod_re = spec_re[0] * freq_re - spec_im[0] * freq_im
    prod_im = spec_re[0] * freq_im + spec_im[0] * freq_re
    field_re, field_im = left_apply(cos_table, sin_table, 1.0, prod_re, prod_im)
    field_re, field_im = right_apply(field_re, field_im, cos_table, sin_table, 1.0)
    field_re = field_re * scale
    field_im = field_im * scale
    plane_weights = weights[0][:, None, None]
    intensity = jnp.sum(plane_weights * (field_re * field_re + field_im * field_im), axis=0)
    interior = intensity[HALO : HALO + core, HALO : HALO + core]
    resist = jax.nn.sigmoid(steepness * (interior - levels[0]))
    slope = 2.0 * (resist - target_core) * steepness * resist * (1.0 - resist)
    factor = 2.0 * plane_weights * jnp.pad(slope, HALO)[None]
    back_re, back_im = left_apply(cos_table, sin_table, -1.0, factor * field_re, factor * field_im)
    back_re, back_im = right_apply(back_re, back_im, cos_table, sin_table, -1.0)
    total_re = jnp.sum(spec_re[0] * back_re + spec_im[0] * back_im, axis=0)
    total_im = jnp.sum(spec_re[0] * back_im - spec_im[0] * back_re, axis=0)
    upper_re, upper_im = left_apply(cos_table, sin_table, 1.0, total_re, total_im)
    return (mult_right(upper_re, cos_table) - mult_right(upper_im, sin_table)) * scale


def depth_sum(values):
    count = lax.axis_size("depth")
    shift = 1
    while shift < count:
        values = values + lax.ppermute(values, "depth", [(i, i ^ shift) for i in range(count)])
        shift *= 2
    return values


def blend(values, partner_local, mirror_local):
    count = lax.axis_size("tile")
    tiles_dev = values.shape[0]
    me = lax.axis_index("tile")
    own_ids = me * tiles_dev + jnp.arange(tiles_dev, dtype=jnp.int32)
    partner_vals = values
    for local in range(tiles_dev):
        partner_vals = jnp.where(
            (partner_local == own_ids[local])[:, None, None], values[local][None], partner_vals
        )
    shift = 1
    while shift < count:
        got = lax.ppermute(values, "tile", [(i, i ^ shift) for i in range(count)])
        source_ids = (me ^ shift) * tiles_dev + jnp.arange(tiles_dev, dtype=jnp.int32)
        for local in range(tiles_dev):
            partner_vals = jnp.where(
                (partner_local == source_ids[local])[:, None, None], got[local][None], partner_vals
            )
        shift *= 2
    flipped = jnp.where((mirror_local == 1)[:, None, None], partner_vals[:, :, ::-1], partner_vals)
    return 0.5 * (values + flipped)


def per_device(
    mask_tiles, target_tiles, kernels, socs_weights, thresholds, partner_table, mirror_flags
):
    tiles_dev, core, unused_width = mask_tiles.shape
    points = FRAME
    index_full = jnp.arange(points, dtype=jnp.int32)
    cos_table, sin_table = angle_tables(index_full, index_full, points)
    offsets = jnp.arange(KSIZE, dtype=jnp.int32) - HALO
    cos_small, sin_small = angle_tables(index_full, offsets, points)
    spec_re, spec_im = left_apply(cos_small, sin_small, -1.0, kernels[0], kernels[1])
    spec_re, spec_im = right_apply(spec_re, spec_im, cos_small.T, sin_small.T, -1.0)
    target_f = target_tiles.astype(jnp.float32)
    strip_height = tiles_dev * core
    step_gradient = jnp.zeros_like(mask_tiles)
    for step_index in range(STEPS):
        strip_rows = mask_tiles.reshape(strip_height, core)
        extended = extended_2(strip_rows, (("tile", 1),), HALO)
        padded = jnp.pad(extended, ((HALO, HALO), (0, 0)))
        canvas = jnp.zeros((strip_height + 2 * HALO, points), jnp.float32)
        for row_index in range(tiles_dev):
            frame_data = padded[row_index * core : row_index * core + points]
            frame_grad = frame_gradient(
                frame_data,
                target_f[row_index],
                spec_re,
                spec_im,
                socs_weights,
                thresholds,
                cos_table,
                sin_table,
            )
            canvas = canvas.at[row_index * core : row_index * core + points].add(frame_grad)
        interior = canvas[HALO : HALO + strip_height]
        rim_cols = jnp.concatenate([interior[:, :HALO], interior[:, HALO + core :]], axis=1)
        received = extended_2(rim_cols, (("tile", 1),), HALO)
        middle = interior[:, HALO : HALO + core]
        middle = middle.at[:, :HALO].add(received[:, :HALO])
        middle = middle.at[:, core - HALO :].add(received[:, 3 * HALO :])
        gradient = middle.reshape(tiles_dev, core, core)
        summed = depth_sum(gradient)
        step_gradient = blend(summed, partner_table, mirror_flags)
        mask_tiles = mask_tiles - step_rate * step_gradient
    return (mask_tiles, step_gradient)


def solution(mesh):
    return jax.shard_map(
        per_device,
        mesh=mesh,
        in_specs=(
            P("tile", None, None),
            P("tile", None, None),
            P(None, "depth", None, None, None),
            P("depth", None),
            P("depth"),
            P("tile"),
            P("tile"),
        ),
        out_specs=(P("tile", None, None), P("tile", None, None)),
        check_vma=False,
    )
```

```python
import jax
import jax.numpy as jnp
import numpy as np
from jax import lax
from jax.sharding import PartitionSpec as P

HALO = 12
FRAME = 152
KSIZE = 25
STEPS = 2


steepness = 3.0
step_rate = 0.05


def extended_2(cells, sides, width):
    for axis, dim in sides:
        count = lax.axis_size(axis)
        ends = count - 1
        head = lax.slice_in_dim(cells, 0, width, axis=dim)
        tail = lax.slice_in_dim(cells, cells.shape[dim] - width, cells.shape[dim], axis=dim)
        cells = jnp.concatenate(
            [
                lax.ppermute(tail, axis, [(i, (i + 1) % count) for i in range(ends)]),
                cells,
                lax.ppermute(head, axis, [((i + 1) % count, i) for i in range(ends)]),
            ],
            axis=dim,
        )
    return cells


def mult_left(matrix, values):
    return jnp.einsum("jk,...kl->...jl", matrix, values, precision=lax.Precision.HIGH)


def mult_right(values, matrix):
    return jnp.einsum("...jk,kl->...jl", values, matrix, precision=lax.Precision.HIGH)


def left_apply(cos_table, sin_table, sign, real_in, imag_in):
    if imag_in is None:
        return (mult_left(cos_table, real_in), sign * mult_left(sin_table, real_in))
    real_out = mult_left(cos_table, real_in) - sign * mult_left(sin_table, imag_in)
    imag_out = mult_left(cos_table, imag_in) + sign * mult_left(sin_table, real_in)
    return (real_out, imag_out)


def right_apply(real_in, imag_in, cos_table, sin_table, sign):
    real_out = mult_right(real_in, cos_table) - sign * mult_right(imag_in, sin_table)
    imag_out = mult_right(imag_in, cos_table) + sign * mult_right(real_in, sin_table)
    return (real_out, imag_out)


def angle_tables(rows_idx, cols_idx, points):
    product = rows_idx[:, None] * cols_idx[None, :] % points
    theta = product.astype(jnp.float32) * (2.0 * np.pi / points)
    return (jnp.cos(theta), jnp.sin(theta))


def frame_gradient(
    frame_data, target_core, spec_re, spec_im, weights, levels, cos_table, sin_table
):
    points = frame_data.shape[0]
    core = target_core.shape[0]
    scale = 1.0 / (points * points)
    freq_re, freq_im = left_apply(cos_table, sin_table, -1.0, frame_data, None)
    freq_re, freq_im = right_apply(freq_re, freq_im, cos_table, sin_table, -1.0)
    prod_re = spec_re[0] * freq_re - spec_im[0] * freq_im
    prod_im = spec_re[0] * freq_im + spec_im[0] * freq_re
    field_re, field_im = left_apply(cos_table, sin_table, 1.0, prod_re, prod_im)
    field_re, field_im = right_apply(field_re, field_im, cos_table, sin_table, 1.0)
    field_re = field_re * scale
    field_im = field_im * scale
    plane_weights = weights[0][:, None, None]
    intensity = jnp.sum(plane_weights * (field_re * field_re + field_im * field_im), axis=0)
    interior = intensity[HALO : HALO + core, HALO : HALO + core]
    resist = jax.nn.sigmoid(steepness * (interior - levels[0]))
    slope = 2.0 * (resist - target_core) * steepness * resist * (1.0 - resist)
    factor = 2.0 * plane_weights * jnp.pad(slope, HALO)[None]
    back_re, back_im = left_apply(cos_table, sin_table, -1.0, factor * field_re, factor * field_im)
    back_re, back_im = right_apply(back_re, back_im, cos_table, sin_table, -1.0)
    total_re = jnp.sum(spec_re[0] * back_re + spec_im[0] * back_im, axis=0)
    total_im = jnp.sum(spec_re[0] * back_im - spec_im[0] * back_re, axis=0)
    upper_re, upper_im = left_apply(cos_table, sin_table, 1.0, total_re, total_im)
    return (mult_right(upper_re, cos_table) - mult_right(upper_im, sin_table)) * scale


def depth_sum(values):
    count = lax.axis_size("depth")
    shift = 1
    while shift < count:
        values = values + lax.ppermute(values, "depth", [(i, i ^ shift) for i in range(count)])
        shift *= 2
    return values


def blend(values, partner_local, mirror_local):
    count = lax.axis_size("tile")
    tiles_dev = values.shape[0]
    me = lax.axis_index("tile")
    own_ids = me * tiles_dev + jnp.arange(tiles_dev, dtype=jnp.int32)
    partner_vals = values
    for local in range(tiles_dev):
        partner_vals = jnp.where(
            (partner_local == own_ids[local])[:, None, None], values[local][None], partner_vals
        )
    shift = 1
    while shift < count:
        got = lax.ppermute(values, "tile", [(i, i ^ shift) for i in range(count)])
        source_ids = (me ^ shift) * tiles_dev + jnp.arange(tiles_dev, dtype=jnp.int32)
        for local in range(tiles_dev):
            partner_vals = jnp.where(
                (partner_local == source_ids[local])[:, None, None], got[local][None], partner_vals
            )
        shift *= 2
    flipped = jnp.where((mirror_local == 1)[:, None, None], partner_vals[:, :, ::-1], partner_vals)
    return 0.5 * (values + flipped)


def per_device(
    mask_tiles, target_tiles, kernels, socs_weights, thresholds, partner_table, mirror_flags
):
    tiles_dev, core, unused_width = mask_tiles.shape
    points = FRAME
    index_full = jnp.arange(points, dtype=jnp.int32)
    cos_table, sin_table = angle_tables(index_full, index_full, points)
    offsets = jnp.arange(KSIZE, dtype=jnp.int32) - HALO
    cos_small, sin_small = angle_tables(index_full, offsets, points)
    spec_re, spec_im = left_apply(cos_small, sin_small, -1.0, kernels[0], kernels[1])
    spec_re, spec_im = right_apply(spec_re, spec_im, cos_small.T, sin_small.T, -1.0)
    target_f = target_tiles.astype(jnp.float32)
    strip_height = tiles_dev * core
    step_gradient = jnp.zeros_like(mask_tiles)
    for step_index in range(STEPS):
        strip_rows = mask_tiles.reshape(strip_height, core)
        extended = extended_2(strip_rows, (("tile", 1),), HALO)
        padded = jnp.pad(extended, ((HALO, HALO), (0, 0)))
        canvas = jnp.zeros((strip_height + 2 * HALO, points), jnp.float32)
        for row_index in range(tiles_dev):
            frame_data = padded[row_index * core : row_index * core + points]
            frame_grad = frame_gradient(
                frame_data,
                target_f[row_index],
                spec_re,
                spec_im,
                socs_weights,
                thresholds,
                cos_table,
                sin_table,
            )
            canvas = canvas.at[row_index * core : row_index * core + points].add(frame_grad)
        interior = canvas[HALO : HALO + strip_height]
        rim_cols = jnp.concatenate([interior[:, :HALO], interior[:, HALO + core :]], axis=1)
        received = extended_2(rim_cols, (("tile", 1),), HALO)
        middle = interior[:, HALO : HALO + core]
        middle = middle.at[:, :HALO].add(received[:, :HALO])
        middle = middle.at[:, core - HALO :].add(received[:, 3 * HALO :])
        gradient = middle.reshape(tiles_dev, core, core)
        summed = depth_sum(gradient)
        step_gradient = blend(summed, partner_table, mirror_flags)
        mask_tiles = mask_tiles - step_rate * step_gradient
    return (mask_tiles, step_gradient)


def solution(mesh):
    return jax.shard_map(
        per_device,
        mesh=mesh,
        in_specs=(
            P("tile", None, None),
            P("tile", None, None),
            P(None, "depth", None, None, None),
            P("depth", None),
            P("depth"),
            P("tile"),
            P("tile"),
        ),
        out_specs=(P("tile", None, None), P("tile", None, None)),
        check_vma=False,
    )
```

```python
import functools

import jax
import jax.numpy as jnp
import numpy as np
from jax import lax
from jax.experimental import pallas as pl
from jax.experimental.pallas import tpu as pltpu
from jax.sharding import PartitionSpec as P

MESH = pl.DeviceIdType.MESH

HALO = 12
FRAME = 152
KSIZE = 25
STEPS = 2


steepness = 3.0
step_rate = 0.05


def extended_2(cells, sides, width):
    for axis, dim in sides:
        count = lax.axis_size(axis)
        ends = count - 1
        head = lax.slice_in_dim(cells, 0, width, axis=dim)
        tail = lax.slice_in_dim(cells, cells.shape[dim] - width, cells.shape[dim], axis=dim)
        cells = jnp.concatenate(
            [
                lax.ppermute(tail, axis, [(i, (i + 1) % count) for i in range(ends)]),
                cells,
                lax.ppermute(head, axis, [((i + 1) % count, i) for i in range(ends)]),
            ],
            axis=dim,
        )
    return cells


def mult_left(matrix, values):
    return jnp.einsum("jk,...kl->...jl", matrix, values, precision=lax.Precision.HIGH)


def mult_right(values, matrix):
    return jnp.einsum("...jk,kl->...jl", values, matrix, precision=lax.Precision.HIGH)


def left_apply(cos_table, sin_table, sign, real_in, imag_in):
    if imag_in is None:
        return (mult_left(cos_table, real_in), sign * mult_left(sin_table, real_in))
    real_out = mult_left(cos_table, real_in) - sign * mult_left(sin_table, imag_in)
    imag_out = mult_left(cos_table, imag_in) + sign * mult_left(sin_table, real_in)
    return (real_out, imag_out)


def right_apply(real_in, imag_in, cos_table, sin_table, sign):
    real_out = mult_right(real_in, cos_table) - sign * mult_right(imag_in, sin_table)
    imag_out = mult_right(imag_in, cos_table) + sign * mult_right(real_in, sin_table)
    return (real_out, imag_out)


def angle_tables(rows_idx, cols_idx, points):
    product = rows_idx[:, None] * cols_idx[None, :] % points
    theta = product.astype(jnp.float32) * (2.0 * np.pi / points)
    return (jnp.cos(theta), jnp.sin(theta))


def frame_gradient(
    frame_data, target_core, spec_re, spec_im, weights, levels, cos_table, sin_table
):
    points = frame_data.shape[0]
    core = target_core.shape[0]
    scale = 1.0 / (points * points)
    freq_re, freq_im = left_apply(cos_table, sin_table, -1.0, frame_data, None)
    freq_re, freq_im = right_apply(freq_re, freq_im, cos_table, sin_table, -1.0)
    prod_re = spec_re[0] * freq_re - spec_im[0] * freq_im
    prod_im = spec_re[0] * freq_im + spec_im[0] * freq_re
    field_re, field_im = left_apply(cos_table, sin_table, 1.0, prod_re, prod_im)
    field_re, field_im = right_apply(field_re, field_im, cos_table, sin_table, 1.0)
    field_re = field_re * scale
    field_im = field_im * scale
    plane_weights = weights[0][:, None, None]
    intensity = jnp.sum(plane_weights * (field_re * field_re + field_im * field_im), axis=0)
    interior = intensity[HALO : HALO + core, HALO : HALO + core]
    resist = jax.nn.sigmoid(steepness * (interior - levels[0]))
    slope = 2.0 * (resist - target_core) * steepness * resist * (1.0 - resist)
    factor = 2.0 * plane_weights * jnp.pad(slope, HALO)[None]
    back_re, back_im = left_apply(cos_table, sin_table, -1.0, factor * field_re, factor * field_im)
    back_re, back_im = right_apply(back_re, back_im, cos_table, sin_table, -1.0)
    total_re = jnp.sum(spec_re[0] * back_re + spec_im[0] * back_im, axis=0)
    total_im = jnp.sum(spec_re[0] * back_im - spec_im[0] * back_re, axis=0)
    upper_re, upper_im = left_apply(cos_table, sin_table, 1.0, total_re, total_im)
    return (mult_right(upper_re, cos_table) - mult_right(upper_im, sin_table)) * scale


def flip_bit(value, shift):
    bit = (value // shift) % 2
    return value + shift * (1 - 2 * bit)


def exchange_kernel(
    n_tile, n_depth, x_ref, g_ref, nb_ref, recv_a, recv_b, g_send, send_a, rsem_a, send_b, rsem_b
):
    me_t = lax.axis_index("tile")
    me_d = lax.axis_index("depth")
    shifts = []
    shift = 1
    while shift < n_tile:
        shifts.append(shift)
        shift *= 2
    barrier = pltpu.get_barrier_semaphore()
    for step in range(1, n_depth):
        pl.semaphore_signal(
            barrier, inc=1, device_id=(me_t, (me_d + step) % n_depth), device_id_type=MESH
        )
    for shift in shifts:
        pl.semaphore_signal(
            barrier, inc=1, device_id=(flip_bit(me_t, shift), me_d), device_id_type=MESH
        )
    pl.semaphore_wait(barrier, n_depth - 1 + len(shifts))

    recv_a[me_d] = x_ref[...]
    sends = []
    for step in range(1, n_depth):
        copy = pltpu.make_async_remote_copy(
            src_ref=x_ref,
            dst_ref=recv_a.at[me_d],
            send_sem=send_a.at[step],
            recv_sem=rsem_a.at[me_d],
            device_id=(me_t, (me_d + step) % n_depth),
            device_id_type=MESH,
        )
        copy.start()
        sends.append(copy)
    for step in range(1, n_depth):
        source = (me_d + n_depth - step) % n_depth
        pltpu.make_async_remote_copy(
            src_ref=x_ref,
            dst_ref=recv_a.at[source],
            send_sem=send_a.at[step],
            recv_sem=rsem_a.at[source],
            device_id=(me_t, source),
            device_id_type=MESH,
        ).wait_recv()
    for copy in sends:
        copy.wait_send()
    total = recv_a[0]
    for slot in range(1, n_depth):
        total = total + recv_a[slot]
    g_send[...] = total
    g_ref[...] = total

    swaps = []
    for slot, shift in enumerate(shifts):
        copy = pltpu.make_async_remote_copy(
            src_ref=g_send,
            dst_ref=recv_b.at[slot],
            send_sem=send_b.at[slot],
            recv_sem=rsem_b.at[slot],
            device_id=(flip_bit(me_t, shift), me_d),
            device_id_type=MESH,
        )
        copy.start()
        swaps.append(copy)
    for copy in swaps:
        copy.wait_recv()
    for copy in swaps:
        copy.wait_send()
    nb_ref[...] = recv_b[...]


def exchange(values, call_id):
    n_tile = lax.axis_size("tile")
    n_depth = lax.axis_size("depth")
    n_shift = max(n_tile - 1, 1).bit_length()
    shape = values.shape
    vmem = pl.BlockSpec(memory_space=pltpu.VMEM)
    return pl.pallas_call(
        functools.partial(exchange_kernel, n_tile, n_depth),
        out_shape=(
            jax.ShapeDtypeStruct(shape, jnp.float32),
            jax.ShapeDtypeStruct((n_shift,) + shape, jnp.float32),
        ),
        in_specs=[vmem],
        out_specs=(vmem, vmem),
        scratch_shapes=[
            pltpu.VMEM((n_depth,) + shape, jnp.float32),
            pltpu.VMEM((n_shift,) + shape, jnp.float32),
            pltpu.VMEM(shape, jnp.float32),
            pltpu.SemaphoreType.DMA((n_depth,)),
            pltpu.SemaphoreType.DMA((n_depth,)),
            pltpu.SemaphoreType.DMA((n_shift,)),
            pltpu.SemaphoreType.DMA((n_shift,)),
        ],
        compiler_params=pltpu.CompilerParams(collective_id=call_id, has_side_effects=True),
    )(values)


def blend(values, neighbours, partner_local, mirror_local):
    tiles_dev = values.shape[0]
    me = lax.axis_index("tile")
    own_ids = me * tiles_dev + jnp.arange(tiles_dev, dtype=jnp.int32)
    partner_vals = values
    for local in range(tiles_dev):
        partner_vals = jnp.where(
            (partner_local == own_ids[local])[:, None, None], values[local][None], partner_vals
        )
    shift = 1
    for slot in range(neighbours.shape[0]):
        got = neighbours[slot]
        source_ids = (me ^ shift) * tiles_dev + jnp.arange(tiles_dev, dtype=jnp.int32)
        for local in range(tiles_dev):
            partner_vals = jnp.where(
                (partner_local == source_ids[local])[:, None, None], got[local][None], partner_vals
            )
        shift *= 2
    flipped = jnp.where((mirror_local == 1)[:, None, None], partner_vals[:, :, ::-1], partner_vals)
    return 0.5 * (values + flipped)


def per_device(
    mask_tiles, target_tiles, kernels, socs_weights, thresholds, partner_table, mirror_flags
):
    tiles_dev, core, unused_width = mask_tiles.shape
    points = FRAME
    index_full = jnp.arange(points, dtype=jnp.int32)
    cos_table, sin_table = angle_tables(index_full, index_full, points)
    offsets = jnp.arange(KSIZE, dtype=jnp.int32) - HALO
    cos_small, sin_small = angle_tables(index_full, offsets, points)
    spec_re, spec_im = left_apply(cos_small, sin_small, -1.0, kernels[0], kernels[1])
    spec_re, spec_im = right_apply(spec_re, spec_im, cos_small.T, sin_small.T, -1.0)
    target_f = target_tiles.astype(jnp.float32)
    strip_height = tiles_dev * core
    step_gradient = jnp.zeros_like(mask_tiles)
    for step_index in range(STEPS):
        strip_rows = mask_tiles.reshape(strip_height, core)
        extended = extended_2(strip_rows, (("tile", 1),), HALO)
        padded = jnp.pad(extended, ((HALO, HALO), (0, 0)))
        canvas = jnp.zeros((strip_height + 2 * HALO, points), jnp.float32)
        for row_index in range(tiles_dev):
            frame_data = padded[row_index * core : row_index * core + points]
            frame_grad = frame_gradient(
                frame_data,
                target_f[row_index],
                spec_re,
                spec_im,
                socs_weights,
                thresholds,
                cos_table,
                sin_table,
            )
            canvas = canvas.at[row_index * core : row_index * core + points].add(frame_grad)
        interior = canvas[HALO : HALO + strip_height]
        rim_cols = jnp.concatenate([interior[:, :HALO], interior[:, HALO + core :]], axis=1)
        received = extended_2(rim_cols, (("tile", 1),), HALO)
        middle = interior[:, HALO : HALO + core]
        middle = middle.at[:, :HALO].add(received[:, :HALO])
        middle = middle.at[:, core - HALO :].add(received[:, 3 * HALO :])
        gradient = middle.reshape(tiles_dev, core, core)
        summed, neighbours = exchange(gradient, step_index)
        step_gradient = blend(summed, neighbours, partner_table, mirror_flags)
        mask_tiles = mask_tiles - step_rate * step_gradient
    return (mask_tiles, step_gradient)


def solution(mesh):
    return jax.shard_map(
        per_device,
        mesh=mesh,
        in_specs=(
            P("tile", None, None),
            P("tile", None, None),
            P(None, "depth", None, None, None),
            P("depth", None),
            P("depth"),
            P("tile"),
            P("tile"),
        ),
        out_specs=(P("tile", None, None), P("tile", None, None)),
        check_vma=False,
    )
```

```python
import functools

import jax
import jax.numpy as jnp
import numpy as np
from jax import lax
from jax.experimental import pallas as pl
from jax.experimental.pallas import tpu as pltpu
from jax.sharding import PartitionSpec as P

MESH = pl.DeviceIdType.MESH

HALO = 12
FRAME = 152
KSIZE = 25
STEPS = 2


steepness = 3.0
step_rate = 0.05


def extended_2(cells, sides, width):
    for axis, dim in sides:
        count = lax.axis_size(axis)
        ends = count - 1
        head = lax.slice_in_dim(cells, 0, width, axis=dim)
        tail = lax.slice_in_dim(cells, cells.shape[dim] - width, cells.shape[dim], axis=dim)
        cells = jnp.concatenate(
            [
                lax.ppermute(tail, axis, [(i, (i + 1) % count) for i in range(ends)]),
                cells,
                lax.ppermute(head, axis, [((i + 1) % count, i) for i in range(ends)]),
            ],
            axis=dim,
        )
    return cells


def mult_left(matrix, values):
    return jnp.einsum("jk,...kl->...jl", matrix, values, precision=lax.Precision.HIGH)


def mult_right(values, matrix):
    return jnp.einsum("...jk,kl->...jl", values, matrix, precision=lax.Precision.HIGH)


def left_apply(cos_table, sin_table, sign, real_in, imag_in):
    if imag_in is None:
        return (mult_left(cos_table, real_in), sign * mult_left(sin_table, real_in))
    real_out = mult_left(cos_table, real_in) - sign * mult_left(sin_table, imag_in)
    imag_out = mult_left(cos_table, imag_in) + sign * mult_left(sin_table, real_in)
    return (real_out, imag_out)


def right_apply(real_in, imag_in, cos_table, sin_table, sign):
    real_out = mult_right(real_in, cos_table) - sign * mult_right(imag_in, sin_table)
    imag_out = mult_right(imag_in, cos_table) + sign * mult_right(real_in, sin_table)
    return (real_out, imag_out)


def angle_tables(rows_idx, cols_idx, points):
    product = rows_idx[:, None] * cols_idx[None, :] % points
    theta = product.astype(jnp.float32) * (2.0 * np.pi / points)
    return (jnp.cos(theta), jnp.sin(theta))


def frame_gradient(
    frame_data, target_core, spec_re, spec_im, weights, levels, cos_table, sin_table
):
    points = frame_data.shape[0]
    core = target_core.shape[0]
    scale = 1.0 / (points * points)
    freq_re, freq_im = left_apply(cos_table, sin_table, -1.0, frame_data, None)
    freq_re, freq_im = right_apply(freq_re, freq_im, cos_table, sin_table, -1.0)
    prod_re = spec_re[0] * freq_re - spec_im[0] * freq_im
    prod_im = spec_re[0] * freq_im + spec_im[0] * freq_re
    field_re, field_im = left_apply(cos_table, sin_table, 1.0, prod_re, prod_im)
    field_re, field_im = right_apply(field_re, field_im, cos_table, sin_table, 1.0)
    field_re = field_re * scale
    field_im = field_im * scale
    plane_weights = weights[0][:, None, None]
    intensity = jnp.sum(plane_weights * (field_re * field_re + field_im * field_im), axis=0)
    interior = intensity[HALO : HALO + core, HALO : HALO + core]
    resist = jax.nn.sigmoid(steepness * (interior - levels[0]))
    slope = 2.0 * (resist - target_core) * steepness * resist * (1.0 - resist)
    factor = 2.0 * plane_weights * jnp.pad(slope, HALO)[None]
    back_re, back_im = left_apply(cos_table, sin_table, -1.0, factor * field_re, factor * field_im)
    back_re, back_im = right_apply(back_re, back_im, cos_table, sin_table, -1.0)
    total_re = jnp.sum(spec_re[0] * back_re + spec_im[0] * back_im, axis=0)
    total_im = jnp.sum(spec_re[0] * back_im - spec_im[0] * back_re, axis=0)
    upper_re, upper_im = left_apply(cos_table, sin_table, 1.0, total_re, total_im)
    return (mult_right(upper_re, cos_table) - mult_right(upper_im, sin_table)) * scale


def flip_bit(value, shift):
    bit = (value // shift) % 2
    return value + shift * (1 - 2 * bit)


def exchange_kernel(
    n_tile,
    n_depth,
    x_ref,
    partner_ref,
    mirror_ref,
    out_ref,
    recv_a,
    part_s,
    recv_b,
    blend_s,
    recv_c,
    send_a,
    rsem_a,
    send_b,
    rsem_b,
    send_c,
    rsem_c,
):
    me_t = lax.axis_index("tile")
    me_d = lax.axis_index("depth")
    tiles_dev, core, width = x_ref.shape
    rows = core // n_depth
    shifts = []
    shift = 1
    while shift < n_tile:
        shifts.append(shift)
        shift *= 2
    barrier = pltpu.get_barrier_semaphore()
    for step in range(1, n_depth):
        pl.semaphore_signal(
            barrier, inc=1, device_id=(me_t, (me_d + step) % n_depth), device_id_type=MESH
        )
    for shift in shifts:
        pl.semaphore_signal(
            barrier, inc=1, device_id=(flip_bit(me_t, shift), me_d), device_id_type=MESH
        )
    pl.semaphore_wait(barrier, n_depth - 1 + len(shifts))

    def band(index):
        return pl.ds(pl.multiple_of(index * rows, rows), rows)

    def depth_round(source_of, dst_buf, send_sem, recv_sem):
        copies = []
        for step in range(1, n_depth):
            target = (me_d + step) % n_depth
            copy = pltpu.make_async_remote_copy(
                src_ref=source_of(target),
                dst_ref=dst_buf.at[me_d],
                send_sem=send_sem.at[step],
                recv_sem=recv_sem.at[me_d],
                device_id=(me_t, target),
                device_id_type=MESH,
            )
            copy.start()
            copies.append(copy)
        for step in range(1, n_depth):
            source = (me_d + n_depth - step) % n_depth
            pltpu.make_async_remote_copy(
                src_ref=source_of(source),
                dst_ref=dst_buf.at[source],
                send_sem=send_sem.at[step],
                recv_sem=recv_sem.at[source],
                device_id=(me_t, source),
                device_id_type=MESH,
            ).wait_recv()
        for copy in copies:
            copy.wait_send()

    recv_a[me_d] = x_ref[:, band(me_d), :]
    depth_round(lambda target: x_ref.at[:, band(target), :], recv_a, send_a, rsem_a)
    total = recv_a[0]
    for slot in range(1, n_depth):
        total = total + recv_a[slot]
    part_s[...] = total

    swaps = []
    for slot, shift in enumerate(shifts):
        copy = pltpu.make_async_remote_copy(
            src_ref=part_s,
            dst_ref=recv_b.at[slot],
            send_sem=send_b.at[slot],
            recv_sem=rsem_b.at[slot],
            device_id=(flip_bit(me_t, shift), me_d),
            device_id_type=MESH,
        )
        copy.start()
        swaps.append(copy)
    for copy in swaps:
        copy.wait_recv()
    for copy in swaps:
        copy.wait_send()

    lane_a = lax.broadcasted_iota(jnp.int32, (width, width), 0)
    lane_b = lax.broadcasted_iota(jnp.int32, (width, width), 1)
    reverse = jnp.where(lane_a + lane_b == width - 1, 1.0, 0.0).astype(jnp.float32)
    for local in range(tiles_dev):
        partner = partner_ref[local]
        chosen = jnp.zeros((rows, width), jnp.float32)
        for other in range(tiles_dev):
            hit = jnp.where(partner == me_t * tiles_dev + other, 1.0, 0.0)
            chosen = chosen + hit * part_s[other]
        for slot, shift in enumerate(shifts):
            source = flip_bit(me_t, shift)
            for other in range(tiles_dev):
                hit = jnp.where(partner == source * tiles_dev + other, 1.0, 0.0)
                chosen = chosen + hit * recv_b[slot, other]
        mirrored = jnp.dot(
            chosen, reverse, precision=lax.Precision.HIGHEST, preferred_element_type=jnp.float32
        )
        use_mirror = jnp.where(mirror_ref[local] == 1, 1.0, 0.0)
        chosen = use_mirror * mirrored + (1.0 - use_mirror) * chosen
        blend_s[local] = 0.5 * (part_s[local] + chosen)

    recv_c[me_d] = blend_s[...]
    depth_round(lambda target: blend_s, recv_c, send_c, rsem_c)
    for slot in range(n_depth):
        out_ref[:, slot * rows : (slot + 1) * rows, :] = recv_c[slot]


def exchange(values, partner_local, mirror_local, call_id):
    n_tile = lax.axis_size("tile")
    n_depth = lax.axis_size("depth")
    n_shift = max(n_tile - 1, 1).bit_length()
    tiles_dev, core, width = values.shape
    piece = (tiles_dev, core // n_depth, width)
    vmem = pl.BlockSpec(memory_space=pltpu.VMEM)
    smem = pl.BlockSpec(memory_space=pltpu.SMEM)
    return pl.pallas_call(
        functools.partial(exchange_kernel, n_tile, n_depth),
        out_shape=jax.ShapeDtypeStruct(values.shape, jnp.float32),
        in_specs=[vmem, smem, smem],
        out_specs=vmem,
        scratch_shapes=[
            pltpu.VMEM((n_depth,) + piece, jnp.float32),
            pltpu.VMEM(piece, jnp.float32),
            pltpu.VMEM((n_shift,) + piece, jnp.float32),
            pltpu.VMEM(piece, jnp.float32),
            pltpu.VMEM((n_depth,) + piece, jnp.float32),
            pltpu.SemaphoreType.DMA((n_depth,)),
            pltpu.SemaphoreType.DMA((n_depth,)),
            pltpu.SemaphoreType.DMA((n_shift,)),
            pltpu.SemaphoreType.DMA((n_shift,)),
            pltpu.SemaphoreType.DMA((n_depth,)),
            pltpu.SemaphoreType.DMA((n_depth,)),
        ],
        compiler_params=pltpu.CompilerParams(collective_id=call_id, has_side_effects=True),
    )(values, partner_local, mirror_local)


def per_device(
    mask_tiles, target_tiles, kernels, socs_weights, thresholds, partner_table, mirror_flags
):
    tiles_dev, core, unused_width = mask_tiles.shape
    points = FRAME
    index_full = jnp.arange(points, dtype=jnp.int32)
    cos_table, sin_table = angle_tables(index_full, index_full, points)
    offsets = jnp.arange(KSIZE, dtype=jnp.int32) - HALO
    cos_small, sin_small = angle_tables(index_full, offsets, points)
    spec_re, spec_im = left_apply(cos_small, sin_small, -1.0, kernels[0], kernels[1])
    spec_re, spec_im = right_apply(spec_re, spec_im, cos_small.T, sin_small.T, -1.0)
    target_f = target_tiles.astype(jnp.float32)
    strip_height = tiles_dev * core
    step_gradient = jnp.zeros_like(mask_tiles)
    for step_index in range(STEPS):
        strip_rows = mask_tiles.reshape(strip_height, core)
        extended = extended_2(strip_rows, (("tile", 1),), HALO)
        padded = jnp.pad(extended, ((HALO, HALO), (0, 0)))
        canvas = jnp.zeros((strip_height + 2 * HALO, points), jnp.float32)
        for row_index in range(tiles_dev):
            frame_data = padded[row_index * core : row_index * core + points]
            frame_grad = frame_gradient(
                frame_data,
                target_f[row_index],
                spec_re,
                spec_im,
                socs_weights,
                thresholds,
                cos_table,
                sin_table,
            )
            canvas = canvas.at[row_index * core : row_index * core + points].add(frame_grad)
        interior = canvas[HALO : HALO + strip_height]
        rim_cols = jnp.concatenate([interior[:, :HALO], interior[:, HALO + core :]], axis=1)
        received = extended_2(rim_cols, (("tile", 1),), HALO)
        middle = interior[:, HALO : HALO + core]
        middle = middle.at[:, :HALO].add(received[:, :HALO])
        middle = middle.at[:, core - HALO :].add(received[:, 3 * HALO :])
        gradient = middle.reshape(tiles_dev, core, core)
        step_gradient = exchange(gradient, partner_table, mirror_flags, step_index)
        mask_tiles = mask_tiles - step_rate * step_gradient
    return (mask_tiles, step_gradient)


def solution(mesh):
    return jax.shard_map(
        per_device,
        mesh=mesh,
        in_specs=(
            P("tile", None, None),
            P("tile", None, None),
            P(None, "depth", None, None, None),
            P("depth", None),
            P("depth"),
            P("tile"),
            P("tile"),
        ),
        out_specs=(P("tile", None, None), P("tile", None, None)),
        check_vma=False,
    )
```

```python
import functools

import jax
import jax.numpy as jnp
import numpy as np
from jax import lax
from jax.experimental import pallas as pl
from jax.experimental.pallas import tpu as pltpu
from jax.sharding import PartitionSpec as P

MESH = pl.DeviceIdType.MESH

HALO = 12
FRAME = 152
KSIZE = 25
STEPS = 2


steepness = 3.0
step_rate = 0.05


def extended_2(cells, sides, width):
    for axis, dim in sides:
        count = lax.axis_size(axis)
        ends = count - 1
        head = lax.slice_in_dim(cells, 0, width, axis=dim)
        tail = lax.slice_in_dim(cells, cells.shape[dim] - width, cells.shape[dim], axis=dim)
        cells = jnp.concatenate(
            [
                lax.ppermute(tail, axis, [(i, (i + 1) % count) for i in range(ends)]),
                cells,
                lax.ppermute(head, axis, [((i + 1) % count, i) for i in range(ends)]),
            ],
            axis=dim,
        )
    return cells


def mult_left(matrix, values):
    return jnp.einsum("jk,...kl->...jl", matrix, values, precision=lax.Precision.HIGH)


def mult_right(values, matrix):
    return jnp.einsum("...jk,kl->...jl", values, matrix, precision=lax.Precision.HIGH)


def left_apply(cos_table, sin_table, sign, real_in, imag_in):
    if imag_in is None:
        return (mult_left(cos_table, real_in), sign * mult_left(sin_table, real_in))
    real_out = mult_left(cos_table, real_in) - sign * mult_left(sin_table, imag_in)
    imag_out = mult_left(cos_table, imag_in) + sign * mult_left(sin_table, real_in)
    return (real_out, imag_out)


def right_apply(real_in, imag_in, cos_table, sin_table, sign):
    real_out = mult_right(real_in, cos_table) - sign * mult_right(imag_in, sin_table)
    imag_out = mult_right(imag_in, cos_table) + sign * mult_right(real_in, sin_table)
    return (real_out, imag_out)


def angle_tables(rows_idx, cols_idx, points):
    product = rows_idx[:, None] * cols_idx[None, :] % points
    theta = product.astype(jnp.float32) * (2.0 * np.pi / points)
    return (jnp.cos(theta), jnp.sin(theta))


def split_bf16(values):
    high = lax.reduce_precision(values, exponent_bits=8, mantissa_bits=7)
    return high.astype(jnp.bfloat16), (values - high).astype(jnp.bfloat16)


def split_inside(values):
    spread = values * 65537.0
    high = spread - (spread - values)
    return high.astype(jnp.bfloat16), (values - high).astype(jnp.bfloat16)


def dot3(a_high, a_low, b_high, b_low):
    def product(a, b):
        return jnp.dot(a, b, preferred_element_type=jnp.float32)

    return product(a_high, b_high) + (product(a_high, b_low) + product(a_low, b_high))


def frame_kernel(
    points,
    frame_ref,
    target_ref,
    sre_ref,
    sim_ref,
    w_ref,
    lvl_ref,
    lhi_ref,
    llo_ref,
    rhi_ref,
    rlo_ref,
    out_ref,
    fre_s,
    fim_s,
    spec_s,
    slope_s,
    acc_s,
):
    size = frame_ref.shape[-1]
    kern = sre_ref.shape[0]
    core = points - 2 * HALO
    scale = 1.0 / (points * points)

    def left_mult(values):
        high, low = split_inside(values)
        both = dot3(lhi_ref[...], llo_ref[...], high, low)
        return both[:size], both[size:]

    def right_mult(values):
        high, low = split_inside(values)
        both = dot3(high, low, rhi_ref[...], rlo_ref[...])
        return both[:, :size], both[:, size:]

    def left(real_in, imag_in, sign):
        cos_re, sin_re = left_mult(real_in)
        cos_im, sin_im = left_mult(imag_in)
        return cos_re - sign * sin_im, cos_im + sign * sin_re

    def right(real_in, imag_in, sign):
        re_cos, re_sin = right_mult(real_in)
        im_cos, im_sin = right_mult(imag_in)
        return re_cos - sign * im_sin, im_cos + sign * re_sin

    cos_x, sin_x = left_mult(frame_ref[0])
    freq_re, freq_im = right(cos_x, -sin_x, -1.0)
    spec_s[0] = freq_re
    spec_s[1] = freq_im

    def forward(k, intensity):
        s_re = sre_ref[k]
        s_im = sim_ref[k]
        f_re = spec_s[0]
        f_im = spec_s[1]
        prod_re = s_re * f_re - s_im * f_im
        prod_im = s_re * f_im + s_im * f_re
        b_re, b_im = left(prod_re, prod_im, 1.0)
        g_re, g_im = right(b_re, b_im, 1.0)
        g_re = g_re * scale
        g_im = g_im * scale
        fre_s[k] = g_re
        fim_s[k] = g_im
        return intensity + w_ref[k] * (g_re * g_re + g_im * g_im)

    intensity = lax.fori_loop(0, kern, forward, jnp.zeros((size, size), jnp.float32))
    rows = lax.broadcasted_iota(jnp.int32, (size, size), 0)
    cols = lax.broadcasted_iota(jnp.int32, (size, size), 1)
    inside = (rows >= HALO) & (rows < HALO + core) & (cols >= HALO) & (cols < HALO + core)
    resist = 1.0 / (1.0 + jnp.exp(-(steepness * (intensity - lvl_ref[0]))))
    slope = 2.0 * (resist - target_ref[0]) * steepness * resist * (1.0 - resist)
    slope_s[...] = jnp.where(inside, slope, 0.0)
    acc_s[...] = jnp.zeros_like(acc_s)

    def backward(k, carry):
        factor = 2.0 * w_ref[k] * slope_s[...]
        b_re, b_im = left(factor * fre_s[k], factor * fim_s[k], -1.0)
        h_re, h_im = right(b_re, b_im, -1.0)
        s_re = sre_ref[k]
        s_im = sim_ref[k]
        acc_s[0] += s_re * h_re + s_im * h_im
        acc_s[1] += s_re * h_im - s_im * h_re
        return carry

    lax.fori_loop(0, kern, backward, 0)
    u_re, u_im = left(acc_s[0], acc_s[1], 1.0)
    re_cos, unused_sin = right_mult(u_re)
    unused_cos, im_sin = right_mult(u_im)
    out_ref[0] = (re_cos - im_sin) * scale


def frame_gradients(frames, targets, spec_re, spec_im, weights, levels, tables, points):
    count, size, unused = frames.shape
    kern = spec_re.shape[0]
    lhi, llo, rhi, rlo = tables
    per_frame = pl.BlockSpec((1, size, size), lambda i: (i, 0, 0))
    whole_spec = pl.BlockSpec((kern, size, size), lambda i: (0, 0, 0))
    smem = pl.BlockSpec(memory_space=pltpu.SMEM)
    flops = count * 324 * 2 * size**3
    return pl.pallas_call(
        functools.partial(frame_kernel, points),
        out_shape=jax.ShapeDtypeStruct(frames.shape, jnp.float32),
        grid=(count,),
        in_specs=[
            per_frame,
            per_frame,
            whole_spec,
            whole_spec,
            smem,
            smem,
            pl.BlockSpec((2 * size, size), lambda i: (0, 0)),
            pl.BlockSpec((2 * size, size), lambda i: (0, 0)),
            pl.BlockSpec((size, 2 * size), lambda i: (0, 0)),
            pl.BlockSpec((size, 2 * size), lambda i: (0, 0)),
        ],
        out_specs=per_frame,
        scratch_shapes=[
            pltpu.VMEM((kern, size, size), jnp.float32),
            pltpu.VMEM((kern, size, size), jnp.float32),
            pltpu.VMEM((2, size, size), jnp.float32),
            pltpu.VMEM((size, size), jnp.float32),
            pltpu.VMEM((2, size, size), jnp.float32),
        ],
        compiler_params=pltpu.CompilerParams(
            dimension_semantics=("arbitrary",), vmem_limit_bytes=48 * 1024 * 1024
        ),
        cost_estimate=pl.CostEstimate(
            flops=flops, transcendentals=count * size * size, bytes_accessed=16 * 1024 * 1024
        ),
    )(frames, targets, spec_re, spec_im, weights, levels, lhi, llo, rhi, rlo)


def flip_bit(value, shift):
    bit = (value // shift) % 2
    return value + shift * (1 - 2 * bit)


def exchange_kernel(
    n_tile,
    n_depth,
    x_ref,
    partner_ref,
    mirror_ref,
    out_ref,
    recv_a,
    part_s,
    recv_b,
    blend_s,
    recv_c,
    send_a,
    rsem_a,
    send_b,
    rsem_b,
    send_c,
    rsem_c,
):
    me_t = lax.axis_index("tile")
    me_d = lax.axis_index("depth")
    tiles_dev, core, width = x_ref.shape
    rows = core // n_depth
    shifts = []
    shift = 1
    while shift < n_tile:
        shifts.append(shift)
        shift *= 2
    barrier = pltpu.get_barrier_semaphore()
    for step in range(1, n_depth):
        pl.semaphore_signal(
            barrier, inc=1, device_id=(me_t, (me_d + step) % n_depth), device_id_type=MESH
        )
    for shift in shifts:
        pl.semaphore_signal(
            barrier, inc=1, device_id=(flip_bit(me_t, shift), me_d), device_id_type=MESH
        )
    pl.semaphore_wait(barrier, n_depth - 1 + len(shifts))

    def band(index):
        return pl.ds(pl.multiple_of(index * rows, rows), rows)

    def depth_round(source_of, dst_buf, send_sem, recv_sem):
        copies = []
        for step in range(1, n_depth):
            target = (me_d + step) % n_depth
            copy = pltpu.make_async_remote_copy(
                src_ref=source_of(target),
                dst_ref=dst_buf.at[me_d],
                send_sem=send_sem.at[step],
                recv_sem=recv_sem.at[me_d],
                device_id=(me_t, target),
                device_id_type=MESH,
            )
            copy.start()
            copies.append(copy)
        for step in range(1, n_depth):
            source = (me_d + n_depth - step) % n_depth
            pltpu.make_async_remote_copy(
                src_ref=source_of(source),
                dst_ref=dst_buf.at[source],
                send_sem=send_sem.at[step],
                recv_sem=recv_sem.at[source],
                device_id=(me_t, source),
                device_id_type=MESH,
            ).wait_recv()
        for copy in copies:
            copy.wait_send()

    recv_a[me_d] = x_ref[:, band(me_d), :]
    depth_round(lambda target: x_ref.at[:, band(target), :], recv_a, send_a, rsem_a)
    total = recv_a[0]
    for slot in range(1, n_depth):
        total = total + recv_a[slot]
    part_s[...] = total

    swaps = []
    for slot, shift in enumerate(shifts):
        copy = pltpu.make_async_remote_copy(
            src_ref=part_s,
            dst_ref=recv_b.at[slot],
            send_sem=send_b.at[slot],
            recv_sem=rsem_b.at[slot],
            device_id=(flip_bit(me_t, shift), me_d),
            device_id_type=MESH,
        )
        copy.start()
        swaps.append(copy)
    for copy in swaps:
        copy.wait_recv()
    for copy in swaps:
        copy.wait_send()

    lane_a = lax.broadcasted_iota(jnp.int32, (width, width), 0)
    lane_b = lax.broadcasted_iota(jnp.int32, (width, width), 1)
    reverse = jnp.where(lane_a + lane_b == width - 1, 1.0, 0.0).astype(jnp.float32)
    for local in range(tiles_dev):
        partner = partner_ref[local]
        chosen = jnp.zeros((rows, width), jnp.float32)
        for other in range(tiles_dev):
            hit = jnp.where(partner == me_t * tiles_dev + other, 1.0, 0.0)
            chosen = chosen + hit * part_s[other]
        for slot, shift in enumerate(shifts):
            source = flip_bit(me_t, shift)
            for other in range(tiles_dev):
                hit = jnp.where(partner == source * tiles_dev + other, 1.0, 0.0)
                chosen = chosen + hit * recv_b[slot, other]
        mirrored = jnp.dot(
            chosen, reverse, precision=lax.Precision.HIGHEST, preferred_element_type=jnp.float32
        )
        use_mirror = jnp.where(mirror_ref[local] == 1, 1.0, 0.0)
        chosen = use_mirror * mirrored + (1.0 - use_mirror) * chosen
        blend_s[local] = 0.5 * (part_s[local] + chosen)

    recv_c[me_d] = blend_s[...]
    depth_round(lambda target: blend_s, recv_c, send_c, rsem_c)
    for slot in range(n_depth):
        out_ref[:, slot * rows : (slot + 1) * rows, :] = recv_c[slot]


def exchange(values, partner_local, mirror_local, call_id):
    n_tile = lax.axis_size("tile")
    n_depth = lax.axis_size("depth")
    n_shift = max(n_tile - 1, 1).bit_length()
    tiles_dev, core, width = values.shape
    piece = (tiles_dev, core // n_depth, width)
    vmem = pl.BlockSpec(memory_space=pltpu.VMEM)
    smem = pl.BlockSpec(memory_space=pltpu.SMEM)
    return pl.pallas_call(
        functools.partial(exchange_kernel, n_tile, n_depth),
        out_shape=jax.ShapeDtypeStruct(values.shape, jnp.float32),
        in_specs=[vmem, smem, smem],
        out_specs=vmem,
        scratch_shapes=[
            pltpu.VMEM((n_depth,) + piece, jnp.float32),
            pltpu.VMEM(piece, jnp.float32),
            pltpu.VMEM((n_shift,) + piece, jnp.float32),
            pltpu.VMEM(piece, jnp.float32),
            pltpu.VMEM((n_depth,) + piece, jnp.float32),
            pltpu.SemaphoreType.DMA((n_depth,)),
            pltpu.SemaphoreType.DMA((n_depth,)),
            pltpu.SemaphoreType.DMA((n_shift,)),
            pltpu.SemaphoreType.DMA((n_shift,)),
            pltpu.SemaphoreType.DMA((n_depth,)),
            pltpu.SemaphoreType.DMA((n_depth,)),
        ],
        compiler_params=pltpu.CompilerParams(collective_id=call_id, has_side_effects=True),
    )(values, partner_local, mirror_local)


def per_device(
    mask_tiles, target_tiles, kernels, socs_weights, thresholds, partner_table, mirror_flags
):
    tiles_dev, core, unused_width = mask_tiles.shape
    points = FRAME
    index_full = jnp.arange(points, dtype=jnp.int32)
    cos_table, sin_table = angle_tables(index_full, index_full, points)
    offsets = jnp.arange(KSIZE, dtype=jnp.int32) - HALO
    cos_small, sin_small = angle_tables(index_full, offsets, points)
    spec_re, spec_im = left_apply(cos_small, sin_small, -1.0, kernels[0], kernels[1])
    spec_re, spec_im = right_apply(spec_re, spec_im, cos_small.T, sin_small.T, -1.0)
    target_f = target_tiles.astype(jnp.float32)
    size = 256
    fill = size - points
    targets = jnp.pad(target_f, ((0, 0), (HALO, size - HALO - core), (HALO, size - HALO - core)))
    spec_re_p = jnp.pad(spec_re[0], ((0, 0), (0, fill), (0, fill)))
    spec_im_p = jnp.pad(spec_im[0], ((0, 0), (0, fill), (0, fill)))
    cos_p = jnp.pad(cos_table, ((0, fill), (0, fill)))
    sin_p = jnp.pad(sin_table, ((0, fill), (0, fill)))
    lhi, llo = split_bf16(jnp.concatenate([cos_p, sin_p], axis=0))
    rhi, rlo = split_bf16(jnp.concatenate([cos_p, sin_p], axis=1))
    tables = (lhi, llo, rhi, rlo)
    strip_height = tiles_dev * core
    step_gradient = jnp.zeros_like(mask_tiles)
    for step_index in range(STEPS):
        strip_rows = mask_tiles.reshape(strip_height, core)
        extended = extended_2(strip_rows, (("tile", 1),), HALO)
        padded = jnp.pad(extended, ((HALO, HALO), (0, 0)))
        canvas = jnp.zeros((strip_height + 2 * HALO, points), jnp.float32)
        frames = jnp.stack(
            [padded[row_index * core : row_index * core + points] for row_index in range(tiles_dev)]
        )
        frames = jnp.pad(frames, ((0, 0), (0, size - points), (0, size - points)))
        grads = frame_gradients(
            frames, targets, spec_re_p, spec_im_p, socs_weights[0], thresholds, tables, points
        )
        for row_index in range(tiles_dev):
            canvas = canvas.at[row_index * core : row_index * core + points].add(
                grads[row_index, :points, :points]
            )
        interior = canvas[HALO : HALO + strip_height]
        rim_cols = jnp.concatenate([interior[:, :HALO], interior[:, HALO + core :]], axis=1)
        received = extended_2(rim_cols, (("tile", 1),), HALO)
        middle = interior[:, HALO : HALO + core]
        middle = middle.at[:, :HALO].add(received[:, :HALO])
        middle = middle.at[:, core - HALO :].add(received[:, 3 * HALO :])
        gradient = middle.reshape(tiles_dev, core, core)
        step_gradient = exchange(gradient, partner_table, mirror_flags, step_index)
        mask_tiles = mask_tiles - step_rate * step_gradient
    return (mask_tiles, step_gradient)


def solution(mesh):
    return jax.shard_map(
        per_device,
        mesh=mesh,
        in_specs=(
            P("tile", None, None),
            P("tile", None, None),
            P(None, "depth", None, None, None),
            P("depth", None),
            P("depth"),
            P("tile"),
            P("tile"),
        ),
        out_specs=(P("tile", None, None), P("tile", None, None)),
        check_vma=False,
    )
```

```python
import functools

import jax
import jax.numpy as jnp
import numpy as np
from jax import lax
from jax.experimental import pallas as pl
from jax.experimental.pallas import tpu as pltpu
from jax.sharding import PartitionSpec as P

MESH = pl.DeviceIdType.MESH

HALO = 12
FRAME = 152
KSIZE = 25
STEPS = 2


steepness = 3.0
step_rate = 0.05


def extended_2(cells, sides, width):
    for axis, dim in sides:
        count = lax.axis_size(axis)
        ends = count - 1
        head = lax.slice_in_dim(cells, 0, width, axis=dim)
        tail = lax.slice_in_dim(cells, cells.shape[dim] - width, cells.shape[dim], axis=dim)
        cells = jnp.concatenate(
            [
                lax.ppermute(tail, axis, [(i, (i + 1) % count) for i in range(ends)]),
                cells,
                lax.ppermute(head, axis, [((i + 1) % count, i) for i in range(ends)]),
            ],
            axis=dim,
        )
    return cells


def mult_left(matrix, values):
    return jnp.einsum("jk,...kl->...jl", matrix, values, precision=lax.Precision.HIGH)


def mult_right(values, matrix):
    return jnp.einsum("...jk,kl->...jl", values, matrix, precision=lax.Precision.HIGH)


def left_apply(cos_table, sin_table, sign, real_in, imag_in):
    if imag_in is None:
        return (mult_left(cos_table, real_in), sign * mult_left(sin_table, real_in))
    real_out = mult_left(cos_table, real_in) - sign * mult_left(sin_table, imag_in)
    imag_out = mult_left(cos_table, imag_in) + sign * mult_left(sin_table, real_in)
    return (real_out, imag_out)


def right_apply(real_in, imag_in, cos_table, sin_table, sign):
    real_out = mult_right(real_in, cos_table) - sign * mult_right(imag_in, sin_table)
    imag_out = mult_right(imag_in, cos_table) + sign * mult_right(real_in, sin_table)
    return (real_out, imag_out)


def angle_tables(rows_idx, cols_idx, points):
    product = rows_idx[:, None] * cols_idx[None, :] % points
    theta = product.astype(jnp.float32) * (2.0 * np.pi / points)
    return (jnp.cos(theta), jnp.sin(theta))


def split_bf16(values):
    high = lax.reduce_precision(values, exponent_bits=8, mantissa_bits=7)
    return high.astype(jnp.bfloat16), (values - high).astype(jnp.bfloat16)


def split_inside(values):
    spread = values * 65537.0
    high = spread - (spread - values)
    return high.astype(jnp.bfloat16), (values - high).astype(jnp.bfloat16)


def dot3(a_high, a_low, b_high, b_low):
    def product(a, b):
        return jnp.dot(a, b, preferred_element_type=jnp.float32)

    return product(a_high, b_high) + (product(a_high, b_low) + product(a_low, b_high))


def frame_kernel(
    points,
    frame_ref,
    target_ref,
    sre_ref,
    sim_ref,
    w_ref,
    lvl_ref,
    lt_ref,
    rt_ref,
    out_ref,
    fre_s,
    fim_s,
    spec_s,
    slope_s,
    acc_s,
):
    rows_n, cols_n = frame_ref.shape[1:]
    kern = sre_ref.shape[0]
    core = points - 2 * HALO
    scale = 1.0 / (points * points)
    picks = {1.0: (0, 2, 3), -1.0: (0, 4, 5)}

    def lmul(index, values):
        high, low = split_inside(values)
        return dot3(lt_ref[index, 0], lt_ref[index, 1], high, low)

    def rmul(values, index):
        high, low = split_inside(values)
        return dot3(high, low, rt_ref[index, 0], rt_ref[index, 1])

    def left(real_in, imag_in, sign):
        plain, plus, minus = picks[sign]
        both = lmul(plain, real_in + imag_in)
        return both - lmul(plus, imag_in), both + lmul(minus, real_in)

    def right(real_in, imag_in, sign):
        plain, plus, minus = picks[sign]
        both = rmul(real_in + imag_in, plain)
        return both - rmul(imag_in, plus), both + rmul(real_in, minus)

    frame = frame_ref[0]
    freq_re, freq_im = right(lmul(0, frame), -lmul(1, frame), -1.0)
    spec_s[0] = freq_re
    spec_s[1] = freq_im

    def forward(k, intensity):
        s_re = sre_ref[k]
        s_im = sim_ref[k]
        f_re = spec_s[0]
        f_im = spec_s[1]
        prod_re = s_re * f_re - s_im * f_im
        prod_im = s_re * f_im + s_im * f_re
        b_re, b_im = left(prod_re, prod_im, 1.0)
        g_re, g_im = right(b_re, b_im, 1.0)
        g_re = g_re * scale
        g_im = g_im * scale
        fre_s[k] = g_re
        fim_s[k] = g_im
        return intensity + w_ref[k] * (g_re * g_re + g_im * g_im)

    intensity = lax.fori_loop(0, kern, forward, jnp.zeros((rows_n, cols_n), jnp.float32))
    rows = lax.broadcasted_iota(jnp.int32, (rows_n, cols_n), 0)
    cols = lax.broadcasted_iota(jnp.int32, (rows_n, cols_n), 1)
    inside = (rows >= HALO) & (rows < HALO + core) & (cols >= HALO) & (cols < HALO + core)
    resist = 1.0 / (1.0 + jnp.exp(-(steepness * (intensity - lvl_ref[0]))))
    slope = 2.0 * (resist - target_ref[0]) * steepness * resist * (1.0 - resist)
    slope_s[...] = jnp.where(inside, slope, 0.0)
    acc_s[...] = jnp.zeros_like(acc_s)

    def backward(k, carry):
        factor = 2.0 * w_ref[k] * slope_s[...]
        b_re, b_im = left(factor * fre_s[k], factor * fim_s[k], -1.0)
        h_re, h_im = right(b_re, b_im, -1.0)
        s_re = sre_ref[k]
        s_im = sim_ref[k]
        acc_s[0] += s_re * h_re + s_im * h_im
        acc_s[1] += s_re * h_im - s_im * h_re
        return carry

    lax.fori_loop(0, kern, backward, 0)
    u_re, u_im = left(acc_s[0], acc_s[1], 1.0)
    out_ref[0] = (rmul(u_re, 0) - rmul(u_im, 1)) * scale


def table_stack(cos_t, sin_t, rows_n, cols_n):
    combos = [cos_t, sin_t, cos_t + sin_t, sin_t - cos_t, cos_t - sin_t, -sin_t - cos_t]
    pieces = []
    for table in combos:
        table = jnp.pad(table, ((0, rows_n - table.shape[0]), (0, cols_n - table.shape[1])))
        pieces.append(jnp.stack(split_bf16(table)))
    return jnp.stack(pieces)


def frame_gradients(frames, targets, spec_re, spec_im, weights, levels, tables, points):
    count, rows_n, cols_n = frames.shape
    kern = spec_re.shape[0]
    left_tables, right_tables = tables
    per_frame = pl.BlockSpec((1, rows_n, cols_n), lambda i: (i, 0, 0))
    whole_spec = pl.BlockSpec((kern, rows_n, cols_n), lambda i: (0, 0, 0))
    smem = pl.BlockSpec(memory_space=pltpu.SMEM)
    flops = count * (kern * 4 + 4) * 9 * 2 * rows_n * cols_n * cols_n
    return pl.pallas_call(
        functools.partial(frame_kernel, points),
        out_shape=jax.ShapeDtypeStruct(frames.shape, jnp.float32),
        grid=(count,),
        in_specs=[
            per_frame,
            per_frame,
            whole_spec,
            whole_spec,
            smem,
            smem,
            pl.BlockSpec(left_tables.shape, lambda i: (0, 0, 0, 0)),
            pl.BlockSpec(right_tables.shape, lambda i: (0, 0, 0, 0)),
        ],
        out_specs=per_frame,
        scratch_shapes=[
            pltpu.VMEM((kern, rows_n, cols_n), jnp.float32),
            pltpu.VMEM((kern, rows_n, cols_n), jnp.float32),
            pltpu.VMEM((2, rows_n, cols_n), jnp.float32),
            pltpu.VMEM((rows_n, cols_n), jnp.float32),
            pltpu.VMEM((2, rows_n, cols_n), jnp.float32),
        ],
        compiler_params=pltpu.CompilerParams(
            dimension_semantics=("arbitrary",), vmem_limit_bytes=48 * 1024 * 1024
        ),
        cost_estimate=pl.CostEstimate(
            flops=flops, transcendentals=count * rows_n * cols_n, bytes_accessed=8 * 1024 * 1024
        ),
    )(frames, targets, spec_re, spec_im, weights, levels, left_tables, right_tables)


def flip_bit(value, shift):
    bit = (value // shift) % 2
    return value + shift * (1 - 2 * bit)


def exchange_kernel(
    n_tile,
    n_depth,
    x_ref,
    partner_ref,
    mirror_ref,
    out_ref,
    recv_a,
    part_s,
    recv_b,
    blend_s,
    recv_c,
    send_a,
    rsem_a,
    send_b,
    rsem_b,
    send_c,
    rsem_c,
):
    me_t = lax.axis_index("tile")
    me_d = lax.axis_index("depth")
    tiles_dev, core, width = x_ref.shape
    rows = core // n_depth
    shifts = []
    shift = 1
    while shift < n_tile:
        shifts.append(shift)
        shift *= 2
    barrier = pltpu.get_barrier_semaphore()
    for step in range(1, n_depth):
        pl.semaphore_signal(
            barrier, inc=1, device_id=(me_t, (me_d + step) % n_depth), device_id_type=MESH
        )
    for shift in shifts:
        pl.semaphore_signal(
            barrier, inc=1, device_id=(flip_bit(me_t, shift), me_d), device_id_type=MESH
        )
    pl.semaphore_wait(barrier, n_depth - 1 + len(shifts))

    def band(index):
        return pl.ds(pl.multiple_of(index * rows, rows), rows)

    def depth_round(source_of, dst_buf, send_sem, recv_sem):
        copies = []
        for step in range(1, n_depth):
            target = (me_d + step) % n_depth
            copy = pltpu.make_async_remote_copy(
                src_ref=source_of(target),
                dst_ref=dst_buf.at[me_d],
                send_sem=send_sem.at[step],
                recv_sem=recv_sem.at[me_d],
                device_id=(me_t, target),
                device_id_type=MESH,
            )
            copy.start()
            copies.append(copy)
        for step in range(1, n_depth):
            source = (me_d + n_depth - step) % n_depth
            pltpu.make_async_remote_copy(
                src_ref=source_of(source),
                dst_ref=dst_buf.at[source],
                send_sem=send_sem.at[step],
                recv_sem=recv_sem.at[source],
                device_id=(me_t, source),
                device_id_type=MESH,
            ).wait_recv()
        for copy in copies:
            copy.wait_send()

    recv_a[me_d] = x_ref[:, band(me_d), :]
    depth_round(lambda target: x_ref.at[:, band(target), :], recv_a, send_a, rsem_a)
    total = recv_a[0]
    for slot in range(1, n_depth):
        total = total + recv_a[slot]
    part_s[...] = total

    swaps = []
    for slot, shift in enumerate(shifts):
        copy = pltpu.make_async_remote_copy(
            src_ref=part_s,
            dst_ref=recv_b.at[slot],
            send_sem=send_b.at[slot],
            recv_sem=rsem_b.at[slot],
            device_id=(flip_bit(me_t, shift), me_d),
            device_id_type=MESH,
        )
        copy.start()
        swaps.append(copy)
    for copy in swaps:
        copy.wait_recv()
    for copy in swaps:
        copy.wait_send()

    lane_a = lax.broadcasted_iota(jnp.int32, (width, width), 0)
    lane_b = lax.broadcasted_iota(jnp.int32, (width, width), 1)
    reverse = jnp.where(lane_a + lane_b == width - 1, 1.0, 0.0).astype(jnp.float32)
    for local in range(tiles_dev):
        partner = partner_ref[local]
        chosen = jnp.zeros((rows, width), jnp.float32)
        for other in range(tiles_dev):
            hit = jnp.where(partner == me_t * tiles_dev + other, 1.0, 0.0)
            chosen = chosen + hit * part_s[other]
        for slot, shift in enumerate(shifts):
            source = flip_bit(me_t, shift)
            for other in range(tiles_dev):
                hit = jnp.where(partner == source * tiles_dev + other, 1.0, 0.0)
                chosen = chosen + hit * recv_b[slot, other]
        mirrored = jnp.dot(
            chosen, reverse, precision=lax.Precision.HIGHEST, preferred_element_type=jnp.float32
        )
        use_mirror = jnp.where(mirror_ref[local] == 1, 1.0, 0.0)
        chosen = use_mirror * mirrored + (1.0 - use_mirror) * chosen
        blend_s[local] = 0.5 * (part_s[local] + chosen)

    recv_c[me_d] = blend_s[...]
    depth_round(lambda target: blend_s, recv_c, send_c, rsem_c)
    for slot in range(n_depth):
        out_ref[:, slot * rows : (slot + 1) * rows, :] = recv_c[slot]


def exchange(values, partner_local, mirror_local, call_id):
    n_tile = lax.axis_size("tile")
    n_depth = lax.axis_size("depth")
    n_shift = max(n_tile - 1, 1).bit_length()
    tiles_dev, core, width = values.shape
    piece = (tiles_dev, core // n_depth, width)
    vmem = pl.BlockSpec(memory_space=pltpu.VMEM)
    smem = pl.BlockSpec(memory_space=pltpu.SMEM)
    return pl.pallas_call(
        functools.partial(exchange_kernel, n_tile, n_depth),
        out_shape=jax.ShapeDtypeStruct(values.shape, jnp.float32),
        in_specs=[vmem, smem, smem],
        out_specs=vmem,
        scratch_shapes=[
            pltpu.VMEM((n_depth,) + piece, jnp.float32),
            pltpu.VMEM(piece, jnp.float32),
            pltpu.VMEM((n_shift,) + piece, jnp.float32),
            pltpu.VMEM(piece, jnp.float32),
            pltpu.VMEM((n_depth,) + piece, jnp.float32),
            pltpu.SemaphoreType.DMA((n_depth,)),
            pltpu.SemaphoreType.DMA((n_depth,)),
            pltpu.SemaphoreType.DMA((n_shift,)),
            pltpu.SemaphoreType.DMA((n_shift,)),
            pltpu.SemaphoreType.DMA((n_depth,)),
            pltpu.SemaphoreType.DMA((n_depth,)),
        ],
        compiler_params=pltpu.CompilerParams(collective_id=call_id, has_side_effects=True),
    )(values, partner_local, mirror_local)


def per_device(
    mask_tiles, target_tiles, kernels, socs_weights, thresholds, partner_table, mirror_flags
):
    tiles_dev, core, unused_width = mask_tiles.shape
    points = FRAME
    index_full = jnp.arange(points, dtype=jnp.int32)
    cos_table, sin_table = angle_tables(index_full, index_full, points)
    offsets = jnp.arange(KSIZE, dtype=jnp.int32) - HALO
    cos_small, sin_small = angle_tables(index_full, offsets, points)
    spec_re, spec_im = left_apply(cos_small, sin_small, -1.0, kernels[0], kernels[1])
    spec_re, spec_im = right_apply(spec_re, spec_im, cos_small.T, sin_small.T, -1.0)
    target_f = target_tiles.astype(jnp.float32)
    rows_n = -(-points // 16) * 16
    cols_n = -(-points // 128) * 128
    row_fill = rows_n - points
    col_fill = cols_n - points
    targets = jnp.pad(
        target_f, ((0, 0), (HALO, rows_n - HALO - core), (HALO, cols_n - HALO - core))
    )
    spec_re_p = jnp.pad(spec_re[0], ((0, 0), (0, row_fill), (0, col_fill)))
    spec_im_p = jnp.pad(spec_im[0], ((0, 0), (0, row_fill), (0, col_fill)))
    tables = (
        table_stack(cos_table, sin_table, rows_n, rows_n),
        table_stack(cos_table, sin_table, cols_n, cols_n),
    )
    strip_height = tiles_dev * core
    step_gradient = jnp.zeros_like(mask_tiles)
    for step_index in range(STEPS):
        strip_rows = mask_tiles.reshape(strip_height, core)
        extended = extended_2(strip_rows, (("tile", 1),), HALO)
        padded = jnp.pad(extended, ((HALO, HALO), (0, 0)))
        canvas = jnp.zeros((strip_height + 2 * HALO, points), jnp.float32)
        frames = jnp.stack(
            [padded[row_index * core : row_index * core + points] for row_index in range(tiles_dev)]
        )
        frames = jnp.pad(frames, ((0, 0), (0, row_fill), (0, col_fill)))
        grads = frame_gradients(
            frames, targets, spec_re_p, spec_im_p, socs_weights[0], thresholds, tables, points
        )
        for row_index in range(tiles_dev):
            canvas = canvas.at[row_index * core : row_index * core + points].add(
                grads[row_index, :points, :points]
            )
        interior = canvas[HALO : HALO + strip_height]
        rim_cols = jnp.concatenate([interior[:, :HALO], interior[:, HALO + core :]], axis=1)
        received = extended_2(rim_cols, (("tile", 1),), HALO)
        middle = interior[:, HALO : HALO + core]
        middle = middle.at[:, :HALO].add(received[:, :HALO])
        middle = middle.at[:, core - HALO :].add(received[:, 3 * HALO :])
        gradient = middle.reshape(tiles_dev, core, core)
        step_gradient = exchange(gradient, partner_table, mirror_flags, step_index)
        mask_tiles = mask_tiles - step_rate * step_gradient
    return (mask_tiles, step_gradient)


def solution(mesh):
    return jax.shard_map(
        per_device,
        mesh=mesh,
        in_specs=(
            P("tile", None, None),
            P("tile", None, None),
            P(None, "depth", None, None, None),
            P("depth", None),
            P("depth"),
            P("tile"),
            P("tile"),
        ),
        out_specs=(P("tile", None, None), P("tile", None, None)),
        check_vma=False,
    )
```

```python
import functools

import jax
import jax.numpy as jnp
import numpy as np
from jax import lax
from jax.experimental import pallas as pl
from jax.experimental.pallas import tpu as pltpu
from jax.sharding import PartitionSpec as P

MESH = pl.DeviceIdType.MESH

HALO = 12
FRAME = 152
KSIZE = 25
STEPS = 2


steepness = 3.0
step_rate = 0.05


def extended_2(cells, sides, width):
    for axis, dim in sides:
        count = lax.axis_size(axis)
        ends = count - 1
        head = lax.slice_in_dim(cells, 0, width, axis=dim)
        tail = lax.slice_in_dim(cells, cells.shape[dim] - width, cells.shape[dim], axis=dim)
        cells = jnp.concatenate(
            [
                lax.ppermute(tail, axis, [(i, (i + 1) % count) for i in range(ends)]),
                cells,
                lax.ppermute(head, axis, [((i + 1) % count, i) for i in range(ends)]),
            ],
            axis=dim,
        )
    return cells


def mult_left(matrix, values):
    return jnp.einsum("jk,...kl->...jl", matrix, values, precision=lax.Precision.HIGH)


def mult_right(values, matrix):
    return jnp.einsum("...jk,kl->...jl", values, matrix, precision=lax.Precision.HIGH)


def left_apply(cos_table, sin_table, sign, real_in, imag_in):
    if imag_in is None:
        return (mult_left(cos_table, real_in), sign * mult_left(sin_table, real_in))
    real_out = mult_left(cos_table, real_in) - sign * mult_left(sin_table, imag_in)
    imag_out = mult_left(cos_table, imag_in) + sign * mult_left(sin_table, real_in)
    return (real_out, imag_out)


def right_apply(real_in, imag_in, cos_table, sin_table, sign):
    real_out = mult_right(real_in, cos_table) - sign * mult_right(imag_in, sin_table)
    imag_out = mult_right(imag_in, cos_table) + sign * mult_right(real_in, sin_table)
    return (real_out, imag_out)


def angle_tables(rows_idx, cols_idx, points):
    product = rows_idx[:, None] * cols_idx[None, :] % points
    theta = product.astype(jnp.float32) * (2.0 * np.pi / points)
    return (jnp.cos(theta), jnp.sin(theta))


def split_bf16(values):
    high = lax.reduce_precision(values, exponent_bits=8, mantissa_bits=7)
    return high.astype(jnp.bfloat16), (values - high).astype(jnp.bfloat16)


def split_inside(values):
    spread = values * 65537.0
    high = spread - (spread - values)
    return high.astype(jnp.bfloat16), (values - high).astype(jnp.bfloat16)


def dot3(a_high, a_low, b_high, b_low):
    def product(a, b):
        return jnp.dot(a, b, preferred_element_type=jnp.float32)

    return product(a_high, b_high) + (product(a_high, b_low) + product(a_low, b_high))


def frame_kernel(
    points,
    frame_ref,
    target_ref,
    sre_ref,
    sim_ref,
    w_ref,
    lvl_ref,
    lt_ref,
    rt_ref,
    out_ref,
    fre_s,
    fim_s,
    spec_s,
    slope_s,
    acc_s,
):
    rows_n, cols_n = frame_ref.shape[1:]
    kern = sre_ref.shape[0]
    core = points - 2 * HALO
    scale = 1.0 / (points * points)
    picks = {1.0: (0, 2, 3), -1.0: (0, 4, 5), 0.0: (6, 7, 8)}

    def lmul(index, values):
        high, low = split_inside(values)
        return dot3(lt_ref[index, 0], lt_ref[index, 1], high, low)

    def rmul(values, index):
        high, low = split_inside(values)
        return dot3(high, low, rt_ref[index, 0], rt_ref[index, 1])

    def left(real_in, imag_in, sign):
        plain, plus, minus = picks[sign]
        both = lmul(plain, real_in + imag_in)
        return both - lmul(plus, imag_in), both + lmul(minus, real_in)

    def right(real_in, imag_in, sign):
        plain, plus, minus = picks[sign]
        both = rmul(real_in + imag_in, plain)
        return both - rmul(imag_in, plus), both + rmul(real_in, minus)

    frame = frame_ref[0]
    freq_re, freq_im = right(lmul(0, frame), -lmul(1, frame), -1.0)
    spec_s[0] = freq_re
    spec_s[1] = freq_im

    def forward(k, intensity):
        s_re = sre_ref[k]
        s_im = sim_ref[k]
        f_re = spec_s[0]
        f_im = spec_s[1]
        prod_re = s_re * f_re - s_im * f_im
        prod_im = s_re * f_im + s_im * f_re
        b_re, b_im = left(prod_re, prod_im, 1.0)
        g_re, g_im = right(b_re, b_im, 1.0)
        g_re = g_re * scale
        g_im = g_im * scale
        fre_s[k] = g_re
        fim_s[k] = g_im
        return intensity + w_ref[k] * (g_re * g_re + g_im * g_im)

    intensity = lax.fori_loop(0, kern, forward, jnp.zeros((rows_n, cols_n), jnp.float32))
    rows = lax.broadcasted_iota(jnp.int32, (rows_n, cols_n), 0)
    cols = lax.broadcasted_iota(jnp.int32, (rows_n, cols_n), 1)
    inside = (rows >= HALO) & (rows < HALO + core) & (cols >= HALO) & (cols < HALO + core)
    resist = 1.0 / (1.0 + jnp.exp(-(steepness * (intensity - lvl_ref[0]))))
    slope = 2.0 * (resist - target_ref[0]) * steepness * resist * (1.0 - resist)
    slope_s[...] = jnp.where(inside, slope, 0.0)
    acc_s[...] = jnp.zeros_like(acc_s)

    def backward(k, carry):
        factor = 2.0 * w_ref[k] * slope_s[...]
        b_re, b_im = left(factor * fre_s[k], factor * fim_s[k], -1.0)
        h_re, h_im = right(b_re, b_im, -1.0)
        s_re = sre_ref[k]
        s_im = sim_ref[k]
        acc_s[0] += s_re * h_re + s_im * h_im
        acc_s[1] += s_re * h_im - s_im * h_re
        return carry

    lax.fori_loop(0, kern, backward, 0)
    u_re, u_im = left(acc_s[0], acc_s[1], 0.0)
    out_ref[0] = (rmul(u_re, 6) - rmul(u_im, 7)) * scale


def shifted_order(length, points):
    order = np.full(length, -1)
    order[: points - HALO] = np.arange(HALO, points)
    order[length - HALO :] = np.arange(HALO)
    return order


def table_stack(cos_t, sin_t, rows_n, cols_n, points, on_rows):
    combos = [cos_t, sin_t, cos_t + sin_t, sin_t - cos_t, cos_t - sin_t, -sin_t - cos_t]
    padded = [
        jnp.pad(table, ((0, rows_n - table.shape[0]), (0, cols_n - table.shape[1])))
        for table in combos
    ]
    if on_rows:
        order = shifted_order(rows_n, points)
        keep = jnp.asarray(order >= 0)[:, None]
        finals = [padded[0], padded[2], padded[3]]
        finals = [jnp.where(keep, table[np.maximum(order, 0)], 0.0) for table in finals]
    else:
        order = shifted_order(cols_n, points)
        keep = jnp.asarray(order >= 0)[None, :]
        finals = [padded[0], padded[1], padded[1]]
        finals = [jnp.where(keep, table[:, np.maximum(order, 0)], 0.0) for table in finals]
    return jnp.stack([jnp.stack(split_bf16(table)) for table in padded + finals])


def frame_gradients(frames, targets, spec_re, spec_im, weights, levels, tables, points):
    count, rows_n, cols_n = frames.shape
    kern = spec_re.shape[0]
    left_tables, right_tables = tables
    per_frame = pl.BlockSpec((1, rows_n, cols_n), lambda i: (i, 0, 0))
    whole_spec = pl.BlockSpec((kern, rows_n, cols_n), lambda i: (0, 0, 0))
    smem = pl.BlockSpec(memory_space=pltpu.SMEM)
    flops = count * (kern * 4 + 4) * 9 * 2 * rows_n * cols_n * cols_n
    return pl.pallas_call(
        functools.partial(frame_kernel, points),
        out_shape=jax.ShapeDtypeStruct(frames.shape, jnp.float32),
        grid=(count,),
        in_specs=[
            per_frame,
            per_frame,
            whole_spec,
            whole_spec,
            smem,
            smem,
            pl.BlockSpec(left_tables.shape, lambda i: (0, 0, 0, 0)),
            pl.BlockSpec(right_tables.shape, lambda i: (0, 0, 0, 0)),
        ],
        out_specs=per_frame,
        scratch_shapes=[
            pltpu.VMEM((kern, rows_n, cols_n), jnp.float32),
            pltpu.VMEM((kern, rows_n, cols_n), jnp.float32),
            pltpu.VMEM((2, rows_n, cols_n), jnp.float32),
            pltpu.VMEM((rows_n, cols_n), jnp.float32),
            pltpu.VMEM((2, rows_n, cols_n), jnp.float32),
        ],
        compiler_params=pltpu.CompilerParams(
            dimension_semantics=("arbitrary",), vmem_limit_bytes=48 * 1024 * 1024
        ),
        cost_estimate=pl.CostEstimate(
            flops=flops, transcendentals=count * rows_n * cols_n, bytes_accessed=8 * 1024 * 1024
        ),
    )(frames, targets, spec_re, spec_im, weights, levels, left_tables, right_tables)


def flip_bit(value, shift):
    bit = (value // shift) % 2
    return value + shift * (1 - 2 * bit)


def exchange_kernel(
    n_tile,
    n_depth,
    x_ref,
    partner_ref,
    mirror_ref,
    out_ref,
    recv_a,
    full_s,
    recv_r,
    part_s,
    recv_b,
    blend_s,
    recv_c,
    send_a,
    rsem_a,
    send_r,
    rsem_r,
    send_b,
    rsem_b,
    send_c,
    rsem_c,
):
    me_t = lax.axis_index("tile")
    me_d = lax.axis_index("depth")
    tiles_dev, core, wide = x_ref.shape
    width = out_ref.shape[-1]
    rows = core // n_depth
    left_t = (me_t + n_tile - 1) % n_tile
    right_t = (me_t + 1) % n_tile
    shifts = []
    shift = 1
    while shift < n_tile:
        shifts.append(shift)
        shift *= 2
    barrier = pltpu.get_barrier_semaphore()
    for step in range(1, n_depth):
        pl.semaphore_signal(
            barrier, inc=1, device_id=(me_t, (me_d + step) % n_depth), device_id_type=MESH
        )
    for shift in shifts:
        pl.semaphore_signal(
            barrier, inc=1, device_id=(flip_bit(me_t, shift), me_d), device_id_type=MESH
        )
    for neighbour in (left_t, right_t):
        pl.semaphore_signal(barrier, inc=1, device_id=(neighbour, me_d), device_id_type=MESH)
    pl.semaphore_wait(barrier, n_depth + 1 + len(shifts))

    def band(index):
        return pl.ds(pl.multiple_of(index * rows, rows), rows)

    def depth_round(source_of, dst_buf, send_sem, recv_sem):
        copies = []
        for step in range(1, n_depth):
            target = (me_d + step) % n_depth
            copy = pltpu.make_async_remote_copy(
                src_ref=source_of(target),
                dst_ref=dst_buf.at[me_d],
                send_sem=send_sem.at[step],
                recv_sem=recv_sem.at[me_d],
                device_id=(me_t, target),
                device_id_type=MESH,
            )
            copy.start()
            copies.append(copy)
        for step in range(1, n_depth):
            source = (me_d + n_depth - step) % n_depth
            pltpu.make_async_remote_copy(
                src_ref=source_of(source),
                dst_ref=dst_buf.at[source],
                send_sem=send_sem.at[step],
                recv_sem=recv_sem.at[source],
                device_id=(me_t, source),
                device_id_type=MESH,
            ).wait_recv()
        for copy in copies:
            copy.wait_send()

    recv_a[me_d] = x_ref[:, band(me_d), :]
    depth_round(lambda target: x_ref.at[:, band(target), :], recv_a, send_a, rsem_a)
    total = recv_a[0]
    for slot in range(1, n_depth):
        total = total + recv_a[slot]
    full_s[...] = total

    rims = []
    for slot, neighbour in enumerate((left_t, right_t)):
        copy = pltpu.make_async_remote_copy(
            src_ref=full_s.at[:, :, pl.ds(width, wide - width)],
            dst_ref=recv_r.at[slot],
            send_sem=send_r.at[slot],
            recv_sem=rsem_r.at[slot],
            device_id=(neighbour, me_d),
            device_id_type=MESH,
        )
        copy.start()
        rims.append(copy)
    for copy in rims:
        copy.wait_recv()
    for copy in rims:
        copy.wait_send()
    lanes = lax.broadcasted_iota(jnp.int32, (tiles_dev, rows, width), 2)
    has_left = jnp.where(me_t > 0, 1.0, 0.0)
    has_right = jnp.where(me_t < n_tile - 1, 1.0, 0.0)
    from_left = jnp.where(lanes < HALO, recv_r[1], 0.0) * has_left
    from_right = jnp.where(lanes >= width - HALO, recv_r[0], 0.0) * has_right
    part_s[...] = full_s[:, :, :width] + (from_left + from_right)

    swaps = []
    for slot, shift in enumerate(shifts):
        copy = pltpu.make_async_remote_copy(
            src_ref=part_s,
            dst_ref=recv_b.at[slot],
            send_sem=send_b.at[slot],
            recv_sem=rsem_b.at[slot],
            device_id=(flip_bit(me_t, shift), me_d),
            device_id_type=MESH,
        )
        copy.start()
        swaps.append(copy)
    for copy in swaps:
        copy.wait_recv()
    for copy in swaps:
        copy.wait_send()

    lane_a = lax.broadcasted_iota(jnp.int32, (width, width), 0)
    lane_b = lax.broadcasted_iota(jnp.int32, (width, width), 1)
    reverse = jnp.where(lane_a + lane_b == width - 1, 1.0, 0.0).astype(jnp.float32)
    for local in range(tiles_dev):
        partner = partner_ref[local]
        chosen = jnp.zeros((rows, width), jnp.float32)
        for other in range(tiles_dev):
            hit = jnp.where(partner == me_t * tiles_dev + other, 1.0, 0.0)
            chosen = chosen + hit * part_s[other]
        for slot, shift in enumerate(shifts):
            source = flip_bit(me_t, shift)
            for other in range(tiles_dev):
                hit = jnp.where(partner == source * tiles_dev + other, 1.0, 0.0)
                chosen = chosen + hit * recv_b[slot, other]
        mirrored = jnp.dot(
            chosen, reverse, precision=lax.Precision.HIGHEST, preferred_element_type=jnp.float32
        )
        use_mirror = jnp.where(mirror_ref[local] == 1, 1.0, 0.0)
        chosen = use_mirror * mirrored + (1.0 - use_mirror) * chosen
        blend_s[local] = 0.5 * (part_s[local] + chosen)

    recv_c[me_d] = blend_s[...]
    depth_round(lambda target: blend_s, recv_c, send_c, rsem_c)
    for slot in range(n_depth):
        out_ref[:, slot * rows : (slot + 1) * rows, :] = recv_c[slot]


def exchange(values, partner_local, mirror_local, call_id):
    n_tile = lax.axis_size("tile")
    n_depth = lax.axis_size("depth")
    n_shift = max(n_tile - 1, 1).bit_length()
    tiles_dev, core, wide = values.shape
    width = core
    piece = (tiles_dev, core // n_depth, width)
    band = (tiles_dev, core // n_depth, wide)
    vmem = pl.BlockSpec(memory_space=pltpu.VMEM)
    smem = pl.BlockSpec(memory_space=pltpu.SMEM)
    return pl.pallas_call(
        functools.partial(exchange_kernel, n_tile, n_depth),
        out_shape=jax.ShapeDtypeStruct((tiles_dev, core, width), jnp.float32),
        in_specs=[vmem, smem, smem],
        out_specs=vmem,
        scratch_shapes=[
            pltpu.VMEM((n_depth,) + band, jnp.float32),
            pltpu.VMEM(band, jnp.float32),
            pltpu.VMEM((2,) + piece, jnp.float32),
            pltpu.VMEM(piece, jnp.float32),
            pltpu.VMEM((n_shift,) + piece, jnp.float32),
            pltpu.VMEM(piece, jnp.float32),
            pltpu.VMEM((n_depth,) + piece, jnp.float32),
            pltpu.SemaphoreType.DMA((n_depth,)),
            pltpu.SemaphoreType.DMA((n_depth,)),
            pltpu.SemaphoreType.DMA((2,)),
            pltpu.SemaphoreType.DMA((2,)),
            pltpu.SemaphoreType.DMA((n_shift,)),
            pltpu.SemaphoreType.DMA((n_shift,)),
            pltpu.SemaphoreType.DMA((n_depth,)),
            pltpu.SemaphoreType.DMA((n_depth,)),
        ],
        compiler_params=pltpu.CompilerParams(collective_id=call_id, has_side_effects=True),
    )(values, partner_local, mirror_local)


def per_device(
    mask_tiles, target_tiles, kernels, socs_weights, thresholds, partner_table, mirror_flags
):
    tiles_dev, core, unused_width = mask_tiles.shape
    points = FRAME
    index_full = jnp.arange(points, dtype=jnp.int32)
    cos_table, sin_table = angle_tables(index_full, index_full, points)
    offsets = jnp.arange(KSIZE, dtype=jnp.int32) - HALO
    cos_small, sin_small = angle_tables(index_full, offsets, points)
    spec_re, spec_im = left_apply(cos_small, sin_small, -1.0, kernels[0], kernels[1])
    spec_re, spec_im = right_apply(spec_re, spec_im, cos_small.T, sin_small.T, -1.0)
    target_f = target_tiles.astype(jnp.float32)
    rows_n = -(-points // 16) * 16
    cols_n = -(-points // 128) * 128
    row_fill = rows_n - points
    col_fill = cols_n - points
    targets = jnp.pad(
        target_f, ((0, 0), (HALO, rows_n - HALO - core), (HALO, cols_n - HALO - core))
    )
    spec_re_p = jnp.pad(spec_re[0], ((0, 0), (0, row_fill), (0, col_fill)))
    spec_im_p = jnp.pad(spec_im[0], ((0, 0), (0, row_fill), (0, col_fill)))
    tables = (
        table_stack(cos_table, sin_table, rows_n, rows_n, points, True),
        table_stack(cos_table, sin_table, cols_n, cols_n, points, False),
    )
    strip_height = tiles_dev * core
    step_gradient = jnp.zeros_like(mask_tiles)
    for step_index in range(STEPS):
        strip_rows = mask_tiles.reshape(strip_height, core)
        extended = extended_2(strip_rows, (("tile", 1),), HALO)
        padded = jnp.pad(extended, ((HALO, HALO), (0, 0)))
        frames = jnp.stack(
            [padded[row_index * core : row_index * core + points] for row_index in range(tiles_dev)]
        )
        frames = jnp.pad(frames, ((0, 0), (0, row_fill), (0, col_fill)))
        grads = frame_gradients(
            frames, targets, spec_re_p, spec_im_p, socs_weights[0], thresholds, tables, points
        )
        gradient = grads[:, :core, :]
        for row_index in range(tiles_dev):
            if row_index + 1 < tiles_dev:
                gradient = gradient.at[row_index, core - HALO :].add(
                    grads[row_index + 1, rows_n - HALO :]
                )
            if row_index > 0:
                gradient = gradient.at[row_index, :HALO].add(
                    grads[row_index - 1, core : core + HALO]
                )
        step_gradient = exchange(gradient, partner_table, mirror_flags, step_index)
        mask_tiles = mask_tiles - step_rate * step_gradient
    return (mask_tiles, step_gradient)


def solution(mesh):
    return jax.shard_map(
        per_device,
        mesh=mesh,
        in_specs=(
            P("tile", None, None),
            P("tile", None, None),
            P(None, "depth", None, None, None),
            P("depth", None),
            P("depth"),
            P("tile"),
            P("tile"),
        ),
        out_specs=(P("tile", None, None), P("tile", None, None)),
        check_vma=False,
    )
```

```python
import functools

import jax
import jax.numpy as jnp
import ml_dtypes
import numpy as np
from jax import lax
from jax.experimental import pallas as pl
from jax.experimental.pallas import tpu as pltpu
from jax.sharding import PartitionSpec as P

MESH = pl.DeviceIdType.MESH

HALO = 12
FRAME = 152
KSIZE = 25
STEPS = 2


steepness = 3.0
step_rate = 0.05


def extended_2(cells, sides, width):
    for axis, dim in sides:
        count = lax.axis_size(axis)
        ends = count - 1
        head = lax.slice_in_dim(cells, 0, width, axis=dim)
        tail = lax.slice_in_dim(cells, cells.shape[dim] - width, cells.shape[dim], axis=dim)
        cells = jnp.concatenate(
            [
                lax.ppermute(tail, axis, [(i, (i + 1) % count) for i in range(ends)]),
                cells,
                lax.ppermute(head, axis, [((i + 1) % count, i) for i in range(ends)]),
            ],
            axis=dim,
        )
    return cells


def mult_left(matrix, values):
    return jnp.einsum("jk,...kl->...jl", matrix, values, precision=lax.Precision.HIGH)


def mult_right(values, matrix):
    return jnp.einsum("...jk,kl->...jl", values, matrix, precision=lax.Precision.HIGH)


def left_apply(cos_table, sin_table, sign, real_in, imag_in):
    if imag_in is None:
        return (mult_left(cos_table, real_in), sign * mult_left(sin_table, real_in))
    real_out = mult_left(cos_table, real_in) - sign * mult_left(sin_table, imag_in)
    imag_out = mult_left(cos_table, imag_in) + sign * mult_left(sin_table, real_in)
    return (real_out, imag_out)


def right_apply(real_in, imag_in, cos_table, sin_table, sign):
    real_out = mult_right(real_in, cos_table) - sign * mult_right(imag_in, sin_table)
    imag_out = mult_right(imag_in, cos_table) + sign * mult_right(real_in, sin_table)
    return (real_out, imag_out)


def angle_tables(rows_idx, cols_idx, points):
    product = rows_idx[:, None] * cols_idx[None, :] % points
    theta = product.astype(jnp.float32) * (2.0 * np.pi / points)
    return (jnp.cos(theta), jnp.sin(theta))


def split_bf16(values):
    high = lax.reduce_precision(values, exponent_bits=8, mantissa_bits=7)
    return high.astype(jnp.bfloat16), (values - high).astype(jnp.bfloat16)


def split_inside(values):
    spread = values * 65537.0
    high = spread - (spread - values)
    return high.astype(jnp.bfloat16), (values - high).astype(jnp.bfloat16)


def dot3(a_high, a_low, b_high, b_low):
    def product(a, b):
        return jnp.dot(a, b, preferred_element_type=jnp.float32)

    return product(a_high, b_high) + (product(a_high, b_low) + product(a_low, b_high))


def frame_kernel(
    points,
    frame_ref,
    target_ref,
    sre_ref,
    sim_ref,
    w_ref,
    lvl_ref,
    lt_ref,
    rt_ref,
    out_ref,
    fre_s,
    fim_s,
    spec_s,
    slope_s,
    acc_s,
):
    rows_n, cols_n = frame_ref.shape[1:]
    kern = sre_ref.shape[0]
    core = points - 2 * HALO
    scale = 1.0 / (points * points)
    picks = {1.0: (0, 2, 3), -1.0: (0, 4, 5), 0.0: (6, 7, 8)}

    def lmul(index, values):
        high, low = split_inside(values)
        return dot3(lt_ref[index, 0], lt_ref[index, 1], high, low)

    def rmul(values, index):
        high, low = split_inside(values)
        return dot3(high, low, rt_ref[index, 0], rt_ref[index, 1])

    def left(real_in, imag_in, sign):
        plain, plus, minus = picks[sign]
        both = lmul(plain, real_in + imag_in)
        return both - lmul(plus, imag_in), both + lmul(minus, real_in)

    def right(real_in, imag_in, sign):
        plain, plus, minus = picks[sign]
        both = rmul(real_in + imag_in, plain)
        return both - rmul(imag_in, plus), both + rmul(real_in, minus)

    frame = frame_ref[0]
    freq_re, freq_im = right(lmul(0, frame), -lmul(1, frame), -1.0)
    spec_s[0] = freq_re
    spec_s[1] = freq_im

    def forward(k, intensity):
        s_re = sre_ref[k]
        s_im = sim_ref[k]
        f_re = spec_s[0]
        f_im = spec_s[1]
        prod_re = s_re * f_re - s_im * f_im
        prod_im = s_re * f_im + s_im * f_re
        b_re, b_im = left(prod_re, prod_im, 1.0)
        g_re, g_im = right(b_re, b_im, 1.0)
        g_re = g_re * scale
        g_im = g_im * scale
        fre_s[k] = g_re
        fim_s[k] = g_im
        return intensity + w_ref[k] * (g_re * g_re + g_im * g_im)

    intensity = lax.fori_loop(0, kern, forward, jnp.zeros((rows_n, cols_n), jnp.float32))
    rows = lax.broadcasted_iota(jnp.int32, (rows_n, cols_n), 0)
    cols = lax.broadcasted_iota(jnp.int32, (rows_n, cols_n), 1)
    inside = (rows >= HALO) & (rows < HALO + core) & (cols >= HALO) & (cols < HALO + core)
    resist = 1.0 / (1.0 + jnp.exp(-(steepness * (intensity - lvl_ref[0]))))
    slope = 2.0 * (resist - target_ref[0]) * steepness * resist * (1.0 - resist)
    slope_s[...] = jnp.where(inside, slope, 0.0)
    acc_s[...] = jnp.zeros_like(acc_s)

    def backward(k, carry):
        factor = 2.0 * w_ref[k] * slope_s[...]
        b_re, b_im = left(factor * fre_s[k], factor * fim_s[k], -1.0)
        h_re, h_im = right(b_re, b_im, -1.0)
        s_re = sre_ref[k]
        s_im = sim_ref[k]
        acc_s[0] += s_re * h_re + s_im * h_im
        acc_s[1] += s_re * h_im - s_im * h_re
        return carry

    lax.fori_loop(0, kern, backward, 0)
    u_re, u_im = left(acc_s[0], acc_s[1], 0.0)
    out_ref[0] = (rmul(u_re, 6) - rmul(u_im, 7)) * scale


def shifted_order(length, points):
    order = np.full(length, -1)
    order[: points - HALO] = np.arange(HALO, points)
    order[length - HALO :] = np.arange(HALO)
    return order


def table_stack(points, rows_n, cols_n, on_rows):
    index = np.arange(points)
    theta = (np.outer(index, index) % points) * (2.0 * np.pi / points)
    cos_t, sin_t = np.cos(theta), np.sin(theta)
    combos = [cos_t, sin_t, cos_t + sin_t, sin_t - cos_t, cos_t - sin_t, -sin_t - cos_t]
    padded = [np.pad(table, ((0, rows_n - points), (0, cols_n - points))) for table in combos]
    if on_rows:
        order = shifted_order(rows_n, points)
        finals = [padded[0], padded[2], padded[3]]
        finals = [np.where((order >= 0)[:, None], table[np.maximum(order, 0)], 0.0) for table in finals]
    else:
        order = shifted_order(cols_n, points)
        finals = [padded[0], padded[1]]
        finals = [
            np.where((order >= 0)[None, :], table[:, np.maximum(order, 0)], 0.0) for table in finals
        ]
    stack = np.stack(padded + finals).astype(np.float32)
    high = stack.astype(ml_dtypes.bfloat16)
    low = (stack - high.astype(np.float32)).astype(ml_dtypes.bfloat16)
    return jnp.asarray(np.stack([high, low], axis=1))


def frame_gradients(frames, targets, spec_re, spec_im, weights, levels, tables, points):
    count, rows_n, cols_n = frames.shape
    kern = spec_re.shape[0]
    left_tables, right_tables = tables
    per_frame = pl.BlockSpec((1, rows_n, cols_n), lambda i: (i, 0, 0))
    whole_spec = pl.BlockSpec((kern, rows_n, cols_n), lambda i: (0, 0, 0))
    smem = pl.BlockSpec(memory_space=pltpu.SMEM)
    flops = count * (kern * 4 + 4) * 9 * 2 * rows_n * cols_n * cols_n
    return pl.pallas_call(
        functools.partial(frame_kernel, points),
        out_shape=jax.ShapeDtypeStruct(frames.shape, jnp.float32),
        grid=(count,),
        in_specs=[
            per_frame,
            per_frame,
            whole_spec,
            whole_spec,
            smem,
            smem,
            pl.BlockSpec(left_tables.shape, lambda i: (0, 0, 0, 0)),
            pl.BlockSpec(right_tables.shape, lambda i: (0, 0, 0, 0)),
        ],
        out_specs=per_frame,
        scratch_shapes=[
            pltpu.VMEM((kern, rows_n, cols_n), jnp.float32),
            pltpu.VMEM((kern, rows_n, cols_n), jnp.float32),
            pltpu.VMEM((2, rows_n, cols_n), jnp.float32),
            pltpu.VMEM((rows_n, cols_n), jnp.float32),
            pltpu.VMEM((2, rows_n, cols_n), jnp.float32),
        ],
        compiler_params=pltpu.CompilerParams(
            dimension_semantics=("arbitrary",), vmem_limit_bytes=48 * 1024 * 1024
        ),
        cost_estimate=pl.CostEstimate(
            flops=flops, transcendentals=count * rows_n * cols_n, bytes_accessed=8 * 1024 * 1024
        ),
    )(frames, targets, spec_re, spec_im, weights, levels, left_tables, right_tables)


def flip_bit(value, shift):
    bit = (value // shift) % 2
    return value + shift * (1 - 2 * bit)


def exchange_kernel(
    n_tile,
    n_depth,
    x_ref,
    partner_ref,
    mirror_ref,
    out_ref,
    recv_a,
    full_s,
    recv_r,
    part_s,
    recv_b,
    blend_s,
    recv_c,
    send_a,
    rsem_a,
    send_r,
    rsem_r,
    send_b,
    rsem_b,
    send_c,
    rsem_c,
):
    me_t = lax.axis_index("tile")
    me_d = lax.axis_index("depth")
    tiles_dev, core, wide = x_ref.shape
    width = out_ref.shape[-1]
    rows = core // n_depth
    left_t = (me_t + n_tile - 1) % n_tile
    right_t = (me_t + 1) % n_tile
    shifts = []
    shift = 1
    while shift < n_tile:
        shifts.append(shift)
        shift *= 2
    barrier = pltpu.get_barrier_semaphore()
    for step in range(1, n_depth):
        pl.semaphore_signal(
            barrier, inc=1, device_id=(me_t, (me_d + step) % n_depth), device_id_type=MESH
        )
    for shift in shifts:
        pl.semaphore_signal(
            barrier, inc=1, device_id=(flip_bit(me_t, shift), me_d), device_id_type=MESH
        )
    for neighbour in (left_t, right_t):
        pl.semaphore_signal(barrier, inc=1, device_id=(neighbour, me_d), device_id_type=MESH)
    pl.semaphore_wait(barrier, n_depth + 1 + len(shifts))

    def band(index):
        return pl.ds(pl.multiple_of(index * rows, rows), rows)

    def depth_round(source_of, dst_buf, send_sem, recv_sem):
        copies = []
        for step in range(1, n_depth):
            target = (me_d + step) % n_depth
            copy = pltpu.make_async_remote_copy(
                src_ref=source_of(target),
                dst_ref=dst_buf.at[me_d],
                send_sem=send_sem.at[step],
                recv_sem=recv_sem.at[me_d],
                device_id=(me_t, target),
                device_id_type=MESH,
            )
            copy.start()
            copies.append(copy)
        for step in range(1, n_depth):
            source = (me_d + n_depth - step) % n_depth
            pltpu.make_async_remote_copy(
                src_ref=source_of(source),
                dst_ref=dst_buf.at[source],
                send_sem=send_sem.at[step],
                recv_sem=recv_sem.at[source],
                device_id=(me_t, source),
                device_id_type=MESH,
            ).wait_recv()
        for copy in copies:
            copy.wait_send()

    recv_a[me_d] = x_ref[:, band(me_d), :]
    depth_round(lambda target: x_ref.at[:, band(target), :], recv_a, send_a, rsem_a)
    total = recv_a[0]
    for slot in range(1, n_depth):
        total = total + recv_a[slot]
    full_s[...] = total

    rims = []
    for slot, neighbour in enumerate((left_t, right_t)):
        copy = pltpu.make_async_remote_copy(
            src_ref=full_s.at[:, :, pl.ds(width, wide - width)],
            dst_ref=recv_r.at[slot],
            send_sem=send_r.at[slot],
            recv_sem=rsem_r.at[slot],
            device_id=(neighbour, me_d),
            device_id_type=MESH,
        )
        copy.start()
        rims.append(copy)
    for copy in rims:
        copy.wait_recv()
    for copy in rims:
        copy.wait_send()
    lanes = lax.broadcasted_iota(jnp.int32, (tiles_dev, rows, width), 2)
    has_left = jnp.where(me_t > 0, 1.0, 0.0)
    has_right = jnp.where(me_t < n_tile - 1, 1.0, 0.0)
    from_left = jnp.where(lanes < HALO, recv_r[1], 0.0) * has_left
    from_right = jnp.where(lanes >= width - HALO, recv_r[0], 0.0) * has_right
    part_s[...] = full_s[:, :, :width] + (from_left + from_right)

    swaps = []
    for slot, shift in enumerate(shifts):
        copy = pltpu.make_async_remote_copy(
            src_ref=part_s,
            dst_ref=recv_b.at[slot],
            send_sem=send_b.at[slot],
            recv_sem=rsem_b.at[slot],
            device_id=(flip_bit(me_t, shift), me_d),
            device_id_type=MESH,
        )
        copy.start()
        swaps.append(copy)
    for copy in swaps:
        copy.wait_recv()
    for copy in swaps:
        copy.wait_send()

    lane_a = lax.broadcasted_iota(jnp.int32, (width, width), 0)
    lane_b = lax.broadcasted_iota(jnp.int32, (width, width), 1)
    reverse = jnp.where(lane_a + lane_b == width - 1, 1.0, 0.0).astype(jnp.float32)
    for local in range(tiles_dev):
        partner = partner_ref[local]
        chosen = jnp.zeros((rows, width), jnp.float32)
        for other in range(tiles_dev):
            hit = jnp.where(partner == me_t * tiles_dev + other, 1.0, 0.0)
            chosen = chosen + hit * part_s[other]
        for slot, shift in enumerate(shifts):
            source = flip_bit(me_t, shift)
            for other in range(tiles_dev):
                hit = jnp.where(partner == source * tiles_dev + other, 1.0, 0.0)
                chosen = chosen + hit * recv_b[slot, other]
        mirrored = jnp.dot(
            chosen, reverse, precision=lax.Precision.HIGHEST, preferred_element_type=jnp.float32
        )
        use_mirror = jnp.where(mirror_ref[local] == 1, 1.0, 0.0)
        chosen = use_mirror * mirrored + (1.0 - use_mirror) * chosen
        blend_s[local] = 0.5 * (part_s[local] + chosen)

    recv_c[me_d] = blend_s[...]
    depth_round(lambda target: blend_s, recv_c, send_c, rsem_c)
    for slot in range(n_depth):
        out_ref[:, slot * rows : (slot + 1) * rows, :] = recv_c[slot]


def exchange(values, partner_local, mirror_local, call_id):
    n_tile = lax.axis_size("tile")
    n_depth = lax.axis_size("depth")
    n_shift = max(n_tile - 1, 1).bit_length()
    tiles_dev, core, wide = values.shape
    width = core
    piece = (tiles_dev, core // n_depth, width)
    band = (tiles_dev, core // n_depth, wide)
    vmem = pl.BlockSpec(memory_space=pltpu.VMEM)
    smem = pl.BlockSpec(memory_space=pltpu.SMEM)
    return pl.pallas_call(
        functools.partial(exchange_kernel, n_tile, n_depth),
        out_shape=jax.ShapeDtypeStruct((tiles_dev, core, width), jnp.float32),
        in_specs=[vmem, smem, smem],
        out_specs=vmem,
        scratch_shapes=[
            pltpu.VMEM((n_depth,) + band, jnp.float32),
            pltpu.VMEM(band, jnp.float32),
            pltpu.VMEM((2,) + piece, jnp.float32),
            pltpu.VMEM(piece, jnp.float32),
            pltpu.VMEM((n_shift,) + piece, jnp.float32),
            pltpu.VMEM(piece, jnp.float32),
            pltpu.VMEM((n_depth,) + piece, jnp.float32),
            pltpu.SemaphoreType.DMA((n_depth,)),
            pltpu.SemaphoreType.DMA((n_depth,)),
            pltpu.SemaphoreType.DMA((2,)),
            pltpu.SemaphoreType.DMA((2,)),
            pltpu.SemaphoreType.DMA((n_shift,)),
            pltpu.SemaphoreType.DMA((n_shift,)),
            pltpu.SemaphoreType.DMA((n_depth,)),
            pltpu.SemaphoreType.DMA((n_depth,)),
        ],
        compiler_params=pltpu.CompilerParams(collective_id=call_id, has_side_effects=True),
    )(values, partner_local, mirror_local)


def per_device(
    mask_tiles, target_tiles, kernels, socs_weights, thresholds, partner_table, mirror_flags
):
    tiles_dev, core, unused_width = mask_tiles.shape
    points = FRAME
    index_full = jnp.arange(points, dtype=jnp.int32)
    cos_table, sin_table = angle_tables(index_full, index_full, points)
    offsets = jnp.arange(KSIZE, dtype=jnp.int32) - HALO
    cos_small, sin_small = angle_tables(index_full, offsets, points)
    spec_re, spec_im = left_apply(cos_small, sin_small, -1.0, kernels[0], kernels[1])
    spec_re, spec_im = right_apply(spec_re, spec_im, cos_small.T, sin_small.T, -1.0)
    target_f = target_tiles.astype(jnp.float32)
    rows_n = -(-points // 16) * 16
    cols_n = -(-points // 128) * 128
    row_fill = rows_n - points
    col_fill = cols_n - points
    targets = jnp.pad(
        target_f, ((0, 0), (HALO, rows_n - HALO - core), (HALO, cols_n - HALO - core))
    )
    spec_re_p = jnp.pad(spec_re[0], ((0, 0), (0, row_fill), (0, col_fill)))
    spec_im_p = jnp.pad(spec_im[0], ((0, 0), (0, row_fill), (0, col_fill)))
    tables = (
        table_stack(points, rows_n, rows_n, True),
        table_stack(points, cols_n, cols_n, False),
    )
    strip_height = tiles_dev * core
    step_gradient = jnp.zeros_like(mask_tiles)
    for step_index in range(STEPS):
        strip_rows = mask_tiles.reshape(strip_height, core)
        extended = extended_2(strip_rows, (("tile", 1),), HALO)
        padded = jnp.pad(extended, ((HALO, HALO), (0, 0)))
        frames = jnp.stack(
            [padded[row_index * core : row_index * core + points] for row_index in range(tiles_dev)]
        )
        frames = jnp.pad(frames, ((0, 0), (0, row_fill), (0, col_fill)))
        grads = frame_gradients(
            frames, targets, spec_re_p, spec_im_p, socs_weights[0], thresholds, tables, points
        )
        gradient = grads[:, :core, :]
        for row_index in range(tiles_dev):
            if row_index + 1 < tiles_dev:
                gradient = gradient.at[row_index, core - HALO :].add(
                    grads[row_index + 1, rows_n - HALO :]
                )
            if row_index > 0:
                gradient = gradient.at[row_index, :HALO].add(
                    grads[row_index - 1, core : core + HALO]
                )
        step_gradient = exchange(gradient, partner_table, mirror_flags, step_index)
        mask_tiles = mask_tiles - step_rate * step_gradient
    return (mask_tiles, step_gradient)


def solution(mesh):
    return jax.shard_map(
        per_device,
        mesh=mesh,
        in_specs=(
            P("tile", None, None),
            P("tile", None, None),
            P(None, "depth", None, None, None),
            P("depth", None),
            P("depth"),
            P("tile"),
            P("tile"),
        ),
        out_specs=(P("tile", None, None), P("tile", None, None)),
        check_vma=False,
    )
```

```python
import functools

import jax
import jax.numpy as jnp
import ml_dtypes
import numpy as np
from jax import lax
from jax.experimental import pallas as pl
from jax.experimental.pallas import tpu as pltpu
from jax.sharding import PartitionSpec as P

MESH = pl.DeviceIdType.MESH

HALO = 12
FRAME = 152
KSIZE = 25
STEPS = 2


steepness = 3.0
step_rate = 0.05


def extended_2(cells, sides, width):
    for axis, dim in sides:
        count = lax.axis_size(axis)
        ends = count - 1
        head = lax.slice_in_dim(cells, 0, width, axis=dim)
        tail = lax.slice_in_dim(cells, cells.shape[dim] - width, cells.shape[dim], axis=dim)
        cells = jnp.concatenate(
            [
                lax.ppermute(tail, axis, [(i, (i + 1) % count) for i in range(ends)]),
                cells,
                lax.ppermute(head, axis, [((i + 1) % count, i) for i in range(ends)]),
            ],
            axis=dim,
        )
    return cells


def mult_left(matrix, values):
    return jnp.einsum("jk,...kl->...jl", matrix, values, precision=lax.Precision.HIGH)


def mult_right(values, matrix):
    return jnp.einsum("...jk,kl->...jl", values, matrix, precision=lax.Precision.HIGH)


def left_apply(cos_table, sin_table, sign, real_in, imag_in):
    if imag_in is None:
        return (mult_left(cos_table, real_in), sign * mult_left(sin_table, real_in))
    real_out = mult_left(cos_table, real_in) - sign * mult_left(sin_table, imag_in)
    imag_out = mult_left(cos_table, imag_in) + sign * mult_left(sin_table, real_in)
    return (real_out, imag_out)


def right_apply(real_in, imag_in, cos_table, sin_table, sign):
    real_out = mult_right(real_in, cos_table) - sign * mult_right(imag_in, sin_table)
    imag_out = mult_right(imag_in, cos_table) + sign * mult_right(real_in, sin_table)
    return (real_out, imag_out)


def angle_tables(rows_idx, cols_idx, points):
    product = rows_idx[:, None] * cols_idx[None, :] % points
    theta = product.astype(jnp.float32) * (2.0 * np.pi / points)
    return (jnp.cos(theta), jnp.sin(theta))


def split_bf16(values):
    high = lax.reduce_precision(values, exponent_bits=8, mantissa_bits=7)
    return high.astype(jnp.bfloat16), (values - high).astype(jnp.bfloat16)


def split_inside(values):
    spread = values * 65537.0
    high = spread - (spread - values)
    return high.astype(jnp.bfloat16), (values - high).astype(jnp.bfloat16)


def dot3(a_high, a_low, b_high, b_low):
    def product(a, b):
        return jnp.dot(a, b, preferred_element_type=jnp.float32)

    return product(a_high, b_high) + (product(a_high, b_low) + product(a_low, b_high))


def frame_kernel(
    points,
    frame_ref,
    target_ref,
    sre_ref,
    sim_ref,
    w_ref,
    lvl_ref,
    lt_ref,
    rt_ref,
    out_ref,
    fre_s,
    fim_s,
    spec_s,
    slope_s,
    acc_s,
):
    rows_n, cols_n = frame_ref.shape[1:]
    kern = sre_ref.shape[0]
    core = points - 2 * HALO
    scale = 1.0 / (points * points)
    picks = {1.0: (0, 2, 3), -1.0: (0, 4, 5), 0.0: (6, 7, 8)}

    def lmul(index, values):
        high, low = split_inside(values)
        return dot3(lt_ref[index, 0], lt_ref[index, 1], high, low)

    def rmul(values, index):
        high, low = split_inside(values)
        return dot3(high, low, rt_ref[index, 0], rt_ref[index, 1])

    def left(real_in, imag_in, sign):
        plain, plus, minus = picks[sign]
        both = lmul(plain, real_in + imag_in)
        return both - lmul(plus, imag_in), both + lmul(minus, real_in)

    def right(real_in, imag_in, sign):
        plain, plus, minus = picks[sign]
        both = rmul(real_in + imag_in, plain)
        return both - rmul(imag_in, plus), both + rmul(real_in, minus)

    frame = frame_ref[0]
    freq_re, freq_im = right(lmul(0, frame), -lmul(1, frame), -1.0)
    spec_s[0] = freq_re
    spec_s[1] = freq_im

    def forward(k, intensity):
        s_re = sre_ref[k]
        s_im = sim_ref[k]
        f_re = spec_s[0]
        f_im = spec_s[1]
        prod_re = s_re * f_re - s_im * f_im
        prod_im = s_re * f_im + s_im * f_re
        b_re, b_im = left(prod_re, prod_im, 1.0)
        g_re, g_im = right(b_re, b_im, 1.0)
        g_re = g_re * scale
        g_im = g_im * scale
        fre_s[k] = g_re
        fim_s[k] = g_im
        return intensity + w_ref[k] * (g_re * g_re + g_im * g_im)

    intensity = lax.fori_loop(0, kern, forward, jnp.zeros((rows_n, cols_n), jnp.float32))
    rows = lax.broadcasted_iota(jnp.int32, (rows_n, cols_n), 0)
    cols = lax.broadcasted_iota(jnp.int32, (rows_n, cols_n), 1)
    inside = (rows >= HALO) & (rows < HALO + core) & (cols >= HALO) & (cols < HALO + core)
    resist = 1.0 / (1.0 + jnp.exp(-(steepness * (intensity - lvl_ref[0]))))
    slope = 2.0 * (resist - target_ref[0]) * steepness * resist * (1.0 - resist)
    slope_s[...] = jnp.where(inside, slope, 0.0)
    acc_s[...] = jnp.zeros_like(acc_s)

    def backward(k, carry):
        factor = 2.0 * w_ref[k] * slope_s[...]
        b_re, b_im = left(factor * fre_s[k], factor * fim_s[k], -1.0)
        h_re, h_im = right(b_re, b_im, -1.0)
        s_re = sre_ref[k]
        s_im = sim_ref[k]
        acc_s[0] += s_re * h_re + s_im * h_im
        acc_s[1] += s_re * h_im - s_im * h_re
        return carry

    lax.fori_loop(0, kern, backward, 0)
    u_re, u_im = left(acc_s[0], acc_s[1], 0.0)
    out_ref[0] = (rmul(u_re, 6) - rmul(u_im, 7)) * scale


def shifted_order(length, points):
    order = np.full(length, -1)
    order[: points - HALO] = np.arange(HALO, points)
    order[length - HALO :] = np.arange(HALO)
    return order


def table_stack(points, rows_n, cols_n, on_rows):
    index = np.arange(points)
    theta = (np.outer(index, index) % points) * (2.0 * np.pi / points)
    cos_t, sin_t = np.cos(theta), np.sin(theta)
    combos = [cos_t, sin_t, cos_t + sin_t, sin_t - cos_t, cos_t - sin_t, -sin_t - cos_t]
    padded = [np.pad(table, ((0, rows_n - points), (0, cols_n - points))) for table in combos]
    if on_rows:
        order = shifted_order(rows_n, points)
        finals = [padded[0], padded[2], padded[3]]
        finals = [np.where((order >= 0)[:, None], table[np.maximum(order, 0)], 0.0) for table in finals]
    else:
        order = shifted_order(cols_n, points)
        finals = [padded[0], padded[1]]
        finals = [
            np.where((order >= 0)[None, :], table[:, np.maximum(order, 0)], 0.0) for table in finals
        ]
    stack = np.stack(padded + finals).astype(np.float32)
    high = stack.astype(ml_dtypes.bfloat16)
    low = (stack - high.astype(np.float32)).astype(ml_dtypes.bfloat16)
    return jnp.asarray(np.stack([high, low], axis=1))


def frame_gradients(frames, targets, spec_re, spec_im, weights, levels, tables, points):
    count, rows_n, cols_n = frames.shape
    kern = spec_re.shape[0]
    left_tables, right_tables = tables
    per_frame = pl.BlockSpec((1, rows_n, cols_n), lambda i: (i, 0, 0))
    whole_spec = pl.BlockSpec((kern, rows_n, cols_n), lambda i: (0, 0, 0))
    smem = pl.BlockSpec(memory_space=pltpu.SMEM)
    flops = count * (kern * 4 + 4) * 9 * 2 * rows_n * cols_n * cols_n
    return pl.pallas_call(
        functools.partial(frame_kernel, points),
        out_shape=jax.ShapeDtypeStruct(frames.shape, jnp.float32),
        grid=(count,),
        in_specs=[
            per_frame,
            per_frame,
            whole_spec,
            whole_spec,
            smem,
            smem,
            pl.BlockSpec(left_tables.shape, lambda i: (0, 0, 0, 0)),
            pl.BlockSpec(right_tables.shape, lambda i: (0, 0, 0, 0)),
        ],
        out_specs=per_frame,
        scratch_shapes=[
            pltpu.VMEM((kern, rows_n, cols_n), jnp.float32),
            pltpu.VMEM((kern, rows_n, cols_n), jnp.float32),
            pltpu.VMEM((2, rows_n, cols_n), jnp.float32),
            pltpu.VMEM((rows_n, cols_n), jnp.float32),
            pltpu.VMEM((2, rows_n, cols_n), jnp.float32),
        ],
        compiler_params=pltpu.CompilerParams(
            dimension_semantics=("arbitrary",), vmem_limit_bytes=48 * 1024 * 1024
        ),
        cost_estimate=pl.CostEstimate(
            flops=flops, transcendentals=count * rows_n * cols_n, bytes_accessed=8 * 1024 * 1024
        ),
    )(frames, targets, spec_re, spec_im, weights, levels, left_tables, right_tables)


def flip_bit(value, shift):
    bit = (value // shift) % 2
    return value + shift * (1 - 2 * bit)


def exchange_kernel(
    n_tile,
    n_depth,
    x_ref,
    partner_ref,
    mirror_ref,
    out_ref,
    recv_a,
    recv_r,
    part_s,
    recv_b,
    blend_s,
    recv_c,
    send_a,
    rsem_a,
    send_r,
    rsem_r,
    send_b,
    rsem_b,
    send_c,
    rsem_c,
):
    me_t = lax.axis_index("tile")
    me_d = lax.axis_index("depth")
    tiles_dev, core, wide = x_ref.shape
    width = out_ref.shape[-1]
    rows = core // n_depth
    left_t = (me_t + n_tile - 1) % n_tile
    right_t = (me_t + 1) % n_tile
    shifts = []
    shift = 1
    while shift < n_tile:
        shifts.append(shift)
        shift *= 2
    barrier = pltpu.get_barrier_semaphore()
    for step in range(1, n_depth):
        pl.semaphore_signal(
            barrier, inc=1, device_id=(me_t, (me_d + step) % n_depth), device_id_type=MESH
        )
    for shift in shifts:
        pl.semaphore_signal(
            barrier, inc=1, device_id=(flip_bit(me_t, shift), me_d), device_id_type=MESH
        )
    for neighbour in (left_t, right_t):
        for depth in range(n_depth):
            pl.semaphore_signal(barrier, inc=1, device_id=(neighbour, depth), device_id_type=MESH)
    pl.semaphore_wait(barrier, 3 * n_depth - 1 + len(shifts))

    def band(index):
        return pl.ds(pl.multiple_of(index * rows, rows), rows)

    def depth_round(source_of, dst_buf, send_sem, recv_sem):
        copies = []
        for step in range(1, n_depth):
            target = (me_d + step) % n_depth
            copy = pltpu.make_async_remote_copy(
                src_ref=source_of(target),
                dst_ref=dst_buf.at[me_d],
                send_sem=send_sem.at[step],
                recv_sem=recv_sem.at[me_d],
                device_id=(me_t, target),
                device_id_type=MESH,
            )
            copy.start()
            copies.append(copy)
        for step in range(1, n_depth):
            source = (me_d + n_depth - step) % n_depth
            pltpu.make_async_remote_copy(
                src_ref=source_of(source),
                dst_ref=dst_buf.at[source],
                send_sem=send_sem.at[step],
                recv_sem=recv_sem.at[source],
                device_id=(me_t, source),
                device_id_type=MESH,
            ).wait_recv()
        for copy in copies:
            copy.wait_send()

    rims = []
    for side, neighbour in enumerate((left_t, right_t)):
        for depth in range(n_depth):
            copy = pltpu.make_async_remote_copy(
                src_ref=x_ref.at[:, pl.ds(depth * rows, rows), pl.ds(width, wide - width)],
                dst_ref=recv_r.at[side, me_d],
                send_sem=send_r.at[side, depth],
                recv_sem=rsem_r.at[side, me_d],
                device_id=(neighbour, depth),
                device_id_type=MESH,
            )
            copy.start()
            rims.append(copy)
    recv_a[me_d] = x_ref[:, band(me_d), :width]
    depth_round(lambda target: x_ref.at[:, band(target), pl.ds(0, width)], recv_a, send_a, rsem_a)
    for side, neighbour in enumerate((left_t, right_t)):
        for depth in range(n_depth):
            pltpu.make_async_remote_copy(
                src_ref=x_ref.at[:, pl.ds(depth * rows, rows), pl.ds(width, wide - width)],
                dst_ref=recv_r.at[side, depth],
                send_sem=send_r.at[side, depth],
                recv_sem=rsem_r.at[side, depth],
                device_id=(neighbour, depth),
                device_id_type=MESH,
            ).wait_recv()
    for copy in rims:
        copy.wait_send()
    total = recv_a[0]
    from_right = recv_r[0, 0]
    from_left = recv_r[1, 0]
    for slot in range(1, n_depth):
        total = total + recv_a[slot]
        from_right = from_right + recv_r[0, slot]
        from_left = from_left + recv_r[1, slot]
    lanes = lax.broadcasted_iota(jnp.int32, (tiles_dev, rows, width), 2)
    has_left = jnp.where(me_t > 0, 1.0, 0.0)
    has_right = jnp.where(me_t < n_tile - 1, 1.0, 0.0)
    from_left = jnp.where(lanes < HALO, from_left, 0.0) * has_left
    from_right = jnp.where(lanes >= width - HALO, from_right, 0.0) * has_right
    part_s[...] = total + (from_left + from_right)

    swaps = []
    for slot, shift in enumerate(shifts):
        copy = pltpu.make_async_remote_copy(
            src_ref=part_s,
            dst_ref=recv_b.at[slot],
            send_sem=send_b.at[slot],
            recv_sem=rsem_b.at[slot],
            device_id=(flip_bit(me_t, shift), me_d),
            device_id_type=MESH,
        )
        copy.start()
        swaps.append(copy)
    for copy in swaps:
        copy.wait_recv()
    for copy in swaps:
        copy.wait_send()

    lane_a = lax.broadcasted_iota(jnp.int32, (width, width), 0)
    lane_b = lax.broadcasted_iota(jnp.int32, (width, width), 1)
    reverse = jnp.where(lane_a + lane_b == width - 1, 1.0, 0.0).astype(jnp.float32)
    for local in range(tiles_dev):
        partner = partner_ref[local]
        chosen = jnp.zeros((rows, width), jnp.float32)
        for other in range(tiles_dev):
            hit = jnp.where(partner == me_t * tiles_dev + other, 1.0, 0.0)
            chosen = chosen + hit * part_s[other]
        for slot, shift in enumerate(shifts):
            source = flip_bit(me_t, shift)
            for other in range(tiles_dev):
                hit = jnp.where(partner == source * tiles_dev + other, 1.0, 0.0)
                chosen = chosen + hit * recv_b[slot, other]
        mirrored = jnp.dot(
            chosen, reverse, precision=lax.Precision.HIGHEST, preferred_element_type=jnp.float32
        )
        use_mirror = jnp.where(mirror_ref[local] == 1, 1.0, 0.0)
        chosen = use_mirror * mirrored + (1.0 - use_mirror) * chosen
        blend_s[local] = 0.5 * (part_s[local] + chosen)

    recv_c[me_d] = blend_s[...]
    depth_round(lambda target: blend_s, recv_c, send_c, rsem_c)
    for slot in range(n_depth):
        out_ref[:, slot * rows : (slot + 1) * rows, :] = recv_c[slot]


def exchange(values, partner_local, mirror_local, call_id):
    n_tile = lax.axis_size("tile")
    n_depth = lax.axis_size("depth")
    n_shift = max(n_tile - 1, 1).bit_length()
    tiles_dev, core, wide = values.shape
    width = core
    piece = (tiles_dev, core // n_depth, width)
    vmem = pl.BlockSpec(memory_space=pltpu.VMEM)
    smem = pl.BlockSpec(memory_space=pltpu.SMEM)
    return pl.pallas_call(
        functools.partial(exchange_kernel, n_tile, n_depth),
        out_shape=jax.ShapeDtypeStruct((tiles_dev, core, width), jnp.float32),
        in_specs=[vmem, smem, smem],
        out_specs=vmem,
        scratch_shapes=[
            pltpu.VMEM((n_depth,) + piece, jnp.float32),
            pltpu.VMEM((2, n_depth) + piece, jnp.float32),
            pltpu.VMEM(piece, jnp.float32),
            pltpu.VMEM((n_shift,) + piece, jnp.float32),
            pltpu.VMEM(piece, jnp.float32),
            pltpu.VMEM((n_depth,) + piece, jnp.float32),
            pltpu.SemaphoreType.DMA((n_depth,)),
            pltpu.SemaphoreType.DMA((n_depth,)),
            pltpu.SemaphoreType.DMA((2, n_depth)),
            pltpu.SemaphoreType.DMA((2, n_depth)),
            pltpu.SemaphoreType.DMA((n_shift,)),
            pltpu.SemaphoreType.DMA((n_shift,)),
            pltpu.SemaphoreType.DMA((n_depth,)),
            pltpu.SemaphoreType.DMA((n_depth,)),
        ],
        compiler_params=pltpu.CompilerParams(collective_id=call_id, has_side_effects=True),
    )(values, partner_local, mirror_local)


def per_device(
    mask_tiles, target_tiles, kernels, socs_weights, thresholds, partner_table, mirror_flags
):
    tiles_dev, core, unused_width = mask_tiles.shape
    points = FRAME
    index_full = jnp.arange(points, dtype=jnp.int32)
    cos_table, sin_table = angle_tables(index_full, index_full, points)
    offsets = jnp.arange(KSIZE, dtype=jnp.int32) - HALO
    cos_small, sin_small = angle_tables(index_full, offsets, points)
    spec_re, spec_im = left_apply(cos_small, sin_small, -1.0, kernels[0], kernels[1])
    spec_re, spec_im = right_apply(spec_re, spec_im, cos_small.T, sin_small.T, -1.0)
    target_f = target_tiles.astype(jnp.float32)
    rows_n = -(-points // 16) * 16
    cols_n = -(-points // 128) * 128
    row_fill = rows_n - points
    col_fill = cols_n - points
    targets = jnp.pad(
        target_f, ((0, 0), (HALO, rows_n - HALO - core), (HALO, cols_n - HALO - core))
    )
    spec_re_p = jnp.pad(spec_re[0], ((0, 0), (0, row_fill), (0, col_fill)))
    spec_im_p = jnp.pad(spec_im[0], ((0, 0), (0, row_fill), (0, col_fill)))
    tables = (
        table_stack(points, rows_n, rows_n, True),
        table_stack(points, cols_n, cols_n, False),
    )
    strip_height = tiles_dev * core
    step_gradient = jnp.zeros_like(mask_tiles)
    for step_index in range(STEPS):
        strip_rows = mask_tiles.reshape(strip_height, core)
        extended = extended_2(strip_rows, (("tile", 1),), HALO)
        padded = jnp.pad(extended, ((HALO, HALO), (0, 0)))
        frames = jnp.stack(
            [padded[row_index * core : row_index * core + points] for row_index in range(tiles_dev)]
        )
        frames = jnp.pad(frames, ((0, 0), (0, row_fill), (0, col_fill)))
        grads = frame_gradients(
            frames, targets, spec_re_p, spec_im_p, socs_weights[0], thresholds, tables, points
        )
        gradient = grads[:, :core, :]
        for row_index in range(tiles_dev):
            if row_index + 1 < tiles_dev:
                gradient = gradient.at[row_index, core - HALO :].add(
                    grads[row_index + 1, rows_n - HALO :]
                )
            if row_index > 0:
                gradient = gradient.at[row_index, :HALO].add(
                    grads[row_index - 1, core : core + HALO]
                )
        step_gradient = exchange(gradient, partner_table, mirror_flags, step_index)
        mask_tiles = mask_tiles - step_rate * step_gradient
    return (mask_tiles, step_gradient)


def solution(mesh):
    return jax.shard_map(
        per_device,
        mesh=mesh,
        in_specs=(
            P("tile", None, None),
            P("tile", None, None),
            P(None, "depth", None, None, None),
            P("depth", None),
            P("depth"),
            P("tile"),
            P("tile"),
        ),
        out_specs=(P("tile", None, None), P("tile", None, None)),
        check_vma=False,
    )
```

```python
import functools

import jax
import jax.numpy as jnp
import ml_dtypes
import numpy as np
from jax import lax
from jax.experimental import pallas as pl
from jax.experimental.pallas import tpu as pltpu
from jax.sharding import PartitionSpec as P

MESH = pl.DeviceIdType.MESH

HALO = 12
FRAME = 152
KSIZE = 25
STEPS = 2


steepness = 3.0
step_rate = 0.05


def extended_2(cells, sides, width):
    for axis, dim in sides:
        count = lax.axis_size(axis)
        ends = count - 1
        head = lax.slice_in_dim(cells, 0, width, axis=dim)
        tail = lax.slice_in_dim(cells, cells.shape[dim] - width, cells.shape[dim], axis=dim)
        cells = jnp.concatenate(
            [
                lax.ppermute(tail, axis, [(i, (i + 1) % count) for i in range(ends)]),
                cells,
                lax.ppermute(head, axis, [((i + 1) % count, i) for i in range(ends)]),
            ],
            axis=dim,
        )
    return cells


def mult_left(matrix, values):
    return jnp.einsum("jk,...kl->...jl", matrix, values, precision=lax.Precision.HIGH)


def mult_right(values, matrix):
    return jnp.einsum("...jk,kl->...jl", values, matrix, precision=lax.Precision.HIGH)


def left_apply(cos_table, sin_table, sign, real_in, imag_in):
    if imag_in is None:
        return (mult_left(cos_table, real_in), sign * mult_left(sin_table, real_in))
    real_out = mult_left(cos_table, real_in) - sign * mult_left(sin_table, imag_in)
    imag_out = mult_left(cos_table, imag_in) + sign * mult_left(sin_table, real_in)
    return (real_out, imag_out)


def right_apply(real_in, imag_in, cos_table, sin_table, sign):
    real_out = mult_right(real_in, cos_table) - sign * mult_right(imag_in, sin_table)
    imag_out = mult_right(imag_in, cos_table) + sign * mult_right(real_in, sin_table)
    return (real_out, imag_out)


def angle_tables(rows_idx, cols_idx, points):
    product = rows_idx[:, None] * cols_idx[None, :] % points
    theta = product.astype(jnp.float32) * (2.0 * np.pi / points)
    return (jnp.cos(theta), jnp.sin(theta))


def split_bf16(values):
    high = lax.reduce_precision(values, exponent_bits=8, mantissa_bits=7)
    return high.astype(jnp.bfloat16), (values - high).astype(jnp.bfloat16)


def split_inside(values):
    spread = values * 65537.0
    high = spread - (spread - values)
    return high.astype(jnp.bfloat16), (values - high).astype(jnp.bfloat16)


def dot3(a_high, a_low, b_high, b_low):
    def product(a, b):
        return jnp.dot(a, b, preferred_element_type=jnp.float32)

    return product(a_high, b_high) + (product(a_high, b_low) + product(a_low, b_high))


def frame_kernel(
    points,
    frame_ref,
    target_ref,
    sre_ref,
    sim_ref,
    w_ref,
    lvl_ref,
    lt_ref,
    rt_ref,
    out_ref,
    fre_s,
    fim_s,
    spec_s,
    slope_s,
    acc_s,
):
    rows_n, cols_n = frame_ref.shape[1:]
    kern = sre_ref.shape[0]
    core = points - 2 * HALO
    scale = 1.0 / (points * points)
    picks = {1.0: (0, 2, 3), -1.0: (0, 4, 5), 0.0: (6, 7, 8)}

    def lmul(index, values):
        high, low = split_inside(values)
        return dot3(lt_ref[index, 0], lt_ref[index, 1], high, low)

    def rmul(values, index):
        high, low = split_inside(values)
        return dot3(high, low, rt_ref[index, 0], rt_ref[index, 1])

    def left(real_in, imag_in, sign):
        plain, plus, minus = picks[sign]
        both = lmul(plain, real_in + imag_in)
        return both - lmul(plus, imag_in), both + lmul(minus, real_in)

    def right(real_in, imag_in, sign):
        plain, plus, minus = picks[sign]
        both = rmul(real_in + imag_in, plain)
        return both - rmul(imag_in, plus), both + rmul(real_in, minus)

    frame = frame_ref[0]
    freq_re, freq_im = right(lmul(0, frame), -lmul(1, frame), -1.0)
    spec_s[0] = freq_re
    spec_s[1] = freq_im

    def forward(k, intensity):
        s_re = sre_ref[k]
        s_im = sim_ref[k]
        f_re = spec_s[0]
        f_im = spec_s[1]
        prod_re = s_re * f_re - s_im * f_im
        prod_im = s_re * f_im + s_im * f_re
        b_re, b_im = left(prod_re, prod_im, 1.0)
        g_re, g_im = right(b_re, b_im, 1.0)
        g_re = g_re * scale
        g_im = g_im * scale
        fre_s[k] = g_re
        fim_s[k] = g_im
        return intensity + w_ref[k] * (g_re * g_re + g_im * g_im)

    intensity = lax.fori_loop(0, kern, forward, jnp.zeros((rows_n, cols_n), jnp.float32))
    rows = lax.broadcasted_iota(jnp.int32, (rows_n, cols_n), 0)
    cols = lax.broadcasted_iota(jnp.int32, (rows_n, cols_n), 1)
    inside = (rows >= HALO) & (rows < HALO + core) & (cols >= HALO) & (cols < HALO + core)
    resist = 1.0 / (1.0 + jnp.exp(-(steepness * (intensity - lvl_ref[0]))))
    slope = 2.0 * (resist - target_ref[0]) * steepness * resist * (1.0 - resist)
    slope_s[...] = jnp.where(inside, slope, 0.0)
    acc_s[...] = jnp.zeros_like(acc_s)

    def backward(k, carry):
        factor = 2.0 * w_ref[k] * slope_s[...]
        b_re, b_im = left(factor * fre_s[k], factor * fim_s[k], -1.0)
        h_re, h_im = right(b_re, b_im, -1.0)
        s_re = sre_ref[k]
        s_im = sim_ref[k]
        acc_s[0] += s_re * h_re + s_im * h_im
        acc_s[1] += s_re * h_im - s_im * h_re
        return carry

    lax.fori_loop(0, kern, backward, 0)
    u_re, u_im = left(acc_s[0], acc_s[1], 0.0)
    out_ref[0] = (rmul(u_re, 6) - rmul(u_im, 7)) * scale


def shifted_order(length, points):
    order = np.full(length, -1)
    order[: points - HALO] = np.arange(HALO, points)
    order[length - HALO :] = np.arange(HALO)
    return order


def table_stack(points, rows_n, cols_n, on_rows):
    index = np.arange(points)
    theta = (np.outer(index, index) % points) * (2.0 * np.pi / points)
    cos_t, sin_t = np.cos(theta), np.sin(theta)
    combos = [cos_t, sin_t, cos_t + sin_t, sin_t - cos_t, cos_t - sin_t, -sin_t - cos_t]
    padded = [np.pad(table, ((0, rows_n - points), (0, cols_n - points))) for table in combos]
    if on_rows:
        order = shifted_order(rows_n, points)
        finals = [padded[0], padded[2], padded[3]]
        finals = [np.where((order >= 0)[:, None], table[np.maximum(order, 0)], 0.0) for table in finals]
    else:
        order = shifted_order(cols_n, points)
        finals = [padded[0], padded[1]]
        finals = [
            np.where((order >= 0)[None, :], table[:, np.maximum(order, 0)], 0.0) for table in finals
        ]
    stack = np.stack(padded + finals).astype(np.float32)
    high = stack.astype(ml_dtypes.bfloat16)
    low = (stack - high.astype(np.float32)).astype(ml_dtypes.bfloat16)
    return jnp.asarray(np.stack([high, low], axis=1))


def frame_gradients(frames, targets, spec_re, spec_im, weights, levels, tables, points):
    count, rows_n, cols_n = frames.shape
    kern = spec_re.shape[0]
    left_tables, right_tables = tables
    per_frame = pl.BlockSpec((1, rows_n, cols_n), lambda i: (i, 0, 0))
    whole_spec = pl.BlockSpec((kern, rows_n, cols_n), lambda i: (0, 0, 0))
    smem = pl.BlockSpec(memory_space=pltpu.SMEM)
    flops = count * (kern * 4 + 4) * 9 * 2 * rows_n * cols_n * cols_n
    return pl.pallas_call(
        functools.partial(frame_kernel, points),
        out_shape=jax.ShapeDtypeStruct(frames.shape, jnp.float32),
        grid=(count,),
        in_specs=[
            per_frame,
            per_frame,
            whole_spec,
            whole_spec,
            smem,
            smem,
            pl.BlockSpec(left_tables.shape, lambda i: (0, 0, 0, 0)),
            pl.BlockSpec(right_tables.shape, lambda i: (0, 0, 0, 0)),
        ],
        out_specs=per_frame,
        scratch_shapes=[
            pltpu.VMEM((kern, rows_n, cols_n), jnp.float32),
            pltpu.VMEM((kern, rows_n, cols_n), jnp.float32),
            pltpu.VMEM((2, rows_n, cols_n), jnp.float32),
            pltpu.VMEM((rows_n, cols_n), jnp.float32),
            pltpu.VMEM((2, rows_n, cols_n), jnp.float32),
        ],
        compiler_params=pltpu.CompilerParams(
            dimension_semantics=("arbitrary",), vmem_limit_bytes=48 * 1024 * 1024
        ),
        cost_estimate=pl.CostEstimate(
            flops=flops, transcendentals=count * rows_n * cols_n, bytes_accessed=8 * 1024 * 1024
        ),
    )(frames, targets, spec_re, spec_im, weights, levels, left_tables, right_tables)


def flip_bit(value, shift):
    bit = (value // shift) % 2
    return value + shift * (1 - 2 * bit)


def exchange_kernel(
    n_tile,
    n_depth,
    x_ref,
    partner_ref,
    mirror_ref,
    out_ref,
    xs,
    recv_a,
    recv_r,
    part_s,
    recv_b,
    blend_s,
    recv_c,
    send_a,
    rsem_a,
    send_r,
    rsem_r,
    send_b,
    rsem_b,
    send_c,
    rsem_c,
):
    me_t = lax.axis_index("tile")
    me_d = lax.axis_index("depth")
    tiles_dev, core, wide = xs.shape
    width = out_ref.shape[-1]
    rows = core // n_depth
    left_t = (me_t + n_tile - 1) % n_tile
    right_t = (me_t + 1) % n_tile
    shifts = []
    shift = 1
    while shift < n_tile:
        shifts.append(shift)
        shift *= 2
    barrier = pltpu.get_barrier_semaphore()
    for step in range(1, n_depth):
        pl.semaphore_signal(
            barrier, inc=1, device_id=(me_t, (me_d + step) % n_depth), device_id_type=MESH
        )
    for shift in shifts:
        pl.semaphore_signal(
            barrier, inc=1, device_id=(flip_bit(me_t, shift), me_d), device_id_type=MESH
        )
    for neighbour in (left_t, right_t):
        for depth in range(n_depth):
            pl.semaphore_signal(barrier, inc=1, device_id=(neighbour, depth), device_id_type=MESH)
    pl.semaphore_wait(barrier, 3 * n_depth - 1 + len(shifts))

    def band(index):
        return pl.ds(pl.multiple_of(index * rows, rows), rows)

    def depth_round(source_of, dst_buf, send_sem, recv_sem):
        copies = []
        for step in range(1, n_depth):
            target = (me_d + step) % n_depth
            copy = pltpu.make_async_remote_copy(
                src_ref=source_of(target),
                dst_ref=dst_buf.at[me_d],
                send_sem=send_sem.at[step],
                recv_sem=recv_sem.at[me_d],
                device_id=(me_t, target),
                device_id_type=MESH,
            )
            copy.start()
            copies.append(copy)
        for step in range(1, n_depth):
            source = (me_d + n_depth - step) % n_depth
            pltpu.make_async_remote_copy(
                src_ref=source_of(source),
                dst_ref=dst_buf.at[source],
                send_sem=send_sem.at[step],
                recv_sem=recv_sem.at[source],
                device_id=(me_t, source),
                device_id_type=MESH,
            ).wait_recv()
        for copy in copies:
            copy.wait_send()

    height = x_ref.shape[1]
    slab = 16
    xs[...] = x_ref[:, :core, :]
    for local in range(tiles_dev):
        if local + 1 < tiles_dev:
            xs[local, core - slab :, :] += x_ref[local + 1, height - slab :, :]
        if local > 0:
            xs[local, :slab, :] += x_ref[local - 1, core : core + slab, :]

    rims = []
    for side, neighbour in enumerate((left_t, right_t)):
        for depth in range(n_depth):
            copy = pltpu.make_async_remote_copy(
                src_ref=xs.at[:, pl.ds(depth * rows, rows), pl.ds(width, wide - width)],
                dst_ref=recv_r.at[side, me_d],
                send_sem=send_r.at[side, depth],
                recv_sem=rsem_r.at[side, me_d],
                device_id=(neighbour, depth),
                device_id_type=MESH,
            )
            copy.start()
            rims.append(copy)
    recv_a[me_d] = xs[:, band(me_d), :width]
    depth_round(lambda target: xs.at[:, band(target), pl.ds(0, width)], recv_a, send_a, rsem_a)
    for side, neighbour in enumerate((left_t, right_t)):
        for depth in range(n_depth):
            pltpu.make_async_remote_copy(
                src_ref=xs.at[:, pl.ds(depth * rows, rows), pl.ds(width, wide - width)],
                dst_ref=recv_r.at[side, depth],
                send_sem=send_r.at[side, depth],
                recv_sem=rsem_r.at[side, depth],
                device_id=(neighbour, depth),
                device_id_type=MESH,
            ).wait_recv()
    for copy in rims:
        copy.wait_send()
    total = recv_a[0]
    from_right = recv_r[0, 0]
    from_left = recv_r[1, 0]
    for slot in range(1, n_depth):
        total = total + recv_a[slot]
        from_right = from_right + recv_r[0, slot]
        from_left = from_left + recv_r[1, slot]
    lanes = lax.broadcasted_iota(jnp.int32, (tiles_dev, rows, width), 2)
    has_left = jnp.where(me_t > 0, 1.0, 0.0)
    has_right = jnp.where(me_t < n_tile - 1, 1.0, 0.0)
    from_left = jnp.where(lanes < HALO, from_left, 0.0) * has_left
    from_right = jnp.where(lanes >= width - HALO, from_right, 0.0) * has_right
    part_s[...] = total + (from_left + from_right)

    swaps = []
    for slot, shift in enumerate(shifts):
        copy = pltpu.make_async_remote_copy(
            src_ref=part_s,
            dst_ref=recv_b.at[slot],
            send_sem=send_b.at[slot],
            recv_sem=rsem_b.at[slot],
            device_id=(flip_bit(me_t, shift), me_d),
            device_id_type=MESH,
        )
        copy.start()
        swaps.append(copy)
    for copy in swaps:
        copy.wait_recv()
    for copy in swaps:
        copy.wait_send()

    lane_a = lax.broadcasted_iota(jnp.int32, (width, width), 0)
    lane_b = lax.broadcasted_iota(jnp.int32, (width, width), 1)
    reverse = jnp.where(lane_a + lane_b == width - 1, 1.0, 0.0).astype(jnp.float32)
    for local in range(tiles_dev):
        partner = partner_ref[local]
        chosen = jnp.zeros((rows, width), jnp.float32)
        for other in range(tiles_dev):
            hit = jnp.where(partner == me_t * tiles_dev + other, 1.0, 0.0)
            chosen = chosen + hit * part_s[other]
        for slot, shift in enumerate(shifts):
            source = flip_bit(me_t, shift)
            for other in range(tiles_dev):
                hit = jnp.where(partner == source * tiles_dev + other, 1.0, 0.0)
                chosen = chosen + hit * recv_b[slot, other]
        mirrored = jnp.dot(
            chosen, reverse, precision=lax.Precision.HIGHEST, preferred_element_type=jnp.float32
        )
        use_mirror = jnp.where(mirror_ref[local] == 1, 1.0, 0.0)
        chosen = use_mirror * mirrored + (1.0 - use_mirror) * chosen
        blend_s[local] = 0.5 * (part_s[local] + chosen)

    recv_c[me_d] = blend_s[...]
    depth_round(lambda target: blend_s, recv_c, send_c, rsem_c)
    for slot in range(n_depth):
        out_ref[:, slot * rows : (slot + 1) * rows, :] = recv_c[slot]


def exchange(values, core, partner_local, mirror_local, call_id):
    n_tile = lax.axis_size("tile")
    n_depth = lax.axis_size("depth")
    n_shift = max(n_tile - 1, 1).bit_length()
    tiles_dev, unused_height, wide = values.shape
    width = core
    piece = (tiles_dev, core // n_depth, width)
    vmem = pl.BlockSpec(memory_space=pltpu.VMEM)
    smem = pl.BlockSpec(memory_space=pltpu.SMEM)
    return pl.pallas_call(
        functools.partial(exchange_kernel, n_tile, n_depth),
        out_shape=jax.ShapeDtypeStruct((tiles_dev, core, width), jnp.float32),
        in_specs=[vmem, smem, smem],
        out_specs=vmem,
        scratch_shapes=[
            pltpu.VMEM((tiles_dev, core, wide), jnp.float32),
            pltpu.VMEM((n_depth,) + piece, jnp.float32),
            pltpu.VMEM((2, n_depth) + piece, jnp.float32),
            pltpu.VMEM(piece, jnp.float32),
            pltpu.VMEM((n_shift,) + piece, jnp.float32),
            pltpu.VMEM(piece, jnp.float32),
            pltpu.VMEM((n_depth,) + piece, jnp.float32),
            pltpu.SemaphoreType.DMA((n_depth,)),
            pltpu.SemaphoreType.DMA((n_depth,)),
            pltpu.SemaphoreType.DMA((2, n_depth)),
            pltpu.SemaphoreType.DMA((2, n_depth)),
            pltpu.SemaphoreType.DMA((n_shift,)),
            pltpu.SemaphoreType.DMA((n_shift,)),
            pltpu.SemaphoreType.DMA((n_depth,)),
            pltpu.SemaphoreType.DMA((n_depth,)),
        ],
        compiler_params=pltpu.CompilerParams(collective_id=call_id, has_side_effects=True),
    )(values, partner_local, mirror_local)


def per_device(
    mask_tiles, target_tiles, kernels, socs_weights, thresholds, partner_table, mirror_flags
):
    tiles_dev, core, unused_width = mask_tiles.shape
    points = FRAME
    index_full = jnp.arange(points, dtype=jnp.int32)
    cos_table, sin_table = angle_tables(index_full, index_full, points)
    offsets = jnp.arange(KSIZE, dtype=jnp.int32) - HALO
    cos_small, sin_small = angle_tables(index_full, offsets, points)
    spec_re, spec_im = left_apply(cos_small, sin_small, -1.0, kernels[0], kernels[1])
    spec_re, spec_im = right_apply(spec_re, spec_im, cos_small.T, sin_small.T, -1.0)
    target_f = target_tiles.astype(jnp.float32)
    rows_n = -(-points // 16) * 16
    cols_n = -(-points // 128) * 128
    row_fill = rows_n - points
    col_fill = cols_n - points
    targets = jnp.pad(
        target_f, ((0, 0), (HALO, rows_n - HALO - core), (HALO, cols_n - HALO - core))
    )
    spec_re_p = jnp.pad(spec_re[0], ((0, 0), (0, row_fill), (0, col_fill)))
    spec_im_p = jnp.pad(spec_im[0], ((0, 0), (0, row_fill), (0, col_fill)))
    tables = (
        table_stack(points, rows_n, rows_n, True),
        table_stack(points, cols_n, cols_n, False),
    )
    strip_height = tiles_dev * core
    step_gradient = jnp.zeros_like(mask_tiles)
    for step_index in range(STEPS):
        strip_rows = mask_tiles.reshape(strip_height, core)
        extended = extended_2(strip_rows, (("tile", 1),), HALO)
        padded = jnp.pad(extended, ((HALO, HALO), (0, 0)))
        frames = jnp.stack(
            [padded[row_index * core : row_index * core + points] for row_index in range(tiles_dev)]
        )
        frames = jnp.pad(frames, ((0, 0), (0, row_fill), (0, col_fill)))
        grads = frame_gradients(
            frames, targets, spec_re_p, spec_im_p, socs_weights[0], thresholds, tables, points
        )
        step_gradient = exchange(grads, core, partner_table, mirror_flags, step_index)
        mask_tiles = mask_tiles - step_rate * step_gradient
    return (mask_tiles, step_gradient)


def solution(mesh):
    return jax.shard_map(
        per_device,
        mesh=mesh,
        in_specs=(
            P("tile", None, None),
            P("tile", None, None),
            P(None, "depth", None, None, None),
            P("depth", None),
            P("depth"),
            P("tile"),
            P("tile"),
        ),
        out_specs=(P("tile", None, None), P("tile", None, None)),
        check_vma=False,
    )
```

```python
import functools

import jax
import jax.numpy as jnp
import ml_dtypes
import numpy as np
from jax import lax
from jax.experimental import pallas as pl
from jax.experimental.pallas import tpu as pltpu
from jax.sharding import PartitionSpec as P

MESH = pl.DeviceIdType.MESH

HALO = 12
FRAME = 152
KSIZE = 25
STEPS = 2


steepness = 3.0
step_rate = 0.05


def extended_2(cells, sides, width):
    for axis, dim in sides:
        count = lax.axis_size(axis)
        ends = count - 1
        head = lax.slice_in_dim(cells, 0, width, axis=dim)
        tail = lax.slice_in_dim(cells, cells.shape[dim] - width, cells.shape[dim], axis=dim)
        cells = jnp.concatenate(
            [
                lax.ppermute(tail, axis, [(i, (i + 1) % count) for i in range(ends)]),
                cells,
                lax.ppermute(head, axis, [((i + 1) % count, i) for i in range(ends)]),
            ],
            axis=dim,
        )
    return cells


def mult_left(matrix, values):
    return jnp.einsum("jk,...kl->...jl", matrix, values, precision=lax.Precision.HIGH)


def mult_right(values, matrix):
    return jnp.einsum("...jk,kl->...jl", values, matrix, precision=lax.Precision.HIGH)


def left_apply(cos_table, sin_table, sign, real_in, imag_in):
    if imag_in is None:
        return (mult_left(cos_table, real_in), sign * mult_left(sin_table, real_in))
    real_out = mult_left(cos_table, real_in) - sign * mult_left(sin_table, imag_in)
    imag_out = mult_left(cos_table, imag_in) + sign * mult_left(sin_table, real_in)
    return (real_out, imag_out)


def right_apply(real_in, imag_in, cos_table, sin_table, sign):
    real_out = mult_right(real_in, cos_table) - sign * mult_right(imag_in, sin_table)
    imag_out = mult_right(imag_in, cos_table) + sign * mult_right(real_in, sin_table)
    return (real_out, imag_out)


def angle_tables(rows_idx, cols_idx, points):
    product = rows_idx[:, None] * cols_idx[None, :] % points
    theta = product.astype(jnp.float32) * (2.0 * np.pi / points)
    return (jnp.cos(theta), jnp.sin(theta))


def split_bf16(values):
    high = lax.reduce_precision(values, exponent_bits=8, mantissa_bits=7)
    return high.astype(jnp.bfloat16), (values - high).astype(jnp.bfloat16)


def split_inside(values):
    spread = values * 65537.0
    high = spread - (spread - values)
    return high.astype(jnp.bfloat16), (values - high).astype(jnp.bfloat16)


def dot3(a_high, a_low, b_high, b_low):
    def product(a, b):
        return jnp.dot(a, b, preferred_element_type=jnp.float32)

    return product(a_high, b_high) + (product(a_high, b_low) + product(a_low, b_high))


def frame_kernel(
    points,
    frame_ref,
    target_ref,
    sre_ref,
    sim_ref,
    w_ref,
    lvl_ref,
    lt_ref,
    rt_ref,
    out_ref,
    fre_s,
    fim_s,
    spec_s,
    slope_s,
    acc_s,
):
    rows_n, cols_n = frame_ref.shape[1:]
    kern = sre_ref.shape[0]
    core = points - 2 * HALO
    scale = 1.0 / (points * points)
    picks = {1.0: (0, 2, 3), -1.0: (0, 4, 5), 0.0: (6, 7, 8)}

    def lmul(index, values):
        high, low = split_inside(values)
        return dot3(lt_ref[index, 0], lt_ref[index, 1], high, low)

    def rmul(values, index):
        high, low = split_inside(values)
        return dot3(high, low, rt_ref[index, 0], rt_ref[index, 1])

    def left(real_in, imag_in, sign):
        plain, plus, minus = picks[sign]
        both = lmul(plain, real_in + imag_in)
        return both - lmul(plus, imag_in), both + lmul(minus, real_in)

    def right(real_in, imag_in, sign):
        plain, plus, minus = picks[sign]
        both = rmul(real_in + imag_in, plain)
        return both - rmul(imag_in, plus), both + rmul(real_in, minus)

    frame = frame_ref[0]
    freq_re, freq_im = right(lmul(0, frame), -lmul(1, frame), -1.0)
    spec_s[0] = freq_re
    spec_s[1] = freq_im

    def forward(k, intensity):
        s_re = sre_ref[k]
        s_im = sim_ref[k]
        f_re = spec_s[0]
        f_im = spec_s[1]
        prod_re = s_re * f_re - s_im * f_im
        prod_im = s_re * f_im + s_im * f_re
        b_re, b_im = left(prod_re, prod_im, 1.0)
        g_re, g_im = right(b_re, b_im, 1.0)
        g_re = g_re * scale
        g_im = g_im * scale
        fre_s[k] = g_re
        fim_s[k] = g_im
        return intensity + w_ref[k] * (g_re * g_re + g_im * g_im)

    intensity = lax.fori_loop(0, kern, forward, jnp.zeros((rows_n, cols_n), jnp.float32))
    rows = lax.broadcasted_iota(jnp.int32, (rows_n, cols_n), 0)
    cols = lax.broadcasted_iota(jnp.int32, (rows_n, cols_n), 1)
    inside = (rows >= HALO) & (rows < HALO + core) & (cols >= HALO) & (cols < HALO + core)
    resist = 1.0 / (1.0 + jnp.exp(-(steepness * (intensity - lvl_ref[0]))))
    slope = 2.0 * (resist - target_ref[0]) * steepness * resist * (1.0 - resist)
    slope_s[...] = jnp.where(inside, slope, 0.0)
    acc_s[...] = jnp.zeros_like(acc_s)

    def backward(k, carry):
        factor = 2.0 * w_ref[k] * slope_s[...]
        b_re, b_im = left(factor * fre_s[k], factor * fim_s[k], -1.0)
        h_re, h_im = right(b_re, b_im, -1.0)
        s_re = sre_ref[k]
        s_im = sim_ref[k]
        acc_s[0] += s_re * h_re + s_im * h_im
        acc_s[1] += s_re * h_im - s_im * h_re
        return carry

    lax.fori_loop(0, kern, backward, 0)
    u_re, u_im = left(acc_s[0], acc_s[1], 0.0)
    out_ref[0] = (rmul(u_re, 6) - rmul(u_im, 7)) * scale


def shifted_order(length, points):
    order = np.full(length, -1)
    order[: points - HALO] = np.arange(HALO, points)
    order[length - HALO :] = np.arange(HALO)
    return order


def table_stack(points, rows_n, cols_n, on_rows):
    index = np.arange(points)
    theta = (np.outer(index, index) % points) * (2.0 * np.pi / points)
    cos_t, sin_t = np.cos(theta), np.sin(theta)
    combos = [cos_t, sin_t, cos_t + sin_t, sin_t - cos_t, cos_t - sin_t, -sin_t - cos_t]
    padded = [np.pad(table, ((0, rows_n - points), (0, cols_n - points))) for table in combos]
    if on_rows:
        order = shifted_order(rows_n, points)
        finals = [padded[0], padded[2], padded[3]]
        finals = [np.where((order >= 0)[:, None], table[np.maximum(order, 0)], 0.0) for table in finals]
    else:
        order = shifted_order(cols_n, points)
        finals = [padded[0], padded[1]]
        finals = [
            np.where((order >= 0)[None, :], table[:, np.maximum(order, 0)], 0.0) for table in finals
        ]
    stack = np.stack(padded + finals).astype(np.float32)
    high = stack.astype(ml_dtypes.bfloat16)
    low = (stack - high.astype(np.float32)).astype(ml_dtypes.bfloat16)
    return jnp.asarray(np.stack([high, low], axis=1))


def frame_gradients(frames, targets, spec_re, spec_im, weights, levels, tables, points):
    count, rows_n, cols_n = frames.shape
    kern = spec_re.shape[0]
    left_tables, right_tables = tables
    per_frame = pl.BlockSpec((1, rows_n, cols_n), lambda i: (i, 0, 0))
    whole_spec = pl.BlockSpec((kern, rows_n, cols_n), lambda i: (0, 0, 0))
    smem = pl.BlockSpec(memory_space=pltpu.SMEM)
    flops = count * (kern * 4 + 4) * 9 * 2 * rows_n * cols_n * cols_n
    return pl.pallas_call(
        functools.partial(frame_kernel, points),
        out_shape=jax.ShapeDtypeStruct(frames.shape, jnp.float32),
        grid=(count,),
        in_specs=[
            per_frame,
            per_frame,
            whole_spec,
            whole_spec,
            smem,
            smem,
            pl.BlockSpec(left_tables.shape, lambda i: (0, 0, 0, 0)),
            pl.BlockSpec(right_tables.shape, lambda i: (0, 0, 0, 0)),
        ],
        out_specs=per_frame,
        scratch_shapes=[
            pltpu.VMEM((kern, rows_n, cols_n), jnp.float32),
            pltpu.VMEM((kern, rows_n, cols_n), jnp.float32),
            pltpu.VMEM((2, rows_n, cols_n), jnp.float32),
            pltpu.VMEM((rows_n, cols_n), jnp.float32),
            pltpu.VMEM((2, rows_n, cols_n), jnp.float32),
        ],
        compiler_params=pltpu.CompilerParams(
            dimension_semantics=("arbitrary",), vmem_limit_bytes=48 * 1024 * 1024
        ),
        cost_estimate=pl.CostEstimate(
            flops=flops, transcendentals=count * rows_n * cols_n, bytes_accessed=8 * 1024 * 1024
        ),
    )(frames, targets, spec_re, spec_im, weights, levels, left_tables, right_tables)


def flip_bit(value, shift):
    bit = (value // shift) % 2
    return value + shift * (1 - 2 * bit)


def exchange_kernel(
    n_tile,
    n_depth,
    x_ref,
    partner_ref,
    mirror_ref,
    out_ref,
    xs,
    recv_a,
    recv_r,
    part_s,
    recv_b,
    blend_s,
    recv_c,
    send_a,
    rsem_a,
    send_r,
    rsem_r,
    send_b,
    rsem_b,
    send_c,
    rsem_c,
):
    me_t = lax.axis_index("tile")
    me_d = lax.axis_index("depth")
    tiles_dev, core, wide = xs.shape
    width = out_ref.shape[-1]
    rows = core // n_depth
    left_t = (me_t + n_tile - 1) % n_tile
    right_t = (me_t + 1) % n_tile
    shifts = []
    shift = 1
    while shift < n_tile:
        shifts.append(shift)
        shift *= 2
    barrier = pltpu.get_barrier_semaphore()
    for step in range(1, n_depth):
        pl.semaphore_signal(
            barrier, inc=1, device_id=(me_t, (me_d + step) % n_depth), device_id_type=MESH
        )
    for shift in shifts:
        pl.semaphore_signal(
            barrier, inc=1, device_id=(flip_bit(me_t, shift), me_d), device_id_type=MESH
        )
    for neighbour in (left_t, right_t):
        for depth in range(n_depth):
            pl.semaphore_signal(barrier, inc=1, device_id=(neighbour, depth), device_id_type=MESH)
    pl.semaphore_wait(barrier, 3 * n_depth - 1 + len(shifts))

    def band(index):
        return pl.ds(pl.multiple_of(index * rows, rows), rows)

    def depth_round(source_of, dst_buf, send_sem, recv_sem):
        copies = []
        for step in range(1, n_depth):
            target = (me_d + step) % n_depth
            copy = pltpu.make_async_remote_copy(
                src_ref=source_of(target),
                dst_ref=dst_buf.at[me_d],
                send_sem=send_sem.at[step],
                recv_sem=recv_sem.at[me_d],
                device_id=(me_t, target),
                device_id_type=MESH,
            )
            copy.start()
            copies.append(copy)
        for step in range(1, n_depth):
            source = (me_d + n_depth - step) % n_depth
            pltpu.make_async_remote_copy(
                src_ref=source_of(source),
                dst_ref=dst_buf.at[source],
                send_sem=send_sem.at[step],
                recv_sem=recv_sem.at[source],
                device_id=(me_t, source),
                device_id_type=MESH,
            ).wait_recv()
        for copy in copies:
            copy.wait_send()

    height = x_ref.shape[1]
    slab = 16
    xs[...] = x_ref[:, :core, :]
    for local in range(tiles_dev):
        if local + 1 < tiles_dev:
            xs[local, core - slab :, :] += x_ref[local + 1, height - slab :, :]
        if local > 0:
            xs[local, :slab, :] += x_ref[local - 1, core : core + slab, :]

    rims = []
    for side, neighbour in enumerate((left_t, right_t)):
        for depth in range(n_depth):
            copy = pltpu.make_async_remote_copy(
                src_ref=xs.at[:, pl.ds(depth * rows, rows), pl.ds(width, wide - width)],
                dst_ref=recv_r.at[side, me_d],
                send_sem=send_r.at[side, depth],
                recv_sem=rsem_r.at[side, me_d],
                device_id=(neighbour, depth),
                device_id_type=MESH,
            )
            copy.start()
            rims.append(copy)
    recv_a[me_d] = xs[:, band(me_d), :width]
    depth_round(lambda target: xs.at[:, band(target), pl.ds(0, width)], recv_a, send_a, rsem_a)
    for side, neighbour in enumerate((left_t, right_t)):
        for depth in range(n_depth):
            pltpu.make_async_remote_copy(
                src_ref=xs.at[:, pl.ds(depth * rows, rows), pl.ds(width, wide - width)],
                dst_ref=recv_r.at[side, depth],
                send_sem=send_r.at[side, depth],
                recv_sem=rsem_r.at[side, depth],
                device_id=(neighbour, depth),
                device_id_type=MESH,
            ).wait_recv()
    for copy in rims:
        copy.wait_send()
    total = recv_a[0]
    from_right = recv_r[0, 0]
    from_left = recv_r[1, 0]
    for slot in range(1, n_depth):
        total = total + recv_a[slot]
        from_right = from_right + recv_r[0, slot]
        from_left = from_left + recv_r[1, slot]
    lanes = lax.broadcasted_iota(jnp.int32, (tiles_dev, rows, width), 2)
    has_left = jnp.where(me_t > 0, 1.0, 0.0)
    has_right = jnp.where(me_t < n_tile - 1, 1.0, 0.0)
    from_left = jnp.where(lanes < HALO, from_left, 0.0) * has_left
    from_right = jnp.where(lanes >= width - HALO, from_right, 0.0) * has_right
    part_s[...] = total + (from_left + from_right)

    swaps = []
    for slot, shift in enumerate(shifts):
        copy = pltpu.make_async_remote_copy(
            src_ref=part_s,
            dst_ref=recv_b.at[slot],
            send_sem=send_b.at[slot],
            recv_sem=rsem_b.at[slot],
            device_id=(flip_bit(me_t, shift), me_d),
            device_id_type=MESH,
        )
        copy.start()
        swaps.append(copy)
    for copy in swaps:
        copy.wait_recv()
    for copy in swaps:
        copy.wait_send()

    lane_a = lax.broadcasted_iota(jnp.int32, (width, width), 0)
    lane_b = lax.broadcasted_iota(jnp.int32, (width, width), 1)
    reverse = jnp.where(lane_a + lane_b == width - 1, 1.0, 0.0).astype(jnp.float32)
    for local in range(tiles_dev):
        partner = partner_ref[local]
        chosen = jnp.zeros((rows, width), jnp.float32)
        for other in range(tiles_dev):
            hit = jnp.where(partner == me_t * tiles_dev + other, 1.0, 0.0)
            chosen = chosen + hit * part_s[other]
        for slot, shift in enumerate(shifts):
            source = flip_bit(me_t, shift)
            for other in range(tiles_dev):
                hit = jnp.where(partner == source * tiles_dev + other, 1.0, 0.0)
                chosen = chosen + hit * recv_b[slot, other]
        mirrored = jnp.dot(
            chosen, reverse, precision=lax.Precision.HIGHEST, preferred_element_type=jnp.float32
        )
        use_mirror = jnp.where(mirror_ref[local] == 1, 1.0, 0.0)
        chosen = use_mirror * mirrored + (1.0 - use_mirror) * chosen
        blend_s[local] = 0.5 * (part_s[local] + chosen)

    recv_c[me_d] = blend_s[...]
    depth_round(lambda target: blend_s, recv_c, send_c, rsem_c)
    for slot in range(n_depth):
        out_ref[:, slot * rows : (slot + 1) * rows, :] = recv_c[slot]


def exchange(values, core, partner_local, mirror_local, call_id):
    n_tile = lax.axis_size("tile")
    n_depth = lax.axis_size("depth")
    n_shift = max(n_tile - 1, 1).bit_length()
    tiles_dev, unused_height, wide = values.shape
    width = core
    piece = (tiles_dev, core // n_depth, width)
    vmem = pl.BlockSpec(memory_space=pltpu.VMEM)
    smem = pl.BlockSpec(memory_space=pltpu.SMEM)
    return pl.pallas_call(
        functools.partial(exchange_kernel, n_tile, n_depth),
        out_shape=jax.ShapeDtypeStruct((tiles_dev, core, width), jnp.float32),
        in_specs=[vmem, smem, smem],
        out_specs=vmem,
        scratch_shapes=[
            pltpu.VMEM((tiles_dev, core, wide), jnp.float32),
            pltpu.VMEM((n_depth,) + piece, jnp.float32),
            pltpu.VMEM((2, n_depth) + piece, jnp.float32),
            pltpu.VMEM(piece, jnp.float32),
            pltpu.VMEM((n_shift,) + piece, jnp.float32),
            pltpu.VMEM(piece, jnp.float32),
            pltpu.VMEM((n_depth,) + piece, jnp.float32),
            pltpu.SemaphoreType.DMA((n_depth,)),
            pltpu.SemaphoreType.DMA((n_depth,)),
            pltpu.SemaphoreType.DMA((2, n_depth)),
            pltpu.SemaphoreType.DMA((2, n_depth)),
            pltpu.SemaphoreType.DMA((n_shift,)),
            pltpu.SemaphoreType.DMA((n_shift,)),
            pltpu.SemaphoreType.DMA((n_depth,)),
            pltpu.SemaphoreType.DMA((n_depth,)),
        ],
        compiler_params=pltpu.CompilerParams(collective_id=call_id, has_side_effects=True),
    )(values, partner_local, mirror_local)


def small_tables(points, length):
    theta = (np.outer(np.arange(length), np.arange(KSIZE) - HALO) % points) * (2.0 * np.pi / points)
    inside = (np.arange(length) < points)[:, None]
    return np.where(inside, np.cos(theta), 0.0), np.where(inside, np.sin(theta), 0.0)


def kernel_spectra(kernel_pair, points, rows_n, cols_n):
    cos_r, sin_r = small_tables(points, rows_n)
    cos_c, sin_c = small_tables(points, cols_n)
    left_t = jnp.asarray(np.concatenate([cos_r, sin_r], axis=0).astype(np.float32))
    right_t = jnp.asarray(np.concatenate([cos_c.T, sin_c.T], axis=1).astype(np.float32))
    both = jnp.einsum("jk,cnkl->cnjl", left_t, kernel_pair, precision=lax.Precision.HIGHEST)
    stage_re = both[0, :, :rows_n] + both[1, :, rows_n:]
    stage_im = both[1, :, :rows_n] - both[0, :, rows_n:]
    stacked = jnp.stack([stage_re, stage_im])
    out = jnp.einsum("cnjk,kl->cnjl", stacked, right_t, precision=lax.Precision.HIGHEST)
    spec_re = out[0, ..., :cols_n] + out[1, ..., cols_n:]
    spec_im = out[1, ..., :cols_n] - out[0, ..., cols_n:]
    return spec_re, spec_im


def per_device(
    mask_tiles, target_tiles, kernels, socs_weights, thresholds, partner_table, mirror_flags
):
    tiles_dev, core, unused_width = mask_tiles.shape
    points = FRAME
    target_f = target_tiles.astype(jnp.float32)
    rows_n = -(-points // 16) * 16
    cols_n = -(-points // 128) * 128
    row_fill = rows_n - points
    col_fill = cols_n - points
    targets = jnp.pad(
        target_f, ((0, 0), (HALO, rows_n - HALO - core), (HALO, cols_n - HALO - core))
    )
    spec_re_p, spec_im_p = kernel_spectra(kernels[:, 0], points, rows_n, cols_n)
    tables = (
        table_stack(points, rows_n, rows_n, True),
        table_stack(points, cols_n, cols_n, False),
    )
    strip_height = tiles_dev * core
    step_gradient = jnp.zeros_like(mask_tiles)
    for step_index in range(STEPS):
        strip_rows = mask_tiles.reshape(strip_height, core)
        extended = extended_2(strip_rows, (("tile", 1),), HALO)
        padded = jnp.pad(extended, ((HALO, HALO), (0, 0)))
        frames = jnp.stack(
            [padded[row_index * core : row_index * core + points] for row_index in range(tiles_dev)]
        )
        frames = jnp.pad(frames, ((0, 0), (0, row_fill), (0, col_fill)))
        grads = frame_gradients(
            frames, targets, spec_re_p, spec_im_p, socs_weights[0], thresholds, tables, points
        )
        step_gradient = exchange(grads, core, partner_table, mirror_flags, step_index)
        mask_tiles = mask_tiles - step_rate * step_gradient
    return (mask_tiles, step_gradient)


def solution(mesh):
    return jax.shard_map(
        per_device,
        mesh=mesh,
        in_specs=(
            P("tile", None, None),
            P("tile", None, None),
            P(None, "depth", None, None, None),
            P("depth", None),
            P("depth"),
            P("tile"),
            P("tile"),
        ),
        out_specs=(P("tile", None, None), P("tile", None, None)),
        check_vma=False,
    )
```

```python
import functools

import jax
import jax.numpy as jnp
import ml_dtypes
import numpy as np
from jax import lax
from jax.experimental import pallas as pl
from jax.experimental.pallas import tpu as pltpu
from jax.sharding import PartitionSpec as P

MESH = pl.DeviceIdType.MESH

HALO = 12
FRAME = 152
KSIZE = 25
STEPS = 2


steepness = 3.0
step_rate = 0.05


def extended_2(cells, sides, width):
    for axis, dim in sides:
        count = lax.axis_size(axis)
        ends = count - 1
        head = lax.slice_in_dim(cells, 0, width, axis=dim)
        tail = lax.slice_in_dim(cells, cells.shape[dim] - width, cells.shape[dim], axis=dim)
        cells = jnp.concatenate(
            [
                lax.ppermute(tail, axis, [(i, (i + 1) % count) for i in range(ends)]),
                cells,
                lax.ppermute(head, axis, [((i + 1) % count, i) for i in range(ends)]),
            ],
            axis=dim,
        )
    return cells


def mult_left(matrix, values):
    return jnp.einsum("jk,...kl->...jl", matrix, values, precision=lax.Precision.HIGH)


def mult_right(values, matrix):
    return jnp.einsum("...jk,kl->...jl", values, matrix, precision=lax.Precision.HIGH)


def left_apply(cos_table, sin_table, sign, real_in, imag_in):
    if imag_in is None:
        return (mult_left(cos_table, real_in), sign * mult_left(sin_table, real_in))
    real_out = mult_left(cos_table, real_in) - sign * mult_left(sin_table, imag_in)
    imag_out = mult_left(cos_table, imag_in) + sign * mult_left(sin_table, real_in)
    return (real_out, imag_out)


def right_apply(real_in, imag_in, cos_table, sin_table, sign):
    real_out = mult_right(real_in, cos_table) - sign * mult_right(imag_in, sin_table)
    imag_out = mult_right(imag_in, cos_table) + sign * mult_right(real_in, sin_table)
    return (real_out, imag_out)


def angle_tables(rows_idx, cols_idx, points):
    product = rows_idx[:, None] * cols_idx[None, :] % points
    theta = product.astype(jnp.float32) * (2.0 * np.pi / points)
    return (jnp.cos(theta), jnp.sin(theta))


def split_bf16(values):
    high = lax.reduce_precision(values, exponent_bits=8, mantissa_bits=7)
    return high.astype(jnp.bfloat16), (values - high).astype(jnp.bfloat16)


def split_inside(values):
    spread = values * 65537.0
    high = spread - (spread - values)
    return high.astype(jnp.bfloat16), (values - high).astype(jnp.bfloat16)


def dot3(a_high, a_low, b_high, b_low):
    def product(a, b):
        return jnp.dot(a, b, preferred_element_type=jnp.float32)

    return product(a_high, b_high) + (product(a_high, b_low) + product(a_low, b_high))


def frame_kernel(
    points,
    frame_ref,
    target_ref,
    sre_ref,
    sim_ref,
    w_ref,
    lvl_ref,
    lt_ref,
    rt_ref,
    out_ref,
    fre_s,
    fim_s,
    spec_s,
    slope_s,
    acc_s,
):
    rows_n, cols_n = frame_ref.shape[1:]
    kern = sre_ref.shape[0]
    core = points - 2 * HALO
    scale = 1.0 / (points * points)
    picks = {1.0: (0, 2, 3), -1.0: (0, 4, 5), 0.0: (6, 7, 8)}

    def lmul(index, values):
        high, low = split_inside(values)
        return dot3(lt_ref[index, 0], lt_ref[index, 1], high, low)

    def rmul(values, index):
        high, low = split_inside(values)
        return dot3(high, low, rt_ref[index, 0], rt_ref[index, 1])

    def left(real_in, imag_in, sign):
        plain, plus, minus = picks[sign]
        both = lmul(plain, real_in + imag_in)
        return both - lmul(plus, imag_in), both + lmul(minus, real_in)

    def right(real_in, imag_in, sign):
        plain, plus, minus = picks[sign]
        both = rmul(real_in + imag_in, plain)
        return both - rmul(imag_in, plus), both + rmul(real_in, minus)

    frame = frame_ref[0]
    freq_re, freq_im = right(lmul(0, frame), -lmul(1, frame), -1.0)
    spec_s[0] = freq_re
    spec_s[1] = freq_im

    def forward(k, intensity):
        s_re = sre_ref[k]
        s_im = sim_ref[k]
        f_re = spec_s[0]
        f_im = spec_s[1]
        prod_re = s_re * f_re - s_im * f_im
        prod_im = s_re * f_im + s_im * f_re
        b_re, b_im = left(prod_re, prod_im, 1.0)
        g_re, g_im = right(b_re, b_im, 1.0)
        g_re = g_re * scale
        g_im = g_im * scale
        fre_s[k] = g_re
        fim_s[k] = g_im
        return intensity + w_ref[k] * (g_re * g_re + g_im * g_im)

    intensity = lax.fori_loop(0, kern, forward, jnp.zeros((rows_n, cols_n), jnp.float32))
    rows = lax.broadcasted_iota(jnp.int32, (rows_n, cols_n), 0)
    cols = lax.broadcasted_iota(jnp.int32, (rows_n, cols_n), 1)
    inside = (rows >= HALO) & (rows < HALO + core) & (cols >= HALO) & (cols < HALO + core)
    resist = 1.0 / (1.0 + jnp.exp(-(steepness * (intensity - lvl_ref[0]))))
    slope = 2.0 * (resist - target_ref[0]) * steepness * resist * (1.0 - resist)
    slope_s[...] = jnp.where(inside, slope, 0.0)
    acc_s[...] = jnp.zeros_like(acc_s)

    def backward(k, carry):
        factor = 2.0 * w_ref[k] * slope_s[...]
        b_re, b_im = left(factor * fre_s[k], factor * fim_s[k], -1.0)
        h_re, h_im = right(b_re, b_im, -1.0)
        s_re = sre_ref[k]
        s_im = sim_ref[k]
        acc_s[0] += s_re * h_re + s_im * h_im
        acc_s[1] += s_re * h_im - s_im * h_re
        return carry

    lax.fori_loop(0, kern, backward, 0)
    u_re, u_im = left(acc_s[0], acc_s[1], 0.0)
    out_ref[0] = (rmul(u_re, 6) - rmul(u_im, 7)) * scale


def shifted_order(length, points):
    order = np.full(length, -1)
    order[: points - HALO] = np.arange(HALO, points)
    order[length - HALO :] = np.arange(HALO)
    return order


def table_stack(points, rows_n, cols_n, on_rows):
    index = np.arange(points)
    theta = (np.outer(index, index) % points) * (2.0 * np.pi / points)
    cos_t, sin_t = np.cos(theta), np.sin(theta)
    combos = [cos_t, sin_t, cos_t + sin_t, sin_t - cos_t, cos_t - sin_t, -sin_t - cos_t]
    padded = [np.pad(table, ((0, rows_n - points), (0, cols_n - points))) for table in combos]
    if on_rows:
        order = shifted_order(rows_n, points)
        finals = [padded[0], padded[2], padded[3]]
        finals = [np.where((order >= 0)[:, None], table[np.maximum(order, 0)], 0.0) for table in finals]
    else:
        order = shifted_order(cols_n, points)
        finals = [padded[0], padded[1]]
        finals = [
            np.where((order >= 0)[None, :], table[:, np.maximum(order, 0)], 0.0) for table in finals
        ]
    stack = np.stack(padded + finals).astype(np.float32)
    high = stack.astype(ml_dtypes.bfloat16)
    low = (stack - high.astype(np.float32)).astype(ml_dtypes.bfloat16)
    return jnp.asarray(np.stack([high, low], axis=1))


def frame_gradients(frames, targets, spec_re, spec_im, weights, levels, tables, points):
    count, rows_n, cols_n = frames.shape
    kern = spec_re.shape[0]
    left_tables, right_tables = tables
    per_frame = pl.BlockSpec((1, rows_n, cols_n), lambda i: (i, 0, 0))
    whole_spec = pl.BlockSpec((kern, rows_n, cols_n), lambda i: (0, 0, 0))
    smem = pl.BlockSpec(memory_space=pltpu.SMEM)
    flops = count * (kern * 4 + 4) * 9 * 2 * rows_n * cols_n * cols_n
    return pl.pallas_call(
        functools.partial(frame_kernel, points),
        out_shape=jax.ShapeDtypeStruct(frames.shape, jnp.float32),
        grid=(count,),
        in_specs=[
            per_frame,
            per_frame,
            whole_spec,
            whole_spec,
            smem,
            smem,
            pl.BlockSpec(left_tables.shape, lambda i: (0, 0, 0, 0)),
            pl.BlockSpec(right_tables.shape, lambda i: (0, 0, 0, 0)),
        ],
        out_specs=per_frame,
        scratch_shapes=[
            pltpu.VMEM((kern, rows_n, cols_n), jnp.float32),
            pltpu.VMEM((kern, rows_n, cols_n), jnp.float32),
            pltpu.VMEM((2, rows_n, cols_n), jnp.float32),
            pltpu.VMEM((rows_n, cols_n), jnp.float32),
            pltpu.VMEM((2, rows_n, cols_n), jnp.float32),
        ],
        compiler_params=pltpu.CompilerParams(
            dimension_semantics=("arbitrary",), vmem_limit_bytes=48 * 1024 * 1024
        ),
        cost_estimate=pl.CostEstimate(
            flops=flops, transcendentals=count * rows_n * cols_n, bytes_accessed=8 * 1024 * 1024
        ),
    )(frames, targets, spec_re, spec_im, weights, levels, left_tables, right_tables)


def flip_bit(value, shift):
    bit = (value // shift) % 2
    return value + shift * (1 - 2 * bit)


def exchange_kernel(n_tile, n_depth, with_halo, x_ref, partner_ref, mirror_ref, *refs):
    outputs = 2 if with_halo else 1
    out_ref = refs[0]
    (
        xs,
        recv_a,
        recv_r,
        part_s,
        recv_b,
        blend_s,
        recv_c,
        send_a,
        rsem_a,
        send_r,
        rsem_r,
        send_b,
        rsem_b,
        send_c,
        rsem_c,
    ) = refs[outputs : outputs + 15]
    me_t = lax.axis_index("tile")
    me_d = lax.axis_index("depth")
    tiles_dev, core, wide = xs.shape
    width = out_ref.shape[-1]
    rows = core // n_depth
    left_t = (me_t + n_tile - 1) % n_tile
    right_t = (me_t + 1) % n_tile
    shifts = []
    shift = 1
    while shift < n_tile:
        shifts.append(shift)
        shift *= 2
    barrier = pltpu.get_barrier_semaphore()
    for step in range(1, n_depth):
        pl.semaphore_signal(
            barrier, inc=1, device_id=(me_t, (me_d + step) % n_depth), device_id_type=MESH
        )
    for shift in shifts:
        pl.semaphore_signal(
            barrier, inc=1, device_id=(flip_bit(me_t, shift), me_d), device_id_type=MESH
        )
    for neighbour in (left_t, right_t):
        for depth in range(n_depth):
            pl.semaphore_signal(barrier, inc=1, device_id=(neighbour, depth), device_id_type=MESH)
    pl.semaphore_wait(barrier, 3 * n_depth - 1 + len(shifts))

    def band(index):
        return pl.ds(pl.multiple_of(index * rows, rows), rows)

    def depth_round(source_of, dst_buf, send_sem, recv_sem):
        copies = []
        for step in range(1, n_depth):
            target = (me_d + step) % n_depth
            copy = pltpu.make_async_remote_copy(
                src_ref=source_of(target),
                dst_ref=dst_buf.at[me_d],
                send_sem=send_sem.at[step],
                recv_sem=recv_sem.at[me_d],
                device_id=(me_t, target),
                device_id_type=MESH,
            )
            copy.start()
            copies.append(copy)
        for step in range(1, n_depth):
            source = (me_d + n_depth - step) % n_depth
            pltpu.make_async_remote_copy(
                src_ref=source_of(source),
                dst_ref=dst_buf.at[source],
                send_sem=send_sem.at[step],
                recv_sem=recv_sem.at[source],
                device_id=(me_t, source),
                device_id_type=MESH,
            ).wait_recv()
        for copy in copies:
            copy.wait_send()

    height = x_ref.shape[1]
    slab = 16
    xs[...] = x_ref[:, :core, :]
    for local in range(tiles_dev):
        if local + 1 < tiles_dev:
            xs[local, core - slab :, :] += x_ref[local + 1, height - slab :, :]
        if local > 0:
            xs[local, :slab, :] += x_ref[local - 1, core : core + slab, :]

    rims = []
    for side, neighbour in enumerate((left_t, right_t)):
        for depth in range(n_depth):
            copy = pltpu.make_async_remote_copy(
                src_ref=xs.at[:, pl.ds(depth * rows, rows), pl.ds(width, wide - width)],
                dst_ref=recv_r.at[side, me_d],
                send_sem=send_r.at[side, depth],
                recv_sem=rsem_r.at[side, me_d],
                device_id=(neighbour, depth),
                device_id_type=MESH,
            )
            copy.start()
            rims.append(copy)
    recv_a[me_d] = xs[:, band(me_d), :width]
    depth_round(lambda target: xs.at[:, band(target), pl.ds(0, width)], recv_a, send_a, rsem_a)
    for side, neighbour in enumerate((left_t, right_t)):
        for depth in range(n_depth):
            pltpu.make_async_remote_copy(
                src_ref=xs.at[:, pl.ds(depth * rows, rows), pl.ds(width, wide - width)],
                dst_ref=recv_r.at[side, depth],
                send_sem=send_r.at[side, depth],
                recv_sem=rsem_r.at[side, depth],
                device_id=(neighbour, depth),
                device_id_type=MESH,
            ).wait_recv()
    for copy in rims:
        copy.wait_send()
    total = recv_a[0]
    from_right = recv_r[0, 0]
    from_left = recv_r[1, 0]
    for slot in range(1, n_depth):
        total = total + recv_a[slot]
        from_right = from_right + recv_r[0, slot]
        from_left = from_left + recv_r[1, slot]
    lanes = lax.broadcasted_iota(jnp.int32, (tiles_dev, rows, width), 2)
    has_left = jnp.where(me_t > 0, 1.0, 0.0)
    has_right = jnp.where(me_t < n_tile - 1, 1.0, 0.0)
    from_left = jnp.where(lanes < HALO, from_left, 0.0) * has_left
    from_right = jnp.where(lanes >= width - HALO, from_right, 0.0) * has_right
    part_s[...] = total + (from_left + from_right)

    swaps = []
    for slot, shift in enumerate(shifts):
        copy = pltpu.make_async_remote_copy(
            src_ref=part_s,
            dst_ref=recv_b.at[slot],
            send_sem=send_b.at[slot],
            recv_sem=rsem_b.at[slot],
            device_id=(flip_bit(me_t, shift), me_d),
            device_id_type=MESH,
        )
        copy.start()
        swaps.append(copy)
    for copy in swaps:
        copy.wait_recv()
    for copy in swaps:
        copy.wait_send()

    lane_a = lax.broadcasted_iota(jnp.int32, (width, width), 0)
    lane_b = lax.broadcasted_iota(jnp.int32, (width, width), 1)
    reverse = jnp.where(lane_a + lane_b == width - 1, 1.0, 0.0).astype(jnp.float32)
    for local in range(tiles_dev):
        partner = partner_ref[local]
        chosen = jnp.zeros((rows, width), jnp.float32)
        for other in range(tiles_dev):
            hit = jnp.where(partner == me_t * tiles_dev + other, 1.0, 0.0)
            chosen = chosen + hit * part_s[other]
        for slot, shift in enumerate(shifts):
            source = flip_bit(me_t, shift)
            for other in range(tiles_dev):
                hit = jnp.where(partner == source * tiles_dev + other, 1.0, 0.0)
                chosen = chosen + hit * recv_b[slot, other]
        mirrored = jnp.dot(
            chosen, reverse, precision=lax.Precision.HIGHEST, preferred_element_type=jnp.float32
        )
        use_mirror = jnp.where(mirror_ref[local] == 1, 1.0, 0.0)
        chosen = use_mirror * mirrored + (1.0 - use_mirror) * chosen
        blend_s[local] = 0.5 * (part_s[local] + chosen)

    recv_c[me_d] = blend_s[...]
    halo_copies = []
    if with_halo:
        nb_ref = refs[1]
        recv_n, send_n, rsem_n = refs[outputs + 15 :]
        for side, neighbour in enumerate((left_t, right_t)):
            for depth in range(n_depth):
                copy = pltpu.make_async_remote_copy(
                    src_ref=blend_s,
                    dst_ref=recv_n.at[side, me_d],
                    send_sem=send_n.at[side, depth],
                    recv_sem=rsem_n.at[side, me_d],
                    device_id=(neighbour, depth),
                    device_id_type=MESH,
                )
                copy.start()
                halo_copies.append(copy)
    depth_round(lambda target: blend_s, recv_c, send_c, rsem_c)
    if with_halo:
        for side, neighbour in enumerate((left_t, right_t)):
            for depth in range(n_depth):
                pltpu.make_async_remote_copy(
                    src_ref=blend_s,
                    dst_ref=recv_n.at[side, depth],
                    send_sem=send_n.at[side, depth],
                    recv_sem=rsem_n.at[side, depth],
                    device_id=(neighbour, depth),
                    device_id_type=MESH,
                ).wait_recv()
        for copy in halo_copies:
            copy.wait_send()
    for slot in range(n_depth):
        out_ref[:, slot * rows : (slot + 1) * rows, :] = recv_c[slot]
        if with_halo:
            for side in range(2):
                nb_ref[side, :, slot * rows : (slot + 1) * rows, :] = recv_n[side, slot]


def exchange(values, core, partner_local, mirror_local, call_id, with_halo):
    n_tile = lax.axis_size("tile")
    n_depth = lax.axis_size("depth")
    n_shift = max(n_tile - 1, 1).bit_length()
    tiles_dev, unused_height, wide = values.shape
    width = core
    piece = (tiles_dev, core // n_depth, width)
    vmem = pl.BlockSpec(memory_space=pltpu.VMEM)
    out_shape = jax.ShapeDtypeStruct((tiles_dev, core, width), jnp.float32)
    out_specs = vmem
    extra_first, extra_last = [], []
    if with_halo:
        out_shape = (out_shape, jax.ShapeDtypeStruct((2, tiles_dev, core, width), jnp.float32))
        out_specs = (vmem, vmem)
        extra_last = [
            pltpu.VMEM((2, n_depth) + piece, jnp.float32),
            pltpu.SemaphoreType.DMA((2, n_depth)),
            pltpu.SemaphoreType.DMA((2, n_depth)),
        ]
    smem = pl.BlockSpec(memory_space=pltpu.SMEM)
    return pl.pallas_call(
        functools.partial(exchange_kernel, n_tile, n_depth, with_halo),
        out_shape=out_shape,
        in_specs=[vmem, smem, smem],
        out_specs=out_specs,
        scratch_shapes=extra_first + [
            pltpu.VMEM((tiles_dev, core, wide), jnp.float32),
            pltpu.VMEM((n_depth,) + piece, jnp.float32),
            pltpu.VMEM((2, n_depth) + piece, jnp.float32),
            pltpu.VMEM(piece, jnp.float32),
            pltpu.VMEM((n_shift,) + piece, jnp.float32),
            pltpu.VMEM(piece, jnp.float32),
            pltpu.VMEM((n_depth,) + piece, jnp.float32),
            pltpu.SemaphoreType.DMA((n_depth,)),
            pltpu.SemaphoreType.DMA((n_depth,)),
            pltpu.SemaphoreType.DMA((2, n_depth)),
            pltpu.SemaphoreType.DMA((2, n_depth)),
            pltpu.SemaphoreType.DMA((n_shift,)),
            pltpu.SemaphoreType.DMA((n_shift,)),
            pltpu.SemaphoreType.DMA((n_depth,)),
            pltpu.SemaphoreType.DMA((n_depth,)),
        ]
        + extra_last,
        compiler_params=pltpu.CompilerParams(collective_id=call_id, has_side_effects=True),
    )(values, partner_local, mirror_local)


def per_device(
    mask_tiles, target_tiles, kernels, socs_weights, thresholds, partner_table, mirror_flags
):
    tiles_dev, core, unused_width = mask_tiles.shape
    points = FRAME
    index_full = jnp.arange(points, dtype=jnp.int32)
    cos_table, sin_table = angle_tables(index_full, index_full, points)
    offsets = jnp.arange(KSIZE, dtype=jnp.int32) - HALO
    cos_small, sin_small = angle_tables(index_full, offsets, points)
    spec_re, spec_im = left_apply(cos_small, sin_small, -1.0, kernels[0], kernels[1])
    spec_re, spec_im = right_apply(spec_re, spec_im, cos_small.T, sin_small.T, -1.0)
    target_f = target_tiles.astype(jnp.float32)
    rows_n = -(-points // 16) * 16
    cols_n = -(-points // 128) * 128
    row_fill = rows_n - points
    col_fill = cols_n - points
    targets = jnp.pad(
        target_f, ((0, 0), (HALO, rows_n - HALO - core), (HALO, cols_n - HALO - core))
    )
    spec_re_p = jnp.pad(spec_re[0], ((0, 0), (0, row_fill), (0, col_fill)))
    spec_im_p = jnp.pad(spec_im[0], ((0, 0), (0, row_fill), (0, col_fill)))
    tables = (
        table_stack(points, rows_n, rows_n, True),
        table_stack(points, cols_n, cols_n, False),
    )
    strip_height = tiles_dev * core
    step_gradient = jnp.zeros_like(mask_tiles)
    me_t = lax.axis_index("tile")
    n_tile = lax.axis_size("tile")
    halo_left = halo_right = None
    for step_index in range(STEPS):
        strip_rows = mask_tiles.reshape(strip_height, core)
        if halo_left is None:
            extended = extended_2(strip_rows, (("tile", 1),), HALO)
            halo_left = extended[:, :HALO]
            halo_right = extended[:, HALO + core :]
        else:
            extended = jnp.concatenate([halo_left, strip_rows, halo_right], axis=1)
        padded = jnp.pad(extended, ((HALO, HALO), (0, 0)))
        frames = jnp.stack(
            [padded[row_index * core : row_index * core + points] for row_index in range(tiles_dev)]
        )
        frames = jnp.pad(frames, ((0, 0), (0, row_fill), (0, col_fill)))
        grads = frame_gradients(
            frames, targets, spec_re_p, spec_im_p, socs_weights[0], thresholds, tables, points
        )
        with_halo = step_index + 1 < STEPS
        result = exchange(grads, core, partner_table, mirror_flags, step_index, with_halo)
        if with_halo:
            step_gradient, beside = result
            from_right = beside[0].reshape(strip_height, core)[:, :HALO]
            from_left = beside[1].reshape(strip_height, core)[:, core - HALO :]
            halo_left = jnp.where(me_t > 0, halo_left - step_rate * from_left, 0.0)
            halo_right = jnp.where(me_t < n_tile - 1, halo_right - step_rate * from_right, 0.0)
        else:
            step_gradient = result
        mask_tiles = mask_tiles - step_rate * step_gradient
    return (mask_tiles, step_gradient)


def solution(mesh):
    return jax.shard_map(
        per_device,
        mesh=mesh,
        in_specs=(
            P("tile", None, None),
            P("tile", None, None),
            P(None, "depth", None, None, None),
            P("depth", None),
            P("depth"),
            P("tile"),
            P("tile"),
        ),
        out_specs=(P("tile", None, None), P("tile", None, None)),
        check_vma=False,
    )
```

```python
import functools

import jax
import jax.numpy as jnp
import ml_dtypes
import numpy as np
from jax import lax
from jax.experimental import pallas as pl
from jax.experimental.pallas import tpu as pltpu
from jax.sharding import PartitionSpec as P

MESH = pl.DeviceIdType.MESH

HALO = 12
FRAME = 152
KSIZE = 25
STEPS = 2


steepness = 3.0
step_rate = 0.05


def extended_2(cells, sides, width):
    for axis, dim in sides:
        count = lax.axis_size(axis)
        ends = count - 1
        head = lax.slice_in_dim(cells, 0, width, axis=dim)
        tail = lax.slice_in_dim(cells, cells.shape[dim] - width, cells.shape[dim], axis=dim)
        cells = jnp.concatenate(
            [
                lax.ppermute(tail, axis, [(i, (i + 1) % count) for i in range(ends)]),
                cells,
                lax.ppermute(head, axis, [((i + 1) % count, i) for i in range(ends)]),
            ],
            axis=dim,
        )
    return cells


def mult_left(matrix, values):
    return jnp.einsum("jk,...kl->...jl", matrix, values, precision=lax.Precision.HIGH)


def mult_right(values, matrix):
    return jnp.einsum("...jk,kl->...jl", values, matrix, precision=lax.Precision.HIGH)


def left_apply(cos_table, sin_table, sign, real_in, imag_in):
    if imag_in is None:
        return (mult_left(cos_table, real_in), sign * mult_left(sin_table, real_in))
    real_out = mult_left(cos_table, real_in) - sign * mult_left(sin_table, imag_in)
    imag_out = mult_left(cos_table, imag_in) + sign * mult_left(sin_table, real_in)
    return (real_out, imag_out)


def right_apply(real_in, imag_in, cos_table, sin_table, sign):
    real_out = mult_right(real_in, cos_table) - sign * mult_right(imag_in, sin_table)
    imag_out = mult_right(imag_in, cos_table) + sign * mult_right(real_in, sin_table)
    return (real_out, imag_out)


def angle_tables(rows_idx, cols_idx, points):
    product = rows_idx[:, None] * cols_idx[None, :] % points
    theta = product.astype(jnp.float32) * (2.0 * np.pi / points)
    return (jnp.cos(theta), jnp.sin(theta))


def split_bf16(values):
    high = lax.reduce_precision(values, exponent_bits=8, mantissa_bits=7)
    return high.astype(jnp.bfloat16), (values - high).astype(jnp.bfloat16)


def split_inside(values):
    spread = values * 65537.0
    high = spread - (spread - values)
    return high.astype(jnp.bfloat16), (values - high).astype(jnp.bfloat16)


def dot3(a_high, a_low, b_high, b_low):
    def product(a, b):
        return jnp.dot(a, b, preferred_element_type=jnp.float32)

    return product(a_high, b_high) + (product(a_high, b_low) + product(a_low, b_high))


def frame_kernel(
    points,
    frame_ref,
    target_ref,
    sre_ref,
    sim_ref,
    w_ref,
    lvl_ref,
    lt_ref,
    rt_ref,
    out_ref,
    fre_s,
    fim_s,
    spec_s,
    slope_s,
    acc_s,
):
    rows_n, cols_n = frame_ref.shape[1:]
    kern = sre_ref.shape[0]
    core = points - 2 * HALO
    scale = 1.0 / (points * points)
    picks = {1.0: (0, 2, 3), -1.0: (0, 4, 5), 0.0: (6, 7, 8)}

    def lmul(index, values):
        high, low = split_inside(values)
        return dot3(lt_ref[index, 0], lt_ref[index, 1], high, low)

    def rmul(values, index):
        high, low = split_inside(values)
        return dot3(high, low, rt_ref[index, 0], rt_ref[index, 1])

    def left(real_in, imag_in, sign):
        plain, plus, minus = picks[sign]
        both = lmul(plain, real_in + imag_in)
        return both - lmul(plus, imag_in), both + lmul(minus, real_in)

    def right(real_in, imag_in, sign):
        plain, plus, minus = picks[sign]
        both = rmul(real_in + imag_in, plain)
        return both - rmul(imag_in, plus), both + rmul(real_in, minus)

    frame = frame_ref[0]
    freq_re, freq_im = right(lmul(0, frame), -lmul(1, frame), -1.0)
    spec_s[0] = freq_re
    spec_s[1] = freq_im

    def forward(k, intensity):
        s_re = sre_ref[k]
        s_im = sim_ref[k]
        f_re = spec_s[0]
        f_im = spec_s[1]
        prod_re = s_re * f_re - s_im * f_im
        prod_im = s_re * f_im + s_im * f_re
        b_re, b_im = left(prod_re, prod_im, 1.0)
        g_re, g_im = right(b_re, b_im, 1.0)
        g_re = g_re * scale
        g_im = g_im * scale
        fre_s[k] = g_re
        fim_s[k] = g_im
        return intensity + w_ref[k] * (g_re * g_re + g_im * g_im)

    intensity = lax.fori_loop(0, kern, forward, jnp.zeros((rows_n, cols_n), jnp.float32))
    rows = lax.broadcasted_iota(jnp.int32, (rows_n, cols_n), 0)
    cols = lax.broadcasted_iota(jnp.int32, (rows_n, cols_n), 1)
    inside = (rows >= HALO) & (rows < HALO + core) & (cols >= HALO) & (cols < HALO + core)
    resist = 1.0 / (1.0 + jnp.exp(-(steepness * (intensity - lvl_ref[0]))))
    slope = 2.0 * (resist - target_ref[0]) * steepness * resist * (1.0 - resist)
    slope_s[...] = jnp.where(inside, slope, 0.0)
    acc_s[...] = jnp.zeros_like(acc_s)

    def backward(k, carry):
        factor = 2.0 * w_ref[k] * slope_s[...]
        b_re, b_im = left(factor * fre_s[k], factor * fim_s[k], -1.0)
        h_re, h_im = right(b_re, b_im, -1.0)
        s_re = sre_ref[k]
        s_im = sim_ref[k]
        acc_s[0] += s_re * h_re + s_im * h_im
        acc_s[1] += s_re * h_im - s_im * h_re
        return carry

    lax.fori_loop(0, kern, backward, 0)
    u_re, u_im = left(acc_s[0], acc_s[1], 0.0)
    out_ref[0] = (rmul(u_re, 6) - rmul(u_im, 7)) * scale


def shifted_order(length, points):
    order = np.full(length, -1)
    order[: points - HALO] = np.arange(HALO, points)
    order[length - HALO :] = np.arange(HALO)
    return order


def table_stack(points, rows_n, cols_n, on_rows):
    index = np.arange(points)
    theta = (np.outer(index, index) % points) * (2.0 * np.pi / points)
    cos_t, sin_t = np.cos(theta), np.sin(theta)
    combos = [cos_t, sin_t, cos_t + sin_t, sin_t - cos_t, cos_t - sin_t, -sin_t - cos_t]
    padded = [np.pad(table, ((0, rows_n - points), (0, cols_n - points))) for table in combos]
    if on_rows:
        order = shifted_order(rows_n, points)
        finals = [padded[0], padded[2], padded[3]]
        finals = [np.where((order >= 0)[:, None], table[np.maximum(order, 0)], 0.0) for table in finals]
    else:
        order = shifted_order(cols_n, points)
        finals = [padded[0], padded[1]]
        finals = [
            np.where((order >= 0)[None, :], table[:, np.maximum(order, 0)], 0.0) for table in finals
        ]
    stack = np.stack(padded + finals).astype(np.float32)
    high = stack.astype(ml_dtypes.bfloat16)
    low = (stack - high.astype(np.float32)).astype(ml_dtypes.bfloat16)
    return jnp.asarray(np.stack([high, low], axis=1))


def frame_gradients(frames, targets, spec_re, spec_im, weights, levels, tables, points):
    count, rows_n, cols_n = frames.shape
    kern = spec_re.shape[0]
    left_tables, right_tables = tables
    per_frame = pl.BlockSpec((1, rows_n, cols_n), lambda i: (i, 0, 0))
    whole_spec = pl.BlockSpec((kern, rows_n, cols_n), lambda i: (0, 0, 0))
    smem = pl.BlockSpec(memory_space=pltpu.SMEM)
    flops = count * (kern * 4 + 4) * 9 * 2 * rows_n * cols_n * cols_n
    return pl.pallas_call(
        functools.partial(frame_kernel, points),
        out_shape=jax.ShapeDtypeStruct(frames.shape, jnp.float32),
        grid=(count,),
        in_specs=[
            per_frame,
            per_frame,
            whole_spec,
            whole_spec,
            smem,
            smem,
            pl.BlockSpec(left_tables.shape, lambda i: (0, 0, 0, 0)),
            pl.BlockSpec(right_tables.shape, lambda i: (0, 0, 0, 0)),
        ],
        out_specs=per_frame,
        scratch_shapes=[
            pltpu.VMEM((kern, rows_n, cols_n), jnp.float32),
            pltpu.VMEM((kern, rows_n, cols_n), jnp.float32),
            pltpu.VMEM((2, rows_n, cols_n), jnp.float32),
            pltpu.VMEM((rows_n, cols_n), jnp.float32),
            pltpu.VMEM((2, rows_n, cols_n), jnp.float32),
        ],
        compiler_params=pltpu.CompilerParams(
            dimension_semantics=("arbitrary",), vmem_limit_bytes=48 * 1024 * 1024
        ),
        cost_estimate=pl.CostEstimate(
            flops=flops, transcendentals=count * rows_n * cols_n, bytes_accessed=8 * 1024 * 1024
        ),
    )(frames, targets, spec_re, spec_im, weights, levels, left_tables, right_tables)


def flip_bit(value, shift):
    bit = (value // shift) % 2
    return value + shift * (1 - 2 * bit)


def exchange_kernel(n_tile, n_depth, with_halo, x_ref, partner_ref, mirror_ref, *refs):
    outputs = 2 if with_halo else 1
    out_ref = refs[0]
    (
        xs,
        recv_a,
        recv_r,
        part_s,
        recv_b,
        blend_s,
        recv_c,
        send_a,
        rsem_a,
        send_r,
        rsem_r,
        send_b,
        rsem_b,
        send_c,
        rsem_c,
    ) = refs[outputs : outputs + 15]
    me_t = lax.axis_index("tile")
    me_d = lax.axis_index("depth")
    tiles_dev, core, wide = xs.shape
    width = out_ref.shape[-1]
    rows = core // n_depth
    left_t = (me_t + n_tile - 1) % n_tile
    right_t = (me_t + 1) % n_tile
    shifts = []
    shift = 1
    while shift < n_tile:
        shifts.append(shift)
        shift *= 2
    barrier = pltpu.get_barrier_semaphore()
    for step in range(1, n_depth):
        pl.semaphore_signal(
            barrier, inc=1, device_id=(me_t, (me_d + step) % n_depth), device_id_type=MESH
        )
    for shift in shifts:
        pl.semaphore_signal(
            barrier, inc=1, device_id=(flip_bit(me_t, shift), me_d), device_id_type=MESH
        )
    for neighbour in (left_t, right_t):
        for depth in range(n_depth):
            pl.semaphore_signal(barrier, inc=1, device_id=(neighbour, depth), device_id_type=MESH)
    pl.semaphore_wait(barrier, 3 * n_depth - 1 + len(shifts))

    def band(index):
        return pl.ds(pl.multiple_of(index * rows, rows), rows)

    def depth_round(source_of, dst_buf, send_sem, recv_sem):
        copies = []
        for step in range(1, n_depth):
            target = (me_d + step) % n_depth
            copy = pltpu.make_async_remote_copy(
                src_ref=source_of(target),
                dst_ref=dst_buf.at[me_d],
                send_sem=send_sem.at[step],
                recv_sem=recv_sem.at[me_d],
                device_id=(me_t, target),
                device_id_type=MESH,
            )
            copy.start()
            copies.append(copy)
        for step in range(1, n_depth):
            source = (me_d + n_depth - step) % n_depth
            pltpu.make_async_remote_copy(
                src_ref=source_of(source),
                dst_ref=dst_buf.at[source],
                send_sem=send_sem.at[step],
                recv_sem=recv_sem.at[source],
                device_id=(me_t, source),
                device_id_type=MESH,
            ).wait_recv()
        for copy in copies:
            copy.wait_send()

    height = x_ref.shape[1]
    slab = 16
    xs[...] = x_ref[:, :core, :]
    for local in range(tiles_dev):
        if local + 1 < tiles_dev:
            xs[local, core - slab :, :] += x_ref[local + 1, height - slab :, :]
        if local > 0:
            xs[local, :slab, :] += x_ref[local - 1, core : core + slab, :]

    rims = []
    for side, neighbour in enumerate((left_t, right_t)):
        for depth in range(n_depth):
            copy = pltpu.make_async_remote_copy(
                src_ref=xs.at[:, pl.ds(depth * rows, rows), pl.ds(width, wide - width)],
                dst_ref=recv_r.at[side, me_d],
                send_sem=send_r.at[side, depth],
                recv_sem=rsem_r.at[side, me_d],
                device_id=(neighbour, depth),
                device_id_type=MESH,
            )
            copy.start()
            rims.append(copy)
    recv_a[me_d] = xs[:, band(me_d), :width]
    depth_round(lambda target: xs.at[:, band(target), pl.ds(0, width)], recv_a, send_a, rsem_a)
    for side, neighbour in enumerate((left_t, right_t)):
        for depth in range(n_depth):
            pltpu.make_async_remote_copy(
                src_ref=xs.at[:, pl.ds(depth * rows, rows), pl.ds(width, wide - width)],
                dst_ref=recv_r.at[side, depth],
                send_sem=send_r.at[side, depth],
                recv_sem=rsem_r.at[side, depth],
                device_id=(neighbour, depth),
                device_id_type=MESH,
            ).wait_recv()
    for copy in rims:
        copy.wait_send()
    total = recv_a[0]
    from_right = recv_r[0, 0]
    from_left = recv_r[1, 0]
    for slot in range(1, n_depth):
        total = total + recv_a[slot]
        from_right = from_right + recv_r[0, slot]
        from_left = from_left + recv_r[1, slot]
    lanes = lax.broadcasted_iota(jnp.int32, (tiles_dev, rows, width), 2)
    has_left = jnp.where(me_t > 0, 1.0, 0.0)
    has_right = jnp.where(me_t < n_tile - 1, 1.0, 0.0)
    from_left = jnp.where(lanes < HALO, from_left, 0.0) * has_left
    from_right = jnp.where(lanes >= width - HALO, from_right, 0.0) * has_right
    part_s[...] = total + (from_left + from_right)

    swaps = []
    for slot, shift in enumerate(shifts):
        copy = pltpu.make_async_remote_copy(
            src_ref=part_s,
            dst_ref=recv_b.at[slot],
            send_sem=send_b.at[slot],
            recv_sem=rsem_b.at[slot],
            device_id=(flip_bit(me_t, shift), me_d),
            device_id_type=MESH,
        )
        copy.start()
        swaps.append(copy)
    for copy in swaps:
        copy.wait_recv()
    for copy in swaps:
        copy.wait_send()

    lane_a = lax.broadcasted_iota(jnp.int32, (width, width), 0)
    lane_b = lax.broadcasted_iota(jnp.int32, (width, width), 1)
    reverse = jnp.where(lane_a + lane_b == width - 1, 1.0, 0.0).astype(jnp.float32)
    for local in range(tiles_dev):
        partner = partner_ref[local]
        chosen = jnp.zeros((rows, width), jnp.float32)
        for other in range(tiles_dev):
            hit = jnp.where(partner == me_t * tiles_dev + other, 1.0, 0.0)
            chosen = chosen + hit * part_s[other]
        for slot, shift in enumerate(shifts):
            source = flip_bit(me_t, shift)
            for other in range(tiles_dev):
                hit = jnp.where(partner == source * tiles_dev + other, 1.0, 0.0)
                chosen = chosen + hit * recv_b[slot, other]
        mirrored = jnp.dot(
            chosen, reverse, precision=lax.Precision.HIGHEST, preferred_element_type=jnp.float32
        )
        use_mirror = jnp.where(mirror_ref[local] == 1, 1.0, 0.0)
        chosen = use_mirror * mirrored + (1.0 - use_mirror) * chosen
        blend_s[local] = 0.5 * (part_s[local] + chosen)

    recv_c[me_d] = blend_s[...]
    halo_copies = []
    if with_halo:
        nb_ref = refs[1]
        recv_n, send_n, rsem_n = refs[outputs + 15 :]
        for side, neighbour in enumerate((left_t, right_t)):
            for depth in range(n_depth):
                copy = pltpu.make_async_remote_copy(
                    src_ref=blend_s,
                    dst_ref=recv_n.at[side, me_d],
                    send_sem=send_n.at[side, depth],
                    recv_sem=rsem_n.at[side, me_d],
                    device_id=(neighbour, depth),
                    device_id_type=MESH,
                )
                copy.start()
                halo_copies.append(copy)
    depth_round(lambda target: blend_s, recv_c, send_c, rsem_c)
    if with_halo:
        for side, neighbour in enumerate((left_t, right_t)):
            for depth in range(n_depth):
                pltpu.make_async_remote_copy(
                    src_ref=blend_s,
                    dst_ref=recv_n.at[side, depth],
                    send_sem=send_n.at[side, depth],
                    recv_sem=rsem_n.at[side, depth],
                    device_id=(neighbour, depth),
                    device_id_type=MESH,
                ).wait_recv()
        for copy in halo_copies:
            copy.wait_send()
    for slot in range(n_depth):
        out_ref[:, slot * rows : (slot + 1) * rows, :] = recv_c[slot]
        if with_halo:
            for side in range(2):
                nb_ref[side, :, slot * rows : (slot + 1) * rows, :] = recv_n[side, slot]


def exchange(values, core, partner_local, mirror_local, call_id, with_halo):
    n_tile = lax.axis_size("tile")
    n_depth = lax.axis_size("depth")
    n_shift = max(n_tile - 1, 1).bit_length()
    tiles_dev, unused_height, wide = values.shape
    width = core
    piece = (tiles_dev, core // n_depth, width)
    vmem = pl.BlockSpec(memory_space=pltpu.VMEM)
    out_shape = jax.ShapeDtypeStruct((tiles_dev, core, width), jnp.float32)
    out_specs = vmem
    extra_first, extra_last = [], []
    if with_halo:
        out_shape = (out_shape, jax.ShapeDtypeStruct((2, tiles_dev, core, width), jnp.float32))
        out_specs = (vmem, vmem)
        extra_last = [
            pltpu.VMEM((2, n_depth) + piece, jnp.float32),
            pltpu.SemaphoreType.DMA((2, n_depth)),
            pltpu.SemaphoreType.DMA((2, n_depth)),
        ]
    smem = pl.BlockSpec(memory_space=pltpu.SMEM)
    return pl.pallas_call(
        functools.partial(exchange_kernel, n_tile, n_depth, with_halo),
        out_shape=out_shape,
        in_specs=[vmem, smem, smem],
        out_specs=out_specs,
        scratch_shapes=extra_first + [
            pltpu.VMEM((tiles_dev, core, wide), jnp.float32),
            pltpu.VMEM((n_depth,) + piece, jnp.float32),
            pltpu.VMEM((2, n_depth) + piece, jnp.float32),
            pltpu.VMEM(piece, jnp.float32),
            pltpu.VMEM((n_shift,) + piece, jnp.float32),
            pltpu.VMEM(piece, jnp.float32),
            pltpu.VMEM((n_depth,) + piece, jnp.float32),
            pltpu.SemaphoreType.DMA((n_depth,)),
            pltpu.SemaphoreType.DMA((n_depth,)),
            pltpu.SemaphoreType.DMA((2, n_depth)),
            pltpu.SemaphoreType.DMA((2, n_depth)),
            pltpu.SemaphoreType.DMA((n_shift,)),
            pltpu.SemaphoreType.DMA((n_shift,)),
            pltpu.SemaphoreType.DMA((n_depth,)),
            pltpu.SemaphoreType.DMA((n_depth,)),
        ]
        + extra_last,
        compiler_params=pltpu.CompilerParams(collective_id=call_id, has_side_effects=True),
    )(values, partner_local, mirror_local)


def per_device(
    mask_tiles, target_tiles, kernels, socs_weights, thresholds, partner_table, mirror_flags
):
    tiles_dev, core, unused_width = mask_tiles.shape
    points = FRAME
    theta = (np.outer(np.arange(points), np.arange(KSIZE) - HALO) % points) * (2.0 * np.pi / points)
    cos_small = jnp.asarray(np.cos(theta).astype(np.float32))
    sin_small = jnp.asarray(np.sin(theta).astype(np.float32))
    spec_re, spec_im = left_apply(cos_small, sin_small, -1.0, kernels[0], kernels[1])
    spec_re, spec_im = right_apply(spec_re, spec_im, cos_small.T, sin_small.T, -1.0)
    target_f = target_tiles.astype(jnp.float32)
    rows_n = -(-points // 16) * 16
    cols_n = -(-points // 128) * 128
    row_fill = rows_n - points
    col_fill = cols_n - points
    targets = jnp.pad(
        target_f, ((0, 0), (HALO, rows_n - HALO - core), (HALO, cols_n - HALO - core))
    )
    spec_re_p = jnp.pad(spec_re[0], ((0, 0), (0, row_fill), (0, col_fill)))
    spec_im_p = jnp.pad(spec_im[0], ((0, 0), (0, row_fill), (0, col_fill)))
    tables = (
        table_stack(points, rows_n, rows_n, True),
        table_stack(points, cols_n, cols_n, False),
    )
    strip_height = tiles_dev * core
    step_gradient = jnp.zeros_like(mask_tiles)
    me_t = lax.axis_index("tile")
    n_tile = lax.axis_size("tile")
    halo_left = halo_right = None
    for step_index in range(STEPS):
        strip_rows = mask_tiles.reshape(strip_height, core)
        if halo_left is None:
            extended = extended_2(strip_rows, (("tile", 1),), HALO)
            halo_left = extended[:, :HALO]
            halo_right = extended[:, HALO + core :]
        else:
            extended = jnp.concatenate([halo_left, strip_rows, halo_right], axis=1)
        padded = jnp.pad(extended, ((HALO, HALO), (0, 0)))
        frames = jnp.stack(
            [padded[row_index * core : row_index * core + points] for row_index in range(tiles_dev)]
        )
        frames = jnp.pad(frames, ((0, 0), (0, row_fill), (0, col_fill)))
        grads = frame_gradients(
            frames, targets, spec_re_p, spec_im_p, socs_weights[0], thresholds, tables, points
        )
        with_halo = step_index + 1 < STEPS
        result = exchange(grads, core, partner_table, mirror_flags, step_index, with_halo)
        if with_halo:
            step_gradient, beside = result
            from_right = beside[0].reshape(strip_height, core)[:, :HALO]
            from_left = beside[1].reshape(strip_height, core)[:, core - HALO :]
            halo_left = jnp.where(me_t > 0, halo_left - step_rate * from_left, 0.0)
            halo_right = jnp.where(me_t < n_tile - 1, halo_right - step_rate * from_right, 0.0)
        else:
            step_gradient = result
        mask_tiles = mask_tiles - step_rate * step_gradient
    return (mask_tiles, step_gradient)


def solution(mesh):
    return jax.shard_map(
        per_device,
        mesh=mesh,
        in_specs=(
            P("tile", None, None),
            P("tile", None, None),
            P(None, "depth", None, None, None),
            P("depth", None),
            P("depth"),
            P("tile"),
            P("tile"),
        ),
        out_specs=(P("tile", None, None), P("tile", None, None)),
        check_vma=False,
    )
```

```python
import functools

import jax
import jax.numpy as jnp
import ml_dtypes
import numpy as np
from jax import lax
from jax.experimental import pallas as pl
from jax.experimental.pallas import tpu as pltpu
from jax.sharding import PartitionSpec as P

MESH = pl.DeviceIdType.MESH

HALO = 12
FRAME = 152
KSIZE = 25
STEPS = 2


steepness = 3.0
step_rate = 0.05


def extended_2(cells, sides, width):
    for axis, dim in sides:
        count = lax.axis_size(axis)
        ends = count - 1
        head = lax.slice_in_dim(cells, 0, width, axis=dim)
        tail = lax.slice_in_dim(cells, cells.shape[dim] - width, cells.shape[dim], axis=dim)
        cells = jnp.concatenate(
            [
                lax.ppermute(tail, axis, [(i, (i + 1) % count) for i in range(ends)]),
                cells,
                lax.ppermute(head, axis, [((i + 1) % count, i) for i in range(ends)]),
            ],
            axis=dim,
        )
    return cells


def mult_left(matrix, values):
    return jnp.einsum("jk,...kl->...jl", matrix, values, precision=lax.Precision.HIGH)


def mult_right(values, matrix):
    return jnp.einsum("...jk,kl->...jl", values, matrix, precision=lax.Precision.HIGH)


def left_apply(cos_table, sin_table, sign, real_in, imag_in):
    if imag_in is None:
        return (mult_left(cos_table, real_in), sign * mult_left(sin_table, real_in))
    real_out = mult_left(cos_table, real_in) - sign * mult_left(sin_table, imag_in)
    imag_out = mult_left(cos_table, imag_in) + sign * mult_left(sin_table, real_in)
    return (real_out, imag_out)


def right_apply(real_in, imag_in, cos_table, sin_table, sign):
    real_out = mult_right(real_in, cos_table) - sign * mult_right(imag_in, sin_table)
    imag_out = mult_right(imag_in, cos_table) + sign * mult_right(real_in, sin_table)
    return (real_out, imag_out)


def angle_tables(rows_idx, cols_idx, points):
    product = rows_idx[:, None] * cols_idx[None, :] % points
    theta = product.astype(jnp.float32) * (2.0 * np.pi / points)
    return (jnp.cos(theta), jnp.sin(theta))


def split_bf16(values):
    high = lax.reduce_precision(values, exponent_bits=8, mantissa_bits=7)
    return high.astype(jnp.bfloat16), (values - high).astype(jnp.bfloat16)


def split_inside(values):
    spread = values * 65537.0
    high = spread - (spread - values)
    return high.astype(jnp.bfloat16), (values - high).astype(jnp.bfloat16)


def dot3(a_high, a_low, b_high, b_low):
    def product(a, b):
        return jnp.dot(a, b, preferred_element_type=jnp.float32)

    return product(a_high, b_high) + (product(a_high, b_low) + product(a_low, b_high))


def frame_kernel(
    points,
    frame_ref,
    target_ref,
    sre_ref,
    sim_ref,
    w_ref,
    lvl_ref,
    lt_ref,
    rt_ref,
    out_ref,
    fre_s,
    fim_s,
    spec_s,
    slope_s,
    acc_s,
):
    rows_n, cols_n = frame_ref.shape[1:]
    kern = sre_ref.shape[0]
    core = points - 2 * HALO
    scale = 1.0 / (points * points)
    picks = {1.0: (0, 2, 3), -1.0: (0, 4, 5), 0.0: (6, 7, 8)}

    def lmul(index, values):
        high, low = split_inside(values)
        return dot3(lt_ref[index, 0], lt_ref[index, 1], high, low)

    def rmul(values, index):
        high, low = split_inside(values)
        return dot3(high, low, rt_ref[index, 0], rt_ref[index, 1])

    def left(real_in, imag_in, sign):
        plain, plus, minus = picks[sign]
        both = lmul(plain, real_in + imag_in)
        return both - lmul(plus, imag_in), both + lmul(minus, real_in)

    def right(real_in, imag_in, sign):
        plain, plus, minus = picks[sign]
        both = rmul(real_in + imag_in, plain)
        return both - rmul(imag_in, plus), both + rmul(real_in, minus)

    frame = frame_ref[0]
    freq_re, freq_im = right(lmul(0, frame), -lmul(1, frame), -1.0)
    spec_s[0] = freq_re
    spec_s[1] = freq_im

    def forward(k, intensity):
        s_re = sre_ref[k]
        s_im = sim_ref[k]
        f_re = spec_s[0]
        f_im = spec_s[1]
        prod_re = s_re * f_re - s_im * f_im
        prod_im = s_re * f_im + s_im * f_re
        b_re, b_im = left(prod_re, prod_im, 1.0)
        g_re, g_im = right(b_re, b_im, 1.0)
        g_re = g_re * scale
        g_im = g_im * scale
        fre_s[k] = g_re
        fim_s[k] = g_im
        return intensity + w_ref[k] * (g_re * g_re + g_im * g_im)

    intensity = lax.fori_loop(0, kern, forward, jnp.zeros((rows_n, cols_n), jnp.float32))
    rows = lax.broadcasted_iota(jnp.int32, (rows_n, cols_n), 0)
    cols = lax.broadcasted_iota(jnp.int32, (rows_n, cols_n), 1)
    inside = (rows >= HALO) & (rows < HALO + core) & (cols >= HALO) & (cols < HALO + core)
    resist = 1.0 / (1.0 + jnp.exp(-(steepness * (intensity - lvl_ref[0]))))
    slope = 2.0 * (resist - target_ref[0]) * steepness * resist * (1.0 - resist)
    slope_s[...] = jnp.where(inside, slope, 0.0)
    acc_s[...] = jnp.zeros_like(acc_s)

    def backward(k, carry):
        factor = 2.0 * w_ref[k] * slope_s[...]
        b_re, b_im = left(factor * fre_s[k], factor * fim_s[k], -1.0)
        h_re, h_im = right(b_re, b_im, -1.0)
        s_re = sre_ref[k]
        s_im = sim_ref[k]
        acc_s[0] += s_re * h_re + s_im * h_im
        acc_s[1] += s_re * h_im - s_im * h_re
        return carry

    lax.fori_loop(0, kern, backward, 0)
    u_re, u_im = left(acc_s[0], acc_s[1], 0.0)
    out_ref[0] = (rmul(u_re, 6) - rmul(u_im, 7)) * scale


def shifted_order(length, points):
    order = np.full(length, -1)
    order[: points - HALO] = np.arange(HALO, points)
    order[length - HALO :] = np.arange(HALO)
    return order


def table_stack(points, rows_n, cols_n, on_rows):
    index = np.arange(points)
    theta = (np.outer(index, index) % points) * (2.0 * np.pi / points)
    cos_t, sin_t = np.cos(theta), np.sin(theta)
    combos = [cos_t, sin_t, cos_t + sin_t, sin_t - cos_t, cos_t - sin_t, -sin_t - cos_t]
    padded = [np.pad(table, ((0, rows_n - points), (0, cols_n - points))) for table in combos]
    if on_rows:
        order = shifted_order(rows_n, points)
        finals = [padded[0], padded[2], padded[3]]
        finals = [np.where((order >= 0)[:, None], table[np.maximum(order, 0)], 0.0) for table in finals]
    else:
        order = shifted_order(cols_n, points)
        finals = [padded[0], padded[1]]
        finals = [
            np.where((order >= 0)[None, :], table[:, np.maximum(order, 0)], 0.0) for table in finals
        ]
    stack = np.stack(padded + finals).astype(np.float32)
    high = stack.astype(ml_dtypes.bfloat16)
    low = (stack - high.astype(np.float32)).astype(ml_dtypes.bfloat16)
    return jnp.asarray(np.stack([high, low], axis=1))


def frame_gradients(frames, targets, spec_re, spec_im, weights, levels, tables, points):
    count, rows_n, cols_n = frames.shape
    kern = spec_re.shape[0]
    left_tables, right_tables = tables
    per_frame = pl.BlockSpec((1, rows_n, cols_n), lambda i: (i, 0, 0))
    whole_spec = pl.BlockSpec((kern, rows_n, cols_n), lambda i: (0, 0, 0))
    smem = pl.BlockSpec(memory_space=pltpu.SMEM)
    flops = count * (kern * 4 + 4) * 9 * 2 * rows_n * cols_n * cols_n
    return pl.pallas_call(
        functools.partial(frame_kernel, points),
        out_shape=jax.ShapeDtypeStruct(frames.shape, jnp.float32),
        grid=(count,),
        in_specs=[
            per_frame,
            per_frame,
            whole_spec,
            whole_spec,
            smem,
            smem,
            pl.BlockSpec(left_tables.shape, lambda i: (0, 0, 0, 0)),
            pl.BlockSpec(right_tables.shape, lambda i: (0, 0, 0, 0)),
        ],
        out_specs=per_frame,
        scratch_shapes=[
            pltpu.VMEM((kern, rows_n, cols_n), jnp.float32),
            pltpu.VMEM((kern, rows_n, cols_n), jnp.float32),
            pltpu.VMEM((2, rows_n, cols_n), jnp.float32),
            pltpu.VMEM((rows_n, cols_n), jnp.float32),
            pltpu.VMEM((2, rows_n, cols_n), jnp.float32),
        ],
        compiler_params=pltpu.CompilerParams(
            dimension_semantics=("arbitrary",), vmem_limit_bytes=48 * 1024 * 1024
        ),
        cost_estimate=pl.CostEstimate(
            flops=flops, transcendentals=count * rows_n * cols_n, bytes_accessed=8 * 1024 * 1024
        ),
    )(frames, targets, spec_re, spec_im, weights, levels, left_tables, right_tables)


def flip_bit(value, shift):
    bit = (value // shift) % 2
    return value + shift * (1 - 2 * bit)


def exchange_kernel(n_tile, n_depth, with_halo, x_ref, partner_ref, mirror_ref, *refs):
    outputs = 2 if with_halo else 1
    out_ref = refs[0]
    (
        xs,
        recv_a,
        recv_r,
        part_s,
        recv_b,
        blend_s,
        recv_c,
        send_a,
        rsem_a,
        send_r,
        rsem_r,
        send_b,
        rsem_b,
        send_c,
        rsem_c,
    ) = refs[outputs : outputs + 15]
    me_t = lax.axis_index("tile")
    me_d = lax.axis_index("depth")
    tiles_dev, core, wide = xs.shape
    width = out_ref.shape[-1]
    rows = core // n_depth
    left_t = (me_t + n_tile - 1) % n_tile
    right_t = (me_t + 1) % n_tile
    shifts = []
    shift = 1
    while shift < n_tile:
        shifts.append(shift)
        shift *= 2
    barrier = pltpu.get_barrier_semaphore()
    for step in range(1, n_depth):
        pl.semaphore_signal(
            barrier, inc=1, device_id=(me_t, (me_d + step) % n_depth), device_id_type=MESH
        )
    for shift in shifts:
        pl.semaphore_signal(
            barrier, inc=1, device_id=(flip_bit(me_t, shift), me_d), device_id_type=MESH
        )
    for neighbour in (left_t, right_t):
        for depth in range(n_depth):
            pl.semaphore_signal(barrier, inc=1, device_id=(neighbour, depth), device_id_type=MESH)
    pl.semaphore_wait(barrier, 3 * n_depth - 1 + len(shifts))

    def band(index):
        return pl.ds(pl.multiple_of(index * rows, rows), rows)

    def depth_round(source_of, dst_buf, send_sem, recv_sem):
        copies = []
        for step in range(1, n_depth):
            target = (me_d + step) % n_depth
            copy = pltpu.make_async_remote_copy(
                src_ref=source_of(target),
                dst_ref=dst_buf.at[me_d],
                send_sem=send_sem.at[step],
                recv_sem=recv_sem.at[me_d],
                device_id=(me_t, target),
                device_id_type=MESH,
            )
            copy.start()
            copies.append(copy)
        for step in range(1, n_depth):
            source = (me_d + n_depth - step) % n_depth
            pltpu.make_async_remote_copy(
                src_ref=source_of(source),
                dst_ref=dst_buf.at[source],
                send_sem=send_sem.at[step],
                recv_sem=recv_sem.at[source],
                device_id=(me_t, source),
                device_id_type=MESH,
            ).wait_recv()
        for copy in copies:
            copy.wait_send()

    height = x_ref.shape[1]
    slab = 16
    xs[...] = x_ref[:, :core, :]
    for local in range(tiles_dev):
        if local + 1 < tiles_dev:
            xs[local, core - slab :, :] += x_ref[local + 1, height - slab :, :]
        if local > 0:
            xs[local, :slab, :] += x_ref[local - 1, core : core + slab, :]

    rims = []
    for side, neighbour in enumerate((left_t, right_t)):
        for depth in range(n_depth):
            copy = pltpu.make_async_remote_copy(
                src_ref=xs.at[:, pl.ds(depth * rows, rows), pl.ds(width, wide - width)],
                dst_ref=recv_r.at[side, me_d],
                send_sem=send_r.at[side, depth],
                recv_sem=rsem_r.at[side, me_d],
                device_id=(neighbour, depth),
                device_id_type=MESH,
            )
            copy.start()
            rims.append(copy)
    recv_a[me_d] = xs[:, band(me_d), :width]
    depth_round(lambda target: xs.at[:, band(target), pl.ds(0, width)], recv_a, send_a, rsem_a)
    for side, neighbour in enumerate((left_t, right_t)):
        for depth in range(n_depth):
            pltpu.make_async_remote_copy(
                src_ref=xs.at[:, pl.ds(depth * rows, rows), pl.ds(width, wide - width)],
                dst_ref=recv_r.at[side, depth],
                send_sem=send_r.at[side, depth],
                recv_sem=rsem_r.at[side, depth],
                device_id=(neighbour, depth),
                device_id_type=MESH,
            ).wait_recv()
    for copy in rims:
        copy.wait_send()
    total = recv_a[0]
    from_right = recv_r[0, 0]
    from_left = recv_r[1, 0]
    for slot in range(1, n_depth):
        total = total + recv_a[slot]
        from_right = from_right + recv_r[0, slot]
        from_left = from_left + recv_r[1, slot]
    lanes = lax.broadcasted_iota(jnp.int32, (tiles_dev, rows, width), 2)
    has_left = jnp.where(me_t > 0, 1.0, 0.0)
    has_right = jnp.where(me_t < n_tile - 1, 1.0, 0.0)
    from_left = jnp.where(lanes < HALO, from_left, 0.0) * has_left
    from_right = jnp.where(lanes >= width - HALO, from_right, 0.0) * has_right
    part_s[...] = total + (from_left + from_right)

    swaps = []
    for slot, shift in enumerate(shifts):
        copy = pltpu.make_async_remote_copy(
            src_ref=part_s,
            dst_ref=recv_b.at[slot],
            send_sem=send_b.at[slot],
            recv_sem=rsem_b.at[slot],
            device_id=(flip_bit(me_t, shift), me_d),
            device_id_type=MESH,
        )
        copy.start()
        swaps.append(copy)
    for copy in swaps:
        copy.wait_recv()
    for copy in swaps:
        copy.wait_send()

    lane_a = lax.broadcasted_iota(jnp.int32, (width, width), 0)
    lane_b = lax.broadcasted_iota(jnp.int32, (width, width), 1)
    reverse = jnp.where(lane_a + lane_b == width - 1, 1.0, 0.0).astype(jnp.float32)
    for local in range(tiles_dev):
        partner = partner_ref[local]
        chosen = jnp.zeros((rows, width), jnp.float32)
        for other in range(tiles_dev):
            hit = jnp.where(partner == me_t * tiles_dev + other, 1.0, 0.0)
            chosen = chosen + hit * part_s[other]
        for slot, shift in enumerate(shifts):
            source = flip_bit(me_t, shift)
            for other in range(tiles_dev):
                hit = jnp.where(partner == source * tiles_dev + other, 1.0, 0.0)
                chosen = chosen + hit * recv_b[slot, other]
        mirrored = jnp.dot(
            chosen, reverse, precision=lax.Precision.HIGHEST, preferred_element_type=jnp.float32
        )
        use_mirror = jnp.where(mirror_ref[local] == 1, 1.0, 0.0)
        chosen = use_mirror * mirrored + (1.0 - use_mirror) * chosen
        blend_s[local] = 0.5 * (part_s[local] + chosen)

    recv_c[me_d] = blend_s[...]
    halo_copies = []
    if with_halo:
        nb_ref = refs[1]
        recv_n, send_n, rsem_n = refs[outputs + 15 :]
        for side, neighbour in enumerate((left_t, right_t)):
            for depth in range(n_depth):
                copy = pltpu.make_async_remote_copy(
                    src_ref=blend_s,
                    dst_ref=recv_n.at[side, me_d],
                    send_sem=send_n.at[side, depth],
                    recv_sem=rsem_n.at[side, me_d],
                    device_id=(neighbour, depth),
                    device_id_type=MESH,
                )
                copy.start()
                halo_copies.append(copy)
    depth_round(lambda target: blend_s, recv_c, send_c, rsem_c)
    if with_halo:
        for side, neighbour in enumerate((left_t, right_t)):
            for depth in range(n_depth):
                pltpu.make_async_remote_copy(
                    src_ref=blend_s,
                    dst_ref=recv_n.at[side, depth],
                    send_sem=send_n.at[side, depth],
                    recv_sem=rsem_n.at[side, depth],
                    device_id=(neighbour, depth),
                    device_id_type=MESH,
                ).wait_recv()
        for copy in halo_copies:
            copy.wait_send()
    for slot in range(n_depth):
        out_ref[:, slot * rows : (slot + 1) * rows, :] = recv_c[slot]
        if with_halo:
            for side in range(2):
                nb_ref[side, :, slot * rows : (slot + 1) * rows, :] = recv_n[side, slot]


def exchange(values, core, partner_local, mirror_local, call_id, with_halo):
    n_tile = lax.axis_size("tile")
    n_depth = lax.axis_size("depth")
    n_shift = max(n_tile - 1, 1).bit_length()
    tiles_dev, unused_height, wide = values.shape
    width = core
    piece = (tiles_dev, core // n_depth, width)
    vmem = pl.BlockSpec(memory_space=pltpu.VMEM)
    out_shape = jax.ShapeDtypeStruct((tiles_dev, core, width), jnp.float32)
    out_specs = vmem
    extra_first, extra_last = [], []
    if with_halo:
        out_shape = (out_shape, jax.ShapeDtypeStruct((2, tiles_dev, core, width), jnp.float32))
        out_specs = (vmem, vmem)
        extra_last = [
            pltpu.VMEM((2, n_depth) + piece, jnp.float32),
            pltpu.SemaphoreType.DMA((2, n_depth)),
            pltpu.SemaphoreType.DMA((2, n_depth)),
        ]
    smem = pl.BlockSpec(memory_space=pltpu.SMEM)
    return pl.pallas_call(
        functools.partial(exchange_kernel, n_tile, n_depth, with_halo),
        out_shape=out_shape,
        in_specs=[vmem, smem, smem],
        out_specs=out_specs,
        scratch_shapes=extra_first + [
            pltpu.VMEM((tiles_dev, core, wide), jnp.float32),
            pltpu.VMEM((n_depth,) + piece, jnp.float32),
            pltpu.VMEM((2, n_depth) + piece, jnp.float32),
            pltpu.VMEM(piece, jnp.float32),
            pltpu.VMEM((n_shift,) + piece, jnp.float32),
            pltpu.VMEM(piece, jnp.float32),
            pltpu.VMEM((n_depth,) + piece, jnp.float32),
            pltpu.SemaphoreType.DMA((n_depth,)),
            pltpu.SemaphoreType.DMA((n_depth,)),
            pltpu.SemaphoreType.DMA((2, n_depth)),
            pltpu.SemaphoreType.DMA((2, n_depth)),
            pltpu.SemaphoreType.DMA((n_shift,)),
            pltpu.SemaphoreType.DMA((n_shift,)),
            pltpu.SemaphoreType.DMA((n_depth,)),
            pltpu.SemaphoreType.DMA((n_depth,)),
        ]
        + extra_last,
        compiler_params=pltpu.CompilerParams(collective_id=call_id, has_side_effects=True),
    )(values, partner_local, mirror_local)


def final_update_kernel(mask_ref, grad_ref, mask_out, grad_out):
    grad = grad_ref[...]
    mask_out[...] = mask_ref[...] - step_rate * grad
    grad_out[...] = grad


def final_update(mask_tiles, step_gradient):
    vmem = pl.BlockSpec(memory_space=pltpu.VMEM)
    shape = jax.ShapeDtypeStruct(mask_tiles.shape, jnp.float32)
    return pl.pallas_call(
        final_update_kernel,
        out_shape=(shape, shape),
        in_specs=[vmem, vmem],
        out_specs=(vmem, vmem),
    )(mask_tiles, step_gradient)


def per_device(
    mask_tiles, target_tiles, kernels, socs_weights, thresholds, partner_table, mirror_flags
):
    tiles_dev, core, unused_width = mask_tiles.shape
    points = FRAME
    index_full = jnp.arange(points, dtype=jnp.int32)
    cos_table, sin_table = angle_tables(index_full, index_full, points)
    offsets = jnp.arange(KSIZE, dtype=jnp.int32) - HALO
    cos_small, sin_small = angle_tables(index_full, offsets, points)
    spec_re, spec_im = left_apply(cos_small, sin_small, -1.0, kernels[0], kernels[1])
    spec_re, spec_im = right_apply(spec_re, spec_im, cos_small.T, sin_small.T, -1.0)
    target_f = target_tiles.astype(jnp.float32)
    rows_n = -(-points // 16) * 16
    cols_n = -(-points // 128) * 128
    row_fill = rows_n - points
    col_fill = cols_n - points
    targets = jnp.pad(
        target_f, ((0, 0), (HALO, rows_n - HALO - core), (HALO, cols_n - HALO - core))
    )
    spec_re_p = jnp.pad(spec_re[0], ((0, 0), (0, row_fill), (0, col_fill)))
    spec_im_p = jnp.pad(spec_im[0], ((0, 0), (0, row_fill), (0, col_fill)))
    tables = (
        table_stack(points, rows_n, rows_n, True),
        table_stack(points, cols_n, cols_n, False),
    )
    strip_height = tiles_dev * core
    step_gradient = jnp.zeros_like(mask_tiles)
    me_t = lax.axis_index("tile")
    n_tile = lax.axis_size("tile")
    halo_left = halo_right = None
    for step_index in range(STEPS):
        strip_rows = mask_tiles.reshape(strip_height, core)
        if halo_left is None:
            extended = extended_2(strip_rows, (("tile", 1),), HALO)
            halo_left = extended[:, :HALO]
            halo_right = extended[:, HALO + core :]
        else:
            extended = jnp.concatenate([halo_left, strip_rows, halo_right], axis=1)
        padded = jnp.pad(extended, ((HALO, HALO), (0, 0)))
        frames = jnp.stack(
            [padded[row_index * core : row_index * core + points] for row_index in range(tiles_dev)]
        )
        frames = jnp.pad(frames, ((0, 0), (0, row_fill), (0, col_fill)))
        grads = frame_gradients(
            frames, targets, spec_re_p, spec_im_p, socs_weights[0], thresholds, tables, points
        )
        with_halo = step_index + 1 < STEPS
        result = exchange(grads, core, partner_table, mirror_flags, step_index, with_halo)
        if with_halo:
            step_gradient, beside = result
            from_right = beside[0].reshape(strip_height, core)[:, :HALO]
            from_left = beside[1].reshape(strip_height, core)[:, core - HALO :]
            halo_left = jnp.where(me_t > 0, halo_left - step_rate * from_left, 0.0)
            halo_right = jnp.where(me_t < n_tile - 1, halo_right - step_rate * from_right, 0.0)
            mask_tiles = mask_tiles - step_rate * step_gradient
        else:
            step_gradient = result
    return final_update(mask_tiles, step_gradient)


def solution(mesh):
    return jax.shard_map(
        per_device,
        mesh=mesh,
        in_specs=(
            P("tile", None, None),
            P("tile", None, None),
            P(None, "depth", None, None, None),
            P("depth", None),
            P("depth"),
            P("tile"),
            P("tile"),
        ),
        out_specs=(P("tile", None, None), P("tile", None, None)),
        check_vma=False,
    )
```

```python
import functools

import jax
import jax.numpy as jnp
import ml_dtypes
import numpy as np
from jax import lax
from jax.experimental import pallas as pl
from jax.experimental.pallas import tpu as pltpu
from jax.sharding import PartitionSpec as P

MESH = pl.DeviceIdType.MESH

HALO = 12
FRAME = 152
KSIZE = 25
STEPS = 2


steepness = 3.0
step_rate = 0.05


def extended_2(cells, sides, width):
    for axis, dim in sides:
        count = lax.axis_size(axis)
        ends = count - 1
        head = lax.slice_in_dim(cells, 0, width, axis=dim)
        tail = lax.slice_in_dim(cells, cells.shape[dim] - width, cells.shape[dim], axis=dim)
        cells = jnp.concatenate(
            [
                lax.ppermute(tail, axis, [(i, (i + 1) % count) for i in range(ends)]),
                cells,
                lax.ppermute(head, axis, [((i + 1) % count, i) for i in range(ends)]),
            ],
            axis=dim,
        )
    return cells


def mult_left(matrix, values):
    return jnp.einsum("jk,...kl->...jl", matrix, values, precision=lax.Precision.HIGH)


def mult_right(values, matrix):
    return jnp.einsum("...jk,kl->...jl", values, matrix, precision=lax.Precision.HIGH)


def left_apply(cos_table, sin_table, sign, real_in, imag_in):
    if imag_in is None:
        return (mult_left(cos_table, real_in), sign * mult_left(sin_table, real_in))
    real_out = mult_left(cos_table, real_in) - sign * mult_left(sin_table, imag_in)
    imag_out = mult_left(cos_table, imag_in) + sign * mult_left(sin_table, real_in)
    return (real_out, imag_out)


def right_apply(real_in, imag_in, cos_table, sin_table, sign):
    real_out = mult_right(real_in, cos_table) - sign * mult_right(imag_in, sin_table)
    imag_out = mult_right(imag_in, cos_table) + sign * mult_right(real_in, sin_table)
    return (real_out, imag_out)


def angle_tables(rows_idx, cols_idx, points):
    product = rows_idx[:, None] * cols_idx[None, :] % points
    theta = product.astype(jnp.float32) * (2.0 * np.pi / points)
    return (jnp.cos(theta), jnp.sin(theta))


def split_bf16(values):
    high = lax.reduce_precision(values, exponent_bits=8, mantissa_bits=7)
    return high.astype(jnp.bfloat16), (values - high).astype(jnp.bfloat16)


def split_inside(values):
    spread = values * 65537.0
    high = spread - (spread - values)
    return high.astype(jnp.bfloat16), (values - high).astype(jnp.bfloat16)


def dot3(a_high, a_low, b_high, b_low):
    def product(a, b):
        return jnp.dot(a, b, preferred_element_type=jnp.float32)

    return product(a_high, b_high) + (product(a_high, b_low) + product(a_low, b_high))


def frame_kernel(
    points,
    frame_ref,
    target_ref,
    sre_ref,
    sim_ref,
    w_ref,
    lvl_ref,
    lt_ref,
    rt_ref,
    out_ref,
    fre_s,
    fim_s,
    spec_s,
    slope_s,
    acc_s,
):
    rows_n, cols_n = frame_ref.shape[1:]
    kern = sre_ref.shape[0]
    core = points - 2 * HALO
    scale = 1.0 / (points * points)
    picks = {1.0: (0, 2, 3), -1.0: (0, 4, 5), 0.0: (6, 7, 8)}

    def lmul(index, values):
        high, low = split_inside(values)
        return dot3(lt_ref[index, 0], lt_ref[index, 1], high, low)

    def rmul(values, index):
        high, low = split_inside(values)
        return dot3(high, low, rt_ref[index, 0], rt_ref[index, 1])

    def left(real_in, imag_in, sign):
        plain, plus, minus = picks[sign]
        both = lmul(plain, real_in + imag_in)
        return both - lmul(plus, imag_in), both + lmul(minus, real_in)

    def right(real_in, imag_in, sign):
        plain, plus, minus = picks[sign]
        both = rmul(real_in + imag_in, plain)
        return both - rmul(imag_in, plus), both + rmul(real_in, minus)

    frame = frame_ref[0]
    freq_re, freq_im = right(lmul(0, frame), -lmul(1, frame), -1.0)
    spec_s[0] = freq_re
    spec_s[1] = freq_im

    def forward(k, intensity):
        s_re = sre_ref[k]
        s_im = sim_ref[k]
        f_re = spec_s[0]
        f_im = spec_s[1]
        prod_re = s_re * f_re - s_im * f_im
        prod_im = s_re * f_im + s_im * f_re
        b_re, b_im = left(prod_re, prod_im, 1.0)
        g_re, g_im = right(b_re, b_im, 1.0)
        g_re = g_re * scale
        g_im = g_im * scale
        fre_s[k] = g_re
        fim_s[k] = g_im
        return intensity + w_ref[k] * (g_re * g_re + g_im * g_im)

    intensity = lax.fori_loop(0, kern, forward, jnp.zeros((rows_n, cols_n), jnp.float32))
    rows = lax.broadcasted_iota(jnp.int32, (rows_n, cols_n), 0)
    cols = lax.broadcasted_iota(jnp.int32, (rows_n, cols_n), 1)
    inside = (rows >= HALO) & (rows < HALO + core) & (cols >= HALO) & (cols < HALO + core)
    resist = 1.0 / (1.0 + jnp.exp(-(steepness * (intensity - lvl_ref[0]))))
    slope = 2.0 * (resist - target_ref[0]) * steepness * resist * (1.0 - resist)
    slope_s[...] = jnp.where(inside, slope, 0.0)
    acc_s[...] = jnp.zeros_like(acc_s)

    def backward(k, carry):
        factor = 2.0 * w_ref[k] * slope_s[...]
        b_re, b_im = left(factor * fre_s[k], factor * fim_s[k], -1.0)
        h_re, h_im = right(b_re, b_im, -1.0)
        s_re = sre_ref[k]
        s_im = sim_ref[k]
        acc_s[0] += s_re * h_re + s_im * h_im
        acc_s[1] += s_re * h_im - s_im * h_re
        return carry

    lax.fori_loop(0, kern, backward, 0)
    u_re, u_im = left(acc_s[0], acc_s[1], 0.0)
    out_ref[0] = (rmul(u_re, 6) - rmul(u_im, 7)) * scale


def shifted_order(length, points):
    order = np.full(length, -1)
    order[: points - HALO] = np.arange(HALO, points)
    order[length - HALO :] = np.arange(HALO)
    return order


def table_stack(points, rows_n, cols_n, on_rows):
    index = np.arange(points)
    theta = (np.outer(index, index) % points) * (2.0 * np.pi / points)
    cos_t, sin_t = np.cos(theta), np.sin(theta)
    combos = [cos_t, sin_t, cos_t + sin_t, sin_t - cos_t, cos_t - sin_t, -sin_t - cos_t]
    padded = [np.pad(table, ((0, rows_n - points), (0, cols_n - points))) for table in combos]
    if on_rows:
        order = shifted_order(rows_n, points)
        finals = [padded[0], padded[2], padded[3]]
        finals = [np.where((order >= 0)[:, None], table[np.maximum(order, 0)], 0.0) for table in finals]
    else:
        order = shifted_order(cols_n, points)
        finals = [padded[0], padded[1]]
        finals = [
            np.where((order >= 0)[None, :], table[:, np.maximum(order, 0)], 0.0) for table in finals
        ]
    stack = np.stack(padded + finals).astype(np.float32)
    high = stack.astype(ml_dtypes.bfloat16)
    low = (stack - high.astype(np.float32)).astype(ml_dtypes.bfloat16)
    return jnp.asarray(np.stack([high, low], axis=1))


def frame_gradients(frames, targets, spec_re, spec_im, weights, levels, tables, points):
    count, rows_n, cols_n = frames.shape
    kern = spec_re.shape[0]
    left_tables, right_tables = tables
    per_frame = pl.BlockSpec((1, rows_n, cols_n), lambda i: (i, 0, 0))
    whole_spec = pl.BlockSpec((kern, rows_n, cols_n), lambda i: (0, 0, 0))
    smem = pl.BlockSpec(memory_space=pltpu.SMEM)
    flops = count * (kern * 4 + 4) * 9 * 2 * rows_n * cols_n * cols_n
    return pl.pallas_call(
        functools.partial(frame_kernel, points),
        out_shape=jax.ShapeDtypeStruct(frames.shape, jnp.float32),
        grid=(count,),
        in_specs=[
            per_frame,
            per_frame,
            whole_spec,
            whole_spec,
            smem,
            smem,
            pl.BlockSpec(left_tables.shape, lambda i: (0, 0, 0, 0)),
            pl.BlockSpec(right_tables.shape, lambda i: (0, 0, 0, 0)),
        ],
        out_specs=per_frame,
        scratch_shapes=[
            pltpu.VMEM((kern, rows_n, cols_n), jnp.float32),
            pltpu.VMEM((kern, rows_n, cols_n), jnp.float32),
            pltpu.VMEM((2, rows_n, cols_n), jnp.float32),
            pltpu.VMEM((rows_n, cols_n), jnp.float32),
            pltpu.VMEM((2, rows_n, cols_n), jnp.float32),
        ],
        compiler_params=pltpu.CompilerParams(
            dimension_semantics=("arbitrary",), vmem_limit_bytes=48 * 1024 * 1024
        ),
        cost_estimate=pl.CostEstimate(
            flops=flops, transcendentals=count * rows_n * cols_n, bytes_accessed=8 * 1024 * 1024
        ),
    )(frames, targets, spec_re, spec_im, weights, levels, left_tables, right_tables)


def flip_bit(value, shift):
    bit = (value // shift) % 2
    return value + shift * (1 - 2 * bit)


def exchange_kernel(n_tile, n_depth, with_halo, x_ref, partner_ref, mirror_ref, mask_ref, *refs):
    outputs = 2 if with_halo else 1
    out_ref = refs[0]
    (
        xs,
        recv_a,
        recv_r,
        part_s,
        recv_b,
        blend_s,
        recv_c,
        send_a,
        rsem_a,
        send_r,
        rsem_r,
        send_b,
        rsem_b,
        send_c,
        rsem_c,
    ) = refs[outputs : outputs + 15]
    me_t = lax.axis_index("tile")
    me_d = lax.axis_index("depth")
    tiles_dev, core, wide = xs.shape
    width = out_ref.shape[-1]
    rows = core // n_depth
    left_t = (me_t + n_tile - 1) % n_tile
    right_t = (me_t + 1) % n_tile
    shifts = []
    shift = 1
    while shift < n_tile:
        shifts.append(shift)
        shift *= 2
    barrier = pltpu.get_barrier_semaphore()
    for step in range(1, n_depth):
        pl.semaphore_signal(
            barrier, inc=1, device_id=(me_t, (me_d + step) % n_depth), device_id_type=MESH
        )
    for shift in shifts:
        pl.semaphore_signal(
            barrier, inc=1, device_id=(flip_bit(me_t, shift), me_d), device_id_type=MESH
        )
    for neighbour in (left_t, right_t):
        for depth in range(n_depth):
            pl.semaphore_signal(barrier, inc=1, device_id=(neighbour, depth), device_id_type=MESH)
    pl.semaphore_wait(barrier, 3 * n_depth - 1 + len(shifts))

    def band(index):
        return pl.ds(pl.multiple_of(index * rows, rows), rows)

    def depth_round(source_of, dst_buf, send_sem, recv_sem):
        copies = []
        for step in range(1, n_depth):
            target = (me_d + step) % n_depth
            copy = pltpu.make_async_remote_copy(
                src_ref=source_of(target),
                dst_ref=dst_buf.at[me_d],
                send_sem=send_sem.at[step],
                recv_sem=recv_sem.at[me_d],
                device_id=(me_t, target),
                device_id_type=MESH,
            )
            copy.start()
            copies.append(copy)
        for step in range(1, n_depth):
            source = (me_d + n_depth - step) % n_depth
            pltpu.make_async_remote_copy(
                src_ref=source_of(source),
                dst_ref=dst_buf.at[source],
                send_sem=send_sem.at[step],
                recv_sem=recv_sem.at[source],
                device_id=(me_t, source),
                device_id_type=MESH,
            ).wait_recv()
        for copy in copies:
            copy.wait_send()

    height = x_ref.shape[1]
    slab = 16
    xs[...] = x_ref[:, :core, :]
    for local in range(tiles_dev):
        if local + 1 < tiles_dev:
            xs[local, core - slab :, :] += x_ref[local + 1, height - slab :, :]
        if local > 0:
            xs[local, :slab, :] += x_ref[local - 1, core : core + slab, :]

    rims = []
    for side, neighbour in enumerate((left_t, right_t)):
        for depth in range(n_depth):
            copy = pltpu.make_async_remote_copy(
                src_ref=xs.at[:, pl.ds(depth * rows, rows), pl.ds(width, wide - width)],
                dst_ref=recv_r.at[side, me_d],
                send_sem=send_r.at[side, depth],
                recv_sem=rsem_r.at[side, me_d],
                device_id=(neighbour, depth),
                device_id_type=MESH,
            )
            copy.start()
            rims.append(copy)
    recv_a[me_d] = xs[:, band(me_d), :width]
    depth_round(lambda target: xs.at[:, band(target), pl.ds(0, width)], recv_a, send_a, rsem_a)
    for side, neighbour in enumerate((left_t, right_t)):
        for depth in range(n_depth):
            pltpu.make_async_remote_copy(
                src_ref=xs.at[:, pl.ds(depth * rows, rows), pl.ds(width, wide - width)],
                dst_ref=recv_r.at[side, depth],
                send_sem=send_r.at[side, depth],
                recv_sem=rsem_r.at[side, depth],
                device_id=(neighbour, depth),
                device_id_type=MESH,
            ).wait_recv()
    for copy in rims:
        copy.wait_send()
    total = recv_a[0]
    from_right = recv_r[0, 0]
    from_left = recv_r[1, 0]
    for slot in range(1, n_depth):
        total = total + recv_a[slot]
        from_right = from_right + recv_r[0, slot]
        from_left = from_left + recv_r[1, slot]
    lanes = lax.broadcasted_iota(jnp.int32, (tiles_dev, rows, width), 2)
    has_left = jnp.where(me_t > 0, 1.0, 0.0)
    has_right = jnp.where(me_t < n_tile - 1, 1.0, 0.0)
    from_left = jnp.where(lanes < HALO, from_left, 0.0) * has_left
    from_right = jnp.where(lanes >= width - HALO, from_right, 0.0) * has_right
    part_s[...] = total + (from_left + from_right)

    swaps = []
    for slot, shift in enumerate(shifts):
        copy = pltpu.make_async_remote_copy(
            src_ref=part_s,
            dst_ref=recv_b.at[slot],
            send_sem=send_b.at[slot],
            recv_sem=rsem_b.at[slot],
            device_id=(flip_bit(me_t, shift), me_d),
            device_id_type=MESH,
        )
        copy.start()
        swaps.append(copy)
    for copy in swaps:
        copy.wait_recv()
    for copy in swaps:
        copy.wait_send()

    lane_a = lax.broadcasted_iota(jnp.int32, (width, width), 0)
    lane_b = lax.broadcasted_iota(jnp.int32, (width, width), 1)
    reverse = jnp.where(lane_a + lane_b == width - 1, 1.0, 0.0).astype(jnp.float32)
    for local in range(tiles_dev):
        partner = partner_ref[local]
        chosen = jnp.zeros((rows, width), jnp.float32)
        for other in range(tiles_dev):
            hit = jnp.where(partner == me_t * tiles_dev + other, 1.0, 0.0)
            chosen = chosen + hit * part_s[other]
        for slot, shift in enumerate(shifts):
            source = flip_bit(me_t, shift)
            for other in range(tiles_dev):
                hit = jnp.where(partner == source * tiles_dev + other, 1.0, 0.0)
                chosen = chosen + hit * recv_b[slot, other]
        mirrored = jnp.dot(
            chosen, reverse, precision=lax.Precision.HIGHEST, preferred_element_type=jnp.float32
        )
        use_mirror = jnp.where(mirror_ref[local] == 1, 1.0, 0.0)
        chosen = use_mirror * mirrored + (1.0 - use_mirror) * chosen
        blend_s[local] = 0.5 * (part_s[local] + chosen)

    recv_c[me_d] = blend_s[...]
    halo_copies = []
    if with_halo:
        nb_ref = refs[1]
        recv_n, send_n, rsem_n = refs[outputs + 15 :]
        for side, neighbour in enumerate((left_t, right_t)):
            for depth in range(n_depth):
                copy = pltpu.make_async_remote_copy(
                    src_ref=blend_s,
                    dst_ref=recv_n.at[side, me_d],
                    send_sem=send_n.at[side, depth],
                    recv_sem=rsem_n.at[side, me_d],
                    device_id=(neighbour, depth),
                    device_id_type=MESH,
                )
                copy.start()
                halo_copies.append(copy)
    depth_round(lambda target: blend_s, recv_c, send_c, rsem_c)
    if with_halo:
        for side, neighbour in enumerate((left_t, right_t)):
            for depth in range(n_depth):
                pltpu.make_async_remote_copy(
                    src_ref=blend_s,
                    dst_ref=recv_n.at[side, depth],
                    send_sem=send_n.at[side, depth],
                    recv_sem=rsem_n.at[side, depth],
                    device_id=(neighbour, depth),
                    device_id_type=MESH,
                ).wait_recv()
        for copy in halo_copies:
            copy.wait_send()
    for slot in range(n_depth):
        if with_halo:
            out_ref[:, slot * rows : (slot + 1) * rows, :] = (
                mask_ref[:, slot * rows : (slot + 1) * rows, :] - step_rate * recv_c[slot]
            )
        else:
            out_ref[:, slot * rows : (slot + 1) * rows, :] = recv_c[slot]
        if with_halo:
            for side in range(2):
                nb_ref[side, :, slot * rows : (slot + 1) * rows, :] = recv_n[side, slot]


def exchange(values, core, partner_local, mirror_local, mask_tiles, call_id, with_halo):
    n_tile = lax.axis_size("tile")
    n_depth = lax.axis_size("depth")
    n_shift = max(n_tile - 1, 1).bit_length()
    tiles_dev, unused_height, wide = values.shape
    width = core
    piece = (tiles_dev, core // n_depth, width)
    vmem = pl.BlockSpec(memory_space=pltpu.VMEM)
    out_shape = jax.ShapeDtypeStruct((tiles_dev, core, width), jnp.float32)
    out_specs = vmem
    extra_first, extra_last = [], []
    if with_halo:
        out_shape = (out_shape, jax.ShapeDtypeStruct((2, tiles_dev, core, width), jnp.float32))
        out_specs = (vmem, vmem)
        extra_last = [
            pltpu.VMEM((2, n_depth) + piece, jnp.float32),
            pltpu.SemaphoreType.DMA((2, n_depth)),
            pltpu.SemaphoreType.DMA((2, n_depth)),
        ]
    smem = pl.BlockSpec(memory_space=pltpu.SMEM)
    return pl.pallas_call(
        functools.partial(exchange_kernel, n_tile, n_depth, with_halo),
        out_shape=out_shape,
        in_specs=[vmem, smem, smem, vmem],
        out_specs=out_specs,
        scratch_shapes=extra_first + [
            pltpu.VMEM((tiles_dev, core, wide), jnp.float32),
            pltpu.VMEM((n_depth,) + piece, jnp.float32),
            pltpu.VMEM((2, n_depth) + piece, jnp.float32),
            pltpu.VMEM(piece, jnp.float32),
            pltpu.VMEM((n_shift,) + piece, jnp.float32),
            pltpu.VMEM(piece, jnp.float32),
            pltpu.VMEM((n_depth,) + piece, jnp.float32),
            pltpu.SemaphoreType.DMA((n_depth,)),
            pltpu.SemaphoreType.DMA((n_depth,)),
            pltpu.SemaphoreType.DMA((2, n_depth)),
            pltpu.SemaphoreType.DMA((2, n_depth)),
            pltpu.SemaphoreType.DMA((n_shift,)),
            pltpu.SemaphoreType.DMA((n_shift,)),
            pltpu.SemaphoreType.DMA((n_depth,)),
            pltpu.SemaphoreType.DMA((n_depth,)),
        ]
        + extra_last,
        compiler_params=pltpu.CompilerParams(collective_id=call_id, has_side_effects=True),
    )(values, partner_local, mirror_local, mask_tiles)


def final_update_kernel(mask_ref, grad_ref, mask_out, grad_out):
    grad = grad_ref[...]
    mask_out[...] = mask_ref[...] - step_rate * grad
    grad_out[...] = grad


def final_update(mask_tiles, step_gradient):
    vmem = pl.BlockSpec(memory_space=pltpu.VMEM)
    shape = jax.ShapeDtypeStruct(mask_tiles.shape, jnp.float32)
    return pl.pallas_call(
        final_update_kernel,
        out_shape=(shape, shape),
        in_specs=[vmem, vmem],
        out_specs=(vmem, vmem),
    )(mask_tiles, step_gradient)


def per_device(
    mask_tiles, target_tiles, kernels, socs_weights, thresholds, partner_table, mirror_flags
):
    tiles_dev, core, unused_width = mask_tiles.shape
    points = FRAME
    index_full = jnp.arange(points, dtype=jnp.int32)
    cos_table, sin_table = angle_tables(index_full, index_full, points)
    offsets = jnp.arange(KSIZE, dtype=jnp.int32) - HALO
    cos_small, sin_small = angle_tables(index_full, offsets, points)
    spec_re, spec_im = left_apply(cos_small, sin_small, -1.0, kernels[0], kernels[1])
    spec_re, spec_im = right_apply(spec_re, spec_im, cos_small.T, sin_small.T, -1.0)
    target_f = target_tiles.astype(jnp.float32)
    rows_n = -(-points // 16) * 16
    cols_n = -(-points // 128) * 128
    row_fill = rows_n - points
    col_fill = cols_n - points
    targets = jnp.pad(
        target_f, ((0, 0), (HALO, rows_n - HALO - core), (HALO, cols_n - HALO - core))
    )
    spec_re_p = jnp.pad(spec_re[0], ((0, 0), (0, row_fill), (0, col_fill)))
    spec_im_p = jnp.pad(spec_im[0], ((0, 0), (0, row_fill), (0, col_fill)))
    tables = (
        table_stack(points, rows_n, rows_n, True),
        table_stack(points, cols_n, cols_n, False),
    )
    strip_height = tiles_dev * core
    step_gradient = jnp.zeros_like(mask_tiles)
    me_t = lax.axis_index("tile")
    n_tile = lax.axis_size("tile")
    halo_left = halo_right = None
    for step_index in range(STEPS):
        strip_rows = mask_tiles.reshape(strip_height, core)
        if halo_left is None:
            extended = extended_2(strip_rows, (("tile", 1),), HALO)
            halo_left = extended[:, :HALO]
            halo_right = extended[:, HALO + core :]
        else:
            extended = jnp.concatenate([halo_left, strip_rows, halo_right], axis=1)
        padded = jnp.pad(extended, ((HALO, HALO), (0, 0)))
        frames = jnp.stack(
            [padded[row_index * core : row_index * core + points] for row_index in range(tiles_dev)]
        )
        frames = jnp.pad(frames, ((0, 0), (0, row_fill), (0, col_fill)))
        grads = frame_gradients(
            frames, targets, spec_re_p, spec_im_p, socs_weights[0], thresholds, tables, points
        )
        with_halo = step_index + 1 < STEPS
        result = exchange(grads, core, partner_table, mirror_flags, mask_tiles, step_index, with_halo)
        if with_halo:
            mask_tiles, beside = result
            from_right = beside[0].reshape(strip_height, core)[:, :HALO]
            from_left = beside[1].reshape(strip_height, core)[:, core - HALO :]
            halo_left = jnp.where(me_t > 0, halo_left - step_rate * from_left, 0.0)
            halo_right = jnp.where(me_t < n_tile - 1, halo_right - step_rate * from_right, 0.0)
        else:
            step_gradient = result
    return final_update(mask_tiles, step_gradient)


def solution(mesh):
    return jax.shard_map(
        per_device,
        mesh=mesh,
        in_specs=(
            P("tile", None, None),
            P("tile", None, None),
            P(None, "depth", None, None, None),
            P("depth", None),
            P("depth"),
            P("tile"),
            P("tile"),
        ),
        out_specs=(P("tile", None, None), P("tile", None, None)),
        check_vma=False,
    )
```

```python
import functools

import jax
import jax.numpy as jnp
import ml_dtypes
import numpy as np
from jax import lax
from jax.experimental import pallas as pl
from jax.experimental.pallas import tpu as pltpu
from jax.sharding import PartitionSpec as P

MESH = pl.DeviceIdType.MESH

HALO = 12
FRAME = 152
KSIZE = 25
STEPS = 2


steepness = 3.0
step_rate = 0.05


def extended_2(cells, sides, width):
    for axis, dim in sides:
        count = lax.axis_size(axis)
        ends = count - 1
        head = lax.slice_in_dim(cells, 0, width, axis=dim)
        tail = lax.slice_in_dim(cells, cells.shape[dim] - width, cells.shape[dim], axis=dim)
        cells = jnp.concatenate(
            [
                lax.ppermute(tail, axis, [(i, (i + 1) % count) for i in range(ends)]),
                cells,
                lax.ppermute(head, axis, [((i + 1) % count, i) for i in range(ends)]),
            ],
            axis=dim,
        )
    return cells


def mult_left(matrix, values):
    return jnp.einsum("jk,...kl->...jl", matrix, values, precision=lax.Precision.HIGH)


def mult_right(values, matrix):
    return jnp.einsum("...jk,kl->...jl", values, matrix, precision=lax.Precision.HIGH)


def left_apply(cos_table, sin_table, sign, real_in, imag_in):
    if imag_in is None:
        return (mult_left(cos_table, real_in), sign * mult_left(sin_table, real_in))
    real_out = mult_left(cos_table, real_in) - sign * mult_left(sin_table, imag_in)
    imag_out = mult_left(cos_table, imag_in) + sign * mult_left(sin_table, real_in)
    return (real_out, imag_out)


def right_apply(real_in, imag_in, cos_table, sin_table, sign):
    real_out = mult_right(real_in, cos_table) - sign * mult_right(imag_in, sin_table)
    imag_out = mult_right(imag_in, cos_table) + sign * mult_right(real_in, sin_table)
    return (real_out, imag_out)


def angle_tables(rows_idx, cols_idx, points):
    product = rows_idx[:, None] * cols_idx[None, :] % points
    theta = product.astype(jnp.float32) * (2.0 * np.pi / points)
    return (jnp.cos(theta), jnp.sin(theta))


def split_bf16(values):
    high = lax.reduce_precision(values, exponent_bits=8, mantissa_bits=7)
    return high.astype(jnp.bfloat16), (values - high).astype(jnp.bfloat16)


def split_inside(values):
    spread = values * 65537.0
    high = spread - (spread - values)
    return high.astype(jnp.bfloat16), (values - high).astype(jnp.bfloat16)


def dot3(a_high, a_low, b_high, b_low):
    def product(a, b):
        return jnp.dot(a, b, preferred_element_type=jnp.float32)

    return product(a_high, b_high) + (product(a_high, b_low) + product(a_low, b_high))


def frame_kernel(
    points,
    frame_ref,
    target_ref,
    sre_ref,
    sim_ref,
    w_ref,
    lvl_ref,
    lt_ref,
    rt_ref,
    out_ref,
    fre_s,
    fim_s,
    spec_s,
    slope_s,
    acc_s,
):
    rows_n, cols_n = frame_ref.shape[1:]
    kern = sre_ref.shape[0]
    core = points - 2 * HALO
    scale = 1.0 / (points * points)
    picks = {1.0: (0, 2, 3), -1.0: (0, 4, 5), 0.0: (6, 7, 8)}

    def lmul(index, values):
        high, low = split_inside(values)
        return dot3(lt_ref[index, 0], lt_ref[index, 1], high, low)

    def rmul(values, index):
        high, low = split_inside(values)
        return dot3(high, low, rt_ref[index, 0], rt_ref[index, 1])

    def left(real_in, imag_in, sign):
        plain, plus, minus = picks[sign]
        both = lmul(plain, real_in + imag_in)
        return both - lmul(plus, imag_in), both + lmul(minus, real_in)

    def right(real_in, imag_in, sign):
        plain, plus, minus = picks[sign]
        both = rmul(real_in + imag_in, plain)
        return both - rmul(imag_in, plus), both + rmul(real_in, minus)

    frame = frame_ref[0]
    freq_re, freq_im = right(lmul(0, frame), -lmul(1, frame), -1.0)
    spec_s[0] = freq_re
    spec_s[1] = freq_im

    def forward(k, intensity):
        s_re = sre_ref[k]
        s_im = sim_ref[k]
        f_re = spec_s[0]
        f_im = spec_s[1]
        prod_re = s_re * f_re - s_im * f_im
        prod_im = s_re * f_im + s_im * f_re
        b_re, b_im = left(prod_re, prod_im, 1.0)
        g_re, g_im = right(b_re, b_im, 1.0)
        g_re = g_re * scale
        g_im = g_im * scale
        fre_s[k] = g_re
        fim_s[k] = g_im
        return intensity + w_ref[k] * (g_re * g_re + g_im * g_im)

    intensity = lax.fori_loop(0, kern, forward, jnp.zeros((rows_n, cols_n), jnp.float32))
    rows = lax.broadcasted_iota(jnp.int32, (rows_n, cols_n), 0)
    cols = lax.broadcasted_iota(jnp.int32, (rows_n, cols_n), 1)
    inside = (rows >= HALO) & (rows < HALO + core) & (cols >= HALO) & (cols < HALO + core)
    resist = 1.0 / (1.0 + jnp.exp(-(steepness * (intensity - lvl_ref[0]))))
    slope = 2.0 * (resist - target_ref[0]) * steepness * resist * (1.0 - resist)
    slope_s[...] = jnp.where(inside, slope, 0.0)
    acc_s[...] = jnp.zeros_like(acc_s)

    def backward(k, carry):
        factor = 2.0 * w_ref[k] * slope_s[...]
        b_re, b_im = left(factor * fre_s[k], factor * fim_s[k], -1.0)
        h_re, h_im = right(b_re, b_im, -1.0)
        s_re = sre_ref[k]
        s_im = sim_ref[k]
        acc_s[0] += s_re * h_re + s_im * h_im
        acc_s[1] += s_re * h_im - s_im * h_re
        return carry

    lax.fori_loop(0, kern, backward, 0)
    u_re, u_im = left(acc_s[0], acc_s[1], 0.0)
    out_ref[0] = (rmul(u_re, 6) - rmul(u_im, 7)) * scale


def shifted_order(length, points):
    order = np.full(length, -1)
    order[: points - HALO] = np.arange(HALO, points)
    order[length - HALO :] = np.arange(HALO)
    return order


def table_stack(points, rows_n, cols_n, on_rows):
    index = np.arange(points)
    theta = (np.outer(index, index) % points) * (2.0 * np.pi / points)
    cos_t, sin_t = np.cos(theta), np.sin(theta)
    combos = [cos_t, sin_t, cos_t + sin_t, sin_t - cos_t, cos_t - sin_t, -sin_t - cos_t]
    padded = [np.pad(table, ((0, rows_n - points), (0, cols_n - points))) for table in combos]
    if on_rows:
        order = shifted_order(rows_n, points)
        finals = [padded[0], padded[2], padded[3]]
        finals = [np.where((order >= 0)[:, None], table[np.maximum(order, 0)], 0.0) for table in finals]
    else:
        order = shifted_order(cols_n, points)
        finals = [padded[0], padded[1]]
        finals = [
            np.where((order >= 0)[None, :], table[:, np.maximum(order, 0)], 0.0) for table in finals
        ]
    stack = np.stack(padded + finals).astype(np.float32)
    high = stack.astype(ml_dtypes.bfloat16)
    low = (stack - high.astype(np.float32)).astype(ml_dtypes.bfloat16)
    return jnp.asarray(np.stack([high, low], axis=1))


def frame_gradients(frames, targets, spec_re, spec_im, weights, levels, tables, points):
    count, rows_n, cols_n = frames.shape
    kern = spec_re.shape[0]
    left_tables, right_tables = tables
    per_frame = pl.BlockSpec((1, rows_n, cols_n), lambda i: (i, 0, 0))
    whole_spec = pl.BlockSpec((kern, rows_n, cols_n), lambda i: (0, 0, 0))
    smem = pl.BlockSpec(memory_space=pltpu.SMEM)
    flops = count * (kern * 4 + 4) * 9 * 2 * rows_n * cols_n * cols_n
    return pl.pallas_call(
        functools.partial(frame_kernel, points),
        out_shape=jax.ShapeDtypeStruct(frames.shape, jnp.float32),
        grid=(count,),
        in_specs=[
            per_frame,
            per_frame,
            whole_spec,
            whole_spec,
            smem,
            smem,
            pl.BlockSpec(left_tables.shape, lambda i: (0, 0, 0, 0)),
            pl.BlockSpec(right_tables.shape, lambda i: (0, 0, 0, 0)),
        ],
        out_specs=per_frame,
        scratch_shapes=[
            pltpu.VMEM((kern, rows_n, cols_n), jnp.float32),
            pltpu.VMEM((kern, rows_n, cols_n), jnp.float32),
            pltpu.VMEM((2, rows_n, cols_n), jnp.float32),
            pltpu.VMEM((rows_n, cols_n), jnp.float32),
            pltpu.VMEM((2, rows_n, cols_n), jnp.float32),
        ],
        compiler_params=pltpu.CompilerParams(
            dimension_semantics=("arbitrary",), vmem_limit_bytes=48 * 1024 * 1024
        ),
        cost_estimate=pl.CostEstimate(
            flops=flops, transcendentals=count * rows_n * cols_n, bytes_accessed=8 * 1024 * 1024
        ),
    )(frames, targets, spec_re, spec_im, weights, levels, left_tables, right_tables)


def flip_bit(value, shift):
    bit = (value // shift) % 2
    return value + shift * (1 - 2 * bit)


def exchange_kernel(n_tile, n_depth, with_halo, x_ref, partner_ref, mirror_ref, *refs):
    if with_halo:
        mask_ref, refs = refs[0], refs[1:]
    outputs = 2 if with_halo else 1
    out_ref = refs[0]
    (
        xs,
        recv_a,
        recv_r,
        part_s,
        recv_b,
        blend_s,
        recv_c,
        send_a,
        rsem_a,
        send_r,
        rsem_r,
        send_b,
        rsem_b,
        send_c,
        rsem_c,
    ) = refs[outputs : outputs + 15]
    me_t = lax.axis_index("tile")
    me_d = lax.axis_index("depth")
    tiles_dev, core, wide = xs.shape
    width = out_ref.shape[-1]
    rows = core // n_depth
    left_t = (me_t + n_tile - 1) % n_tile
    right_t = (me_t + 1) % n_tile
    shifts = []
    shift = 1
    while shift < n_tile:
        shifts.append(shift)
        shift *= 2
    barrier = pltpu.get_barrier_semaphore()
    for step in range(1, n_depth):
        pl.semaphore_signal(
            barrier, inc=1, device_id=(me_t, (me_d + step) % n_depth), device_id_type=MESH
        )
    for shift in shifts:
        pl.semaphore_signal(
            barrier, inc=1, device_id=(flip_bit(me_t, shift), me_d), device_id_type=MESH
        )
    for neighbour in (left_t, right_t):
        for depth in range(n_depth):
            pl.semaphore_signal(barrier, inc=1, device_id=(neighbour, depth), device_id_type=MESH)
    pl.semaphore_wait(barrier, 3 * n_depth - 1 + len(shifts))

    def band(index):
        return pl.ds(pl.multiple_of(index * rows, rows), rows)

    def depth_round(source_of, dst_buf, send_sem, recv_sem):
        copies = []
        for step in range(1, n_depth):
            target = (me_d + step) % n_depth
            copy = pltpu.make_async_remote_copy(
                src_ref=source_of(target),
                dst_ref=dst_buf.at[me_d],
                send_sem=send_sem.at[step],
                recv_sem=recv_sem.at[me_d],
                device_id=(me_t, target),
                device_id_type=MESH,
            )
            copy.start()
            copies.append(copy)
        for step in range(1, n_depth):
            source = (me_d + n_depth - step) % n_depth
            pltpu.make_async_remote_copy(
                src_ref=source_of(source),
                dst_ref=dst_buf.at[source],
                send_sem=send_sem.at[step],
                recv_sem=recv_sem.at[source],
                device_id=(me_t, source),
                device_id_type=MESH,
            ).wait_recv()
        for copy in copies:
            copy.wait_send()

    height = x_ref.shape[1]
    slab = 16
    xs[...] = x_ref[:, :core, :]
    for local in range(tiles_dev):
        if local + 1 < tiles_dev:
            xs[local, core - slab :, :] += x_ref[local + 1, height - slab :, :]
        if local > 0:
            xs[local, :slab, :] += x_ref[local - 1, core : core + slab, :]

    rims = []
    for side, neighbour in enumerate((left_t, right_t)):
        for depth in range(n_depth):
            copy = pltpu.make_async_remote_copy(
                src_ref=xs.at[:, pl.ds(depth * rows, rows), pl.ds(width, wide - width)],
                dst_ref=recv_r.at[side, me_d],
                send_sem=send_r.at[side, depth],
                recv_sem=rsem_r.at[side, me_d],
                device_id=(neighbour, depth),
                device_id_type=MESH,
            )
            copy.start()
            rims.append(copy)
    recv_a[me_d] = xs[:, band(me_d), :width]
    depth_round(lambda target: xs.at[:, band(target), pl.ds(0, width)], recv_a, send_a, rsem_a)
    for side, neighbour in enumerate((left_t, right_t)):
        for depth in range(n_depth):
            pltpu.make_async_remote_copy(
                src_ref=xs.at[:, pl.ds(depth * rows, rows), pl.ds(width, wide - width)],
                dst_ref=recv_r.at[side, depth],
                send_sem=send_r.at[side, depth],
                recv_sem=rsem_r.at[side, depth],
                device_id=(neighbour, depth),
                device_id_type=MESH,
            ).wait_recv()
    for copy in rims:
        copy.wait_send()
    total = recv_a[0]
    from_right = recv_r[0, 0]
    from_left = recv_r[1, 0]
    for slot in range(1, n_depth):
        total = total + recv_a[slot]
        from_right = from_right + recv_r[0, slot]
        from_left = from_left + recv_r[1, slot]
    lanes = lax.broadcasted_iota(jnp.int32, (tiles_dev, rows, width), 2)
    has_left = jnp.where(me_t > 0, 1.0, 0.0)
    has_right = jnp.where(me_t < n_tile - 1, 1.0, 0.0)
    from_left = jnp.where(lanes < HALO, from_left, 0.0) * has_left
    from_right = jnp.where(lanes >= width - HALO, from_right, 0.0) * has_right
    part_s[...] = total + (from_left + from_right)

    swaps = []
    for slot, shift in enumerate(shifts):
        copy = pltpu.make_async_remote_copy(
            src_ref=part_s,
            dst_ref=recv_b.at[slot],
            send_sem=send_b.at[slot],
            recv_sem=rsem_b.at[slot],
            device_id=(flip_bit(me_t, shift), me_d),
            device_id_type=MESH,
        )
        copy.start()
        swaps.append(copy)
    for copy in swaps:
        copy.wait_recv()
    for copy in swaps:
        copy.wait_send()

    lane_a = lax.broadcasted_iota(jnp.int32, (width, width), 0)
    lane_b = lax.broadcasted_iota(jnp.int32, (width, width), 1)
    reverse = jnp.where(lane_a + lane_b == width - 1, 1.0, 0.0).astype(jnp.float32)
    for local in range(tiles_dev):
        partner = partner_ref[local]
        chosen = jnp.zeros((rows, width), jnp.float32)
        for other in range(tiles_dev):
            hit = jnp.where(partner == me_t * tiles_dev + other, 1.0, 0.0)
            chosen = chosen + hit * part_s[other]
        for slot, shift in enumerate(shifts):
            source = flip_bit(me_t, shift)
            for other in range(tiles_dev):
                hit = jnp.where(partner == source * tiles_dev + other, 1.0, 0.0)
                chosen = chosen + hit * recv_b[slot, other]
        mirrored = jnp.dot(
            chosen, reverse, precision=lax.Precision.HIGHEST, preferred_element_type=jnp.float32
        )
        use_mirror = jnp.where(mirror_ref[local] == 1, 1.0, 0.0)
        chosen = use_mirror * mirrored + (1.0 - use_mirror) * chosen
        blend_s[local] = 0.5 * (part_s[local] + chosen)

    recv_c[me_d] = blend_s[...]
    halo_copies = []
    if with_halo:
        nb_ref = refs[1]
        recv_n, send_n, rsem_n = refs[outputs + 15 :]
        for side, neighbour in enumerate((left_t, right_t)):
            for depth in range(n_depth):
                copy = pltpu.make_async_remote_copy(
                    src_ref=blend_s,
                    dst_ref=recv_n.at[side, me_d],
                    send_sem=send_n.at[side, depth],
                    recv_sem=rsem_n.at[side, me_d],
                    device_id=(neighbour, depth),
                    device_id_type=MESH,
                )
                copy.start()
                halo_copies.append(copy)
    depth_round(lambda target: blend_s, recv_c, send_c, rsem_c)
    if with_halo:
        for side, neighbour in enumerate((left_t, right_t)):
            for depth in range(n_depth):
                pltpu.make_async_remote_copy(
                    src_ref=blend_s,
                    dst_ref=recv_n.at[side, depth],
                    send_sem=send_n.at[side, depth],
                    recv_sem=rsem_n.at[side, depth],
                    device_id=(neighbour, depth),
                    device_id_type=MESH,
                ).wait_recv()
        for copy in halo_copies:
            copy.wait_send()
    for slot in range(n_depth):
        if with_halo:
            out_ref[:, slot * rows : (slot + 1) * rows, :] = (
                mask_ref[:, slot * rows : (slot + 1) * rows, :] - step_rate * recv_c[slot]
            )
        else:
            out_ref[:, slot * rows : (slot + 1) * rows, :] = recv_c[slot]
        if with_halo:
            for side in range(2):
                nb_ref[side, :, slot * rows : (slot + 1) * rows, :] = recv_n[side, slot]


def exchange(values, core, partner_local, mirror_local, mask_tiles, call_id, with_halo):
    n_tile = lax.axis_size("tile")
    n_depth = lax.axis_size("depth")
    n_shift = max(n_tile - 1, 1).bit_length()
    tiles_dev, unused_height, wide = values.shape
    width = core
    piece = (tiles_dev, core // n_depth, width)
    vmem = pl.BlockSpec(memory_space=pltpu.VMEM)
    out_shape = jax.ShapeDtypeStruct((tiles_dev, core, width), jnp.float32)
    out_specs = vmem
    extra_first, extra_last = [], []
    extra_in = [mask_tiles] if with_halo else []
    if with_halo:
        out_shape = (out_shape, jax.ShapeDtypeStruct((2, tiles_dev, core, width), jnp.float32))
        out_specs = (vmem, vmem)
        extra_last = [
            pltpu.VMEM((2, n_depth) + piece, jnp.float32),
            pltpu.SemaphoreType.DMA((2, n_depth)),
            pltpu.SemaphoreType.DMA((2, n_depth)),
        ]
    smem = pl.BlockSpec(memory_space=pltpu.SMEM)
    return pl.pallas_call(
        functools.partial(exchange_kernel, n_tile, n_depth, with_halo),
        out_shape=out_shape,
        in_specs=[vmem, smem, smem] + [vmem] * len(extra_in),
        out_specs=out_specs,
        scratch_shapes=extra_first + [
            pltpu.VMEM((tiles_dev, core, wide), jnp.float32),
            pltpu.VMEM((n_depth,) + piece, jnp.float32),
            pltpu.VMEM((2, n_depth) + piece, jnp.float32),
            pltpu.VMEM(piece, jnp.float32),
            pltpu.VMEM((n_shift,) + piece, jnp.float32),
            pltpu.VMEM(piece, jnp.float32),
            pltpu.VMEM((n_depth,) + piece, jnp.float32),
            pltpu.SemaphoreType.DMA((n_depth,)),
            pltpu.SemaphoreType.DMA((n_depth,)),
            pltpu.SemaphoreType.DMA((2, n_depth)),
            pltpu.SemaphoreType.DMA((2, n_depth)),
            pltpu.SemaphoreType.DMA((n_shift,)),
            pltpu.SemaphoreType.DMA((n_shift,)),
            pltpu.SemaphoreType.DMA((n_depth,)),
            pltpu.SemaphoreType.DMA((n_depth,)),
        ]
        + extra_last,
        compiler_params=pltpu.CompilerParams(collective_id=call_id, has_side_effects=True),
    )(values, partner_local, mirror_local, *extra_in)


def final_update_kernel(mask_ref, grad_ref, mask_out, grad_out):
    grad = grad_ref[...]
    mask_out[...] = mask_ref[...] - step_rate * grad
    grad_out[...] = grad


def final_update(mask_tiles, step_gradient):
    vmem = pl.BlockSpec(memory_space=pltpu.VMEM)
    shape = jax.ShapeDtypeStruct(mask_tiles.shape, jnp.float32)
    return pl.pallas_call(
        final_update_kernel,
        out_shape=(shape, shape),
        in_specs=[vmem, vmem],
        out_specs=(vmem, vmem),
    )(mask_tiles, step_gradient)


def per_device(
    mask_tiles, target_tiles, kernels, socs_weights, thresholds, partner_table, mirror_flags
):
    tiles_dev, core, unused_width = mask_tiles.shape
    points = FRAME
    index_full = jnp.arange(points, dtype=jnp.int32)
    cos_table, sin_table = angle_tables(index_full, index_full, points)
    offsets = jnp.arange(KSIZE, dtype=jnp.int32) - HALO
    cos_small, sin_small = angle_tables(index_full, offsets, points)
    spec_re, spec_im = left_apply(cos_small, sin_small, -1.0, kernels[0], kernels[1])
    spec_re, spec_im = right_apply(spec_re, spec_im, cos_small.T, sin_small.T, -1.0)
    target_f = target_tiles.astype(jnp.float32)
    rows_n = -(-points // 16) * 16
    cols_n = -(-points // 128) * 128
    row_fill = rows_n - points
    col_fill = cols_n - points
    targets = jnp.pad(
        target_f, ((0, 0), (HALO, rows_n - HALO - core), (HALO, cols_n - HALO - core))
    )
    spec_re_p = jnp.pad(spec_re[0], ((0, 0), (0, row_fill), (0, col_fill)))
    spec_im_p = jnp.pad(spec_im[0], ((0, 0), (0, row_fill), (0, col_fill)))
    tables = (
        table_stack(points, rows_n, rows_n, True),
        table_stack(points, cols_n, cols_n, False),
    )
    strip_height = tiles_dev * core
    step_gradient = jnp.zeros_like(mask_tiles)
    me_t = lax.axis_index("tile")
    n_tile = lax.axis_size("tile")
    halo_left = halo_right = None
    for step_index in range(STEPS):
        strip_rows = mask_tiles.reshape(strip_height, core)
        if halo_left is None:
            extended = extended_2(strip_rows, (("tile", 1),), HALO)
            halo_left = extended[:, :HALO]
            halo_right = extended[:, HALO + core :]
        else:
            extended = jnp.concatenate([halo_left, strip_rows, halo_right], axis=1)
        padded = jnp.pad(extended, ((HALO, HALO), (0, 0)))
        frames = jnp.stack(
            [padded[row_index * core : row_index * core + points] for row_index in range(tiles_dev)]
        )
        frames = jnp.pad(frames, ((0, 0), (0, row_fill), (0, col_fill)))
        grads = frame_gradients(
            frames, targets, spec_re_p, spec_im_p, socs_weights[0], thresholds, tables, points
        )
        with_halo = step_index + 1 < STEPS
        result = exchange(grads, core, partner_table, mirror_flags, mask_tiles, step_index, with_halo)
        if with_halo:
            mask_tiles, beside = result
            from_right = beside[0].reshape(strip_height, core)[:, :HALO]
            from_left = beside[1].reshape(strip_height, core)[:, core - HALO :]
            halo_left = jnp.where(me_t > 0, halo_left - step_rate * from_left, 0.0)
            halo_right = jnp.where(me_t < n_tile - 1, halo_right - step_rate * from_right, 0.0)
        else:
            step_gradient = result
    return final_update(mask_tiles, step_gradient)


def solution(mesh):
    return jax.shard_map(
        per_device,
        mesh=mesh,
        in_specs=(
            P("tile", None, None),
            P("tile", None, None),
            P(None, "depth", None, None, None),
            P("depth", None),
            P("depth"),
            P("tile"),
            P("tile"),
        ),
        out_specs=(P("tile", None, None), P("tile", None, None)),
        check_vma=False,
    )
```
